32 devices in a mesh: groups: 2 (over y), scanx: 4 (over z), scany: 2 (over x), pos: 2 (over core).
Axes of the slice: x: 2, y: 2, z: 4, core: 2. Of those that a mesh axis runs over, the one named last changes fastest.
Arguments:
- specimen: float32 [2, 2048, 512], P(None, ('groups', 'scanx'), 'scany'), parts along dimension 1, may hold values from -5 to 5
- probe_wave: float32 [2, 512, 256], P(None, 'groups'), parts along dimension 1, may hold values from -6 to 6
- amplitudes: bfloat16 [64, 256, 256], P(('groups', 'scanx', 'scany', 'pos')), parts along dimension 0, may hold values from 0 to 2
- offsets: int32 [64, 2], P(('groups', 'scanx', 'scany', 'pos')), parts along dimension 0, may hold values from 0 to 255
Outputs:
- new_specimen: float32 [2, 2048, 512], P(None, ('groups', 'scanx'), 'scany'), parts along dimension 1
- new_probe: float32 [2, 512, 256], P(None, 'groups'), parts along dimension 1
The draws below stay inside these ranges and needn't reach their ends.
There are 2 independent parts, one for each index of `groups`. The reference program is written for one: setup_inputs(seed, part) draws one part's arguments, and reference() takes and returns one part's arrays. A program takes and returns all parts, laid end to end along the dimension named above; each array names one. Nothing has to cross between parts.
Inputs may be any that keep to these rules, and one draw needn't show every extreme that they name: offsets are pixels from the top-left corner of the position's tile.
All inputs are finite; a program needn't handle non-finite values.
Results may differ from the reference program's by a relative error of at most 0.002.
The reference program's roundings to bfloat16 on the way count: a program that leaves them out, or rounds other values in their place, can miss the bound.
Values sent between devices are 32-bit elements; how exact they have to be, the bound alone decides.
A program may use at most 64 MiB of HBM per device.

```python
import math
import jax
import jax.numpy as jnp
from jax import lax

M = 256
TILE = 256
PER_TILE = 4
TILES_Y = 2
POSITIONS = 32
NXO = 1024
NYO = 512


def place_ends(drawn, stream_key, low, largest):
    index_at = [jax.random.randint(jax.random.fold_in(stream_key, axis), (), 0, length) for axis, length in enumerate(drawn.shape)]
    longest = drawn.shape.index(max(drawn.shape))
    neighbour = index_at[:longest] + [(index_at[longest] + 1) % drawn.shape[longest]] + index_at[longest + 1:]
    return drawn.at[tuple(index_at)].set(low).at[tuple(neighbour)].set(largest)


def level_of(rng, extent, pieces, smallest, largest):
    factor_of = 1.0
    for axis_at, shards_of in pieces:
        steps = jax.random.uniform(jax.random.fold_in(jax.random.fold_in(rng, 6), axis_at), (shards_of,), jnp.float32, smallest / len(pieces), largest / len(pieces))
        factor_of = factor_of * jnp.repeat(jnp.exp(steps), extent[axis_at] // shards_of).reshape((-1,) + (1,) * (len(extent) - 1 - axis_at))
    return factor_of


def noise(stream_key, extent, scale, limit, cuts=(), kind=jnp.bfloat16):
    result = scale * jax.random.normal(stream_key, extent, jnp.float32)
    if cuts:
        result = result * level_of(stream_key, extent, cuts, -0.22, 0.18)
    return jnp.clip(result, -limit, limit).astype(kind)


def setup_inputs(seed: int = 0, part: int = 0) -> dict:
    arg_keys = jax.random.split(jax.random.key(seed), 5)
    part_splits = jax.random.split(jax.random.fold_in(arg_keys[4], part), 5)
    specimen = noise(part_splits[0], (2, NXO, NYO), 0.7, 5.0, ((1, 4), (2, 2)), jnp.float32)
    probe_wave = noise(part_splits[1], (2, M, M), 1.0, 6.0, (), jnp.float32)
    amplitudes = jnp.clip(2.0 * jax.random.uniform(part_splits[2], (POSITIONS, M, M), jnp.float32) ** level_of(part_splits[2], (POSITIONS, M, M), ((0, 16),), -0.2, 0.2), 0.0, 2.0).astype(jnp.bfloat16)
    offsets = place_ends(jax.random.randint(part_splits[3], (POSITIONS, 2), 0, TILE), jax.random.fold_in(part_splits[3], 1), 0, TILE - 1).astype(jnp.int32)
    return dict(specimen=specimen, probe_wave=probe_wave, amplitudes=amplitudes, offsets=offsets)


def dft_tables(length):
    positions_index = jnp.arange(length, dtype=jnp.int32)
    phase_index = positions_index[:, None] * positions_index[None, :] % length
    angle_rad = phase_index.astype(jnp.float32) * (2.0 * math.pi / length)
    scale_factor = 1.0 / math.sqrt(length)
    cosine = (jnp.cos(angle_rad) * scale_factor).astype(jnp.bfloat16)
    sine_part = (jnp.sin(angle_rad) * scale_factor).astype(jnp.bfloat16)
    forward_left = jnp.stack([jnp.stack([cosine, sine_part], 1), jnp.stack([-sine_part, cosine], 1)], 0)
    forward_right = jnp.stack([jnp.stack([cosine, -sine_part], 1), jnp.stack([sine_part, cosine], 1)], 0)
    inverse_left = jnp.stack([jnp.stack([cosine, -sine_part], 1), jnp.stack([sine_part, cosine], 1)], 0)
    inverse_right = jnp.stack([jnp.stack([cosine, sine_part], 1), jnp.stack([-sine_part, cosine], 1)], 0)
    return (forward_left, forward_right, inverse_left, inverse_right)

def left_product(matrix, field_in):
    return jnp.einsum('akbr,brv->akv', matrix.astype(jnp.float32), field_in.astype(jnp.float32))

def right_product(field_in, matrix):
    return jnp.einsum('bkv,bval->akl', field_in.astype(jnp.float32), matrix.astype(jnp.float32))

def project_exit(patch_wave, probe_real, probe_imag, amplitude, tables):
    forward_left, forward_right, inverse_left, inverse_right = tables
    patch_real = patch_wave[0]
    patch_imag = patch_wave[1]
    exit_real = probe_real * patch_real - probe_imag * patch_imag
    exit_imag = probe_real * patch_imag + probe_imag * patch_real
    exit_wave = jnp.stack([exit_real, exit_imag]).astype(jnp.bfloat16)
    half_done = left_product(forward_left, exit_wave).astype(jnp.bfloat16)
    far_field = right_product(half_done, forward_right)
    magnitude = jnp.sqrt(far_field[0] * far_field[0] + far_field[1] * far_field[1])
    scale_ratio = amplitude.astype(jnp.float32) / jnp.maximum(magnitude, 0.2)
    projected = (far_field * scale_ratio[None]).astype(jnp.bfloat16)
    back_half = left_product(inverse_left, projected).astype(jnp.bfloat16)
    back_wave = right_product(back_half, inverse_right)
    return (back_wave[0] - exit_real, back_wave[1] - exit_imag, patch_real, patch_imag)

def reference(specimen, probe_wave, amplitudes, offsets):
    margin = M // 2
    tables = dft_tables(M)
    padded = jnp.pad(specimen, ((0, 0), (margin, margin), (margin, margin)))
    probe_real = probe_wave[0]
    probe_imag = probe_wave[1]
    probe_power = probe_real * probe_real + probe_imag * probe_imag
    tile_index = jnp.arange(POSITIONS, dtype=jnp.int32) // PER_TILE
    tile_row = tile_index // TILES_Y
    tile_col = tile_index % TILES_Y
    row_starts = (tile_row * TILE + offsets[:, 0]).astype(jnp.int32)
    col_starts = (tile_col * TILE + offsets[:, 1]).astype(jnp.int32)
    zero_index = jnp.zeros((), jnp.int32)

    def visit_position(carried, inputs):
        object_grad, probe_grad = carried
        amplitude, row_start, col_start = inputs
        patch_wave = lax.dynamic_slice(padded, (zero_index, row_start, col_start), (2, M, M))
        diff_real, diff_imag, patch_real, patch_imag = project_exit(patch_wave, probe_real, probe_imag, amplitude, tables)
        object_term = jnp.stack([probe_real * diff_real + probe_imag * diff_imag, probe_real * diff_imag - probe_imag * diff_real, probe_power])
        current = lax.dynamic_slice(object_grad, (zero_index, row_start, col_start), (3, M, M))
        object_grad = lax.dynamic_update_slice(object_grad, current + object_term, (zero_index, row_start, col_start))
        probe_term = jnp.stack([patch_real * diff_real + patch_imag * diff_imag, patch_real * diff_imag - patch_imag * diff_real])
        return ((object_grad, probe_grad + probe_term), None)
    start_grad = jnp.zeros((3, NXO + M, NYO + M), jnp.float32)
    start_probe = jnp.zeros((2, M, M), jnp.float32)
    (object_grad, probe_grad), unused = lax.scan(visit_position, (start_grad, start_probe), (amplitudes, row_starts, col_starts))
    core_sum = object_grad[:, margin:margin + NXO, margin:margin + NYO]
    new_specimen = specimen + core_sum[0:2] / (core_sum[2:3] + 1.0)
    step_size = 1.0 / math.sqrt(POSITIONS)
    new_probe = probe_wave + probe_grad * step_size
    return (new_specimen, new_probe)
```

```python
import functools
import math

import jax
import jax.numpy as jnp
import numpy as np
from jax import lax
from jax.experimental import pallas as pl
from jax.experimental.pallas import tpu as pltpu
from jax.sharding import PartitionSpec as P

MESH = pl.DeviceIdType.MESH
VMEM = pltpu.VMEM


def remote(src, dst, send, recv, where):
    return pltpu.make_async_remote_copy(
        src_ref=src, dst_ref=dst, send_sem=send, recv_sem=recv, device_id=where, device_id_type=MESH
    )


def greet(conditions_devices):
    barrier = pltpu.get_barrier_semaphore()
    for present, where in conditions_devices:
        if present is True:
            pl.semaphore_signal(barrier, inc=1, device_id=where, device_id_type=MESH)
        else:

            @pl.when(present)
            def _(where=where):
                pl.semaphore_signal(barrier, inc=1, device_id=where, device_id_type=MESH)

    fixed = sum(1 for present, _ in conditions_devices if present is True)
    peers = [present.astype(jnp.int32) for present, _ in conditions_devices if present is not True]
    pl.semaphore_wait(barrier, sum(peers, fixed))


class Side:
    def __init__(self, axis, count, step):
        me = lax.axis_index(axis)
        self.has = me > 0 if step < 0 else me < count - 1
        self.where = {axis: me + step}


class Role:
    def __init__(self, q, nx, ny):
        along_x = ("scanx", nx, Side("scanx", nx, -1), Side("scanx", nx, 1))
        along_y = ("scany", ny, Side("scany", ny, -1), Side("scany", ny, 1))
        one, two = (along_y, along_x) if q == 0 else (along_x, along_y)
        self.q, self.o, self.rows_first = q, 1 - q, q == 1
        self.axis1, self.n1, self.sides1 = one[0], one[1], one[2:]
        self.axis2, self.n2, self.sides2 = two[0], two[1], two[2:]
        self.me1, self.me2 = lax.axis_index(self.axis1), lax.axis_index(self.axis2)


def when(*conditions):
    return pl.when(functools.reduce(jnp.logical_and, conditions))


def dot(a, b):
    return jnp.dot(a, b, preferred_element_type=jnp.float32)


class Halo:
    def __init__(self, role, spec, pad, send, recv, partner):
        self.r, self.spec, self.pad, self.partner = role, spec, pad, partner
        self.send, self.recv = send, recv
        tile = spec.shape[3]
        half = (pad.shape[3] - tile) // 2
        self.own = (half, tile)
        self.margins = ((0, half), (half + tile, half))
        self.edges = ((0, half), (tile - half, half))
        self.pad_edges = ((half, half), (tile, half))
        self.whole = (0, tile)

    def at(self, one, two):
        rows, cols = (one, two) if self.r.rows_first else (two, one)
        return (self.r.q, pl.ds(rows[0] // 8, rows[1] // 8), slice(None), pl.ds(*cols))

    def copy(self, src, dst, i, where):
        return remote(src, dst, self.send.at[i], self.recv.at[i], where)

    def strip1(self, m):
        return self.copy(
            self.spec.at[self.at(self.edges[1 - m], self.whole)],
            self.pad.at[self.at(self.margins[m], self.own)],
            m,
            self.r.sides1[1 - m].where,
        )

    def strip2(self, m):
        return self.copy(
            self.spec.at[self.at(self.whole, self.edges[1 - m])],
            self.pad.at[self.at(self.own, self.margins[m])],
            2 + m,
            self.r.sides2[1 - m].where,
        )

    def corner(self, m1, m2):
        return self.copy(
            self.pad.at[self.at(self.margins[m1], self.pad_edges[1 - m2])],
            self.pad.at[self.at(self.margins[m1], self.margins[m2])],
            4 + 2 * m1 + m2,
            self.r.sides2[1 - m2].where,
        )

    def share(self, i, one, two):
        ref = self.pad.at[self.at(one, two)]
        return self.copy(ref, ref, 8 + i, self.partner)

    def share1(self, m):
        return self.share(m, self.margins[m], self.own)

    def share2(self, m):
        return self.share(2 + m, self.own, self.margins[m])

    def share_corner(self, m1, m2):
        return self.share(4 + 2 * m1 + m2, self.margins[m1], self.margins[m2])

    def begin(self):
        for m in range(2):
            when(self.r.sides1[1 - m].has)(self.strip1(m).start)
        for m in range(2):
            when(self.r.sides2[1 - m].has)(self.strip2(m).start)

    def relay(self):
        r = self.r
        for m1 in range(2):

            @when(r.sides1[m1].has)
            def _():
                self.strip1(m1).wait_recv()
                for m2 in range(2):
                    when(r.sides2[1 - m2].has)(self.corner(m1, m2).start)
                self.share1(m1).start()

        for m in range(2):

            @when(r.sides2[m].has)
            def _():
                self.strip2(m).wait_recv()
                self.share2(m).start()

        for m1 in range(2):
            for m2 in range(2):

                @when(r.sides1[m1].has, r.sides2[m2].has)
                def _():
                    self.corner(m1, m2).wait_recv()
                    self.share_corner(m1, m2).start()

    def arrive(self):
        r = self.r
        for m in range(2):
            when(r.sides1[m].has)(self.share1(m).wait_recv)
            when(r.sides2[m].has)(self.share2(m).wait_recv)
        for m1 in range(2):
            for m2 in range(2):
                when(r.sides1[m1].has, r.sides2[m2].has)(self.share_corner(m1, m2).wait_recv)

    def finish(self):
        r = self.r
        for m in range(2):
            when(r.sides1[1 - m].has)(self.strip1(m).wait_send)
            when(r.sides2[1 - m].has)(self.strip2(m).wait_send)
            when(r.sides1[m].has)(self.share1(m).wait_send)
            when(r.sides2[m].has)(self.share2(m).wait_send)
        for m1 in range(2):
            for m2 in range(2):
                when(r.sides1[m1].has, r.sides2[1 - m2].has)(self.corner(m1, m2).wait_send)
                when(r.sides1[m1].has, r.sides2[m2].has)(self.share_corner(m1, m2).wait_send)


class Fold:
    def __init__(self, role, mine, theirs, pair, acc, rims, core, send, recv, partner):
        self.r, self.mine, self.theirs, self.pair, self.acc = role, mine, theirs, pair, acc
        self.xr1, self.xr2, self.zr1, self.zr2 = rims
        self.core, self.send, self.recv, self.partner = core, send, recv, partner
        w = acc.shape[-1]
        self.w, self.q4 = w, w // 4

    def pieces(self, rows):
        q4, w = self.q4, self.w
        if rows:
            return [(pl.ds(0, 1),), (pl.ds(3, 1),), (pl.ds(1, 2),)]
        lead = (slice(None),) * 3
        return [lead + (pl.ds(0, q4),), lead + (pl.ds(3 * q4, q4),), lead + (pl.ds(q4, 2 * q4),)]

    def pair_copy(self, i, rows):
        at = self.pieces(rows)[i]
        return remote(self.theirs.at[at], self.pair.at[at], self.send.at[i], self.recv.at[i], self.partner)

    def begin(self):
        for i in range(3):
            self.pair_copy(i, not self.r.rows_first).start()

    def add(self, i):
        self.pair_copy(i, self.r.rows_first).wait_recv()
        at = self.pieces(self.r.rows_first)[i]
        self.acc[at] = self.mine[at] + self.pair[at]

    def rim_copy(self, stage, m):
        r, q4, w = self.r, self.q4, self.w
        rows = r.rows_first == (stage == 0)
        k = 1 - m
        if rows:
            cols = pl.ds(0, w) if stage == 0 else pl.ds(q4, 2 * q4)
            src = self.acc.at[3 * k, :, :, cols]
            rim = self.zr1 if stage == 0 else self.zr2
        else:
            groups = pl.ds(0, 4) if stage == 0 else pl.ds(1, 2)
            src = self.acc.at[groups, :, :, pl.ds(3 * k * q4, q4)]
            rim = self.xr1 if stage == 0 else self.xr2
        sides = r.sides1 if stage == 0 else r.sides2
        i = 3 + 2 * stage + m
        return remote(src, rim.at[m], self.send.at[i], self.recv.at[i], sides[k].where)

    def send_rims(self, stage):
        sides = self.r.sides1 if stage == 0 else self.r.sides2
        for m in range(2):
            when(sides[1 - m].has)(self.rim_copy(stage, m).start)

    def fold(self, stage):
        r, q4, w, acc = self.r, self.q4, self.w, self.acc
        rows = r.rows_first == (stage == 0)
        sides = r.sides1 if stage == 0 else r.sides2
        for m in range(2):

            @when(sides[m].has)
            def _():
                self.rim_copy(stage, m).wait_recv()
                if rows:
                    cols = pl.ds(0, w) if stage == 0 else pl.ds(q4, 2 * q4)
                    rim = self.zr1 if stage == 0 else self.zr2
                    acc[1 + m, :, :, cols] = acc[1 + m, :, :, cols] + rim[m]
                else:
                    groups = pl.ds(0, 4) if stage == 0 else pl.ds(1, 2)
                    cols = pl.ds((1 + m) * q4, q4)
                    rim = self.xr1 if stage == 0 else self.xr2
                    acc[groups, :, :, cols] = acc[groups, :, :, cols] + rim[m]

    def share_copy(self, q):
        return remote(self.core.at[q], self.core.at[q], self.send.at[7], self.recv.at[7], self.partner)

    def share(self):
        q4 = self.q4
        self.core[self.r.q] = self.acc[1:3, :, :, q4 : 3 * q4]
        self.share_copy(self.r.q).start()

    def arrive(self):
        self.share_copy(self.r.o).wait_recv()

    def finish(self):
        r = self.r
        for i in range(3):
            self.pair_copy(i, not r.rows_first).wait_send()
        for m in range(2):
            when(r.sides1[1 - m].has)(self.rim_copy(0, m).wait_send)
            when(r.sides2[1 - m].has)(self.rim_copy(1, m).wait_send)
        if self.core is not None:
            self.share_copy(r.q).wait_send()


class ProbeSum:
    def __init__(self, role, mine, theirs, ppair, pacc, p1, pr1, pr2, total, send, recv, partner):
        self.r, self.mine, self.theirs = role, mine, theirs
        self.ppair, self.pacc, self.p1 = ppair, pacc, p1
        self.pr1, self.pr2, self.total = pr1, pr2, total
        self.send, self.recv, self.partner = send, recv, partner

    def copy(self, src, dst, stage, d, where):
        return remote(src, dst, self.send.at[stage, d], self.recv.at[stage, d], where)

    def pair_copy(self):
        return self.copy(self.theirs, self.ppair, 0, 0, self.partner)

    def begin(self):
        self.pair_copy().start()

    def scatter1(self):
        r = self.r
        out = []
        for d in range(1, r.n1):
            j = lax.rem(r.me1 + d, r.n1)
            src = self.pacc.at[pl.ds(j * r.n2, r.n2)]
            out.append(self.copy(src, self.pr1.at[pl.ds(d * r.n2, r.n2)], 1, d, {r.axis1: j}))
        return out

    def scatter2(self):
        r = self.r
        out = []
        for d in range(1, r.n2):
            j = lax.rem(r.me2 + d, r.n2)
            out.append(self.copy(self.p1.at[pl.ds(j, 1)], self.pr2.at[pl.ds(d, 1)], 2, d, {r.axis2: j}))
        return out

    def gather2(self, back):
        r = self.r
        out = []
        for d in range(1, r.n2):
            j = lax.rem(r.me2 + d, r.n2)
            origin = lax.rem(r.me2 - d + r.n2, r.n2) if back else r.me2
            ref = self.total.at[r.q, pl.ds(r.me1 * r.n2 + origin, 1)]
            out.append(self.copy(ref, ref, 3, d, {r.axis2: j}))
        return out

    def gather1(self, back):
        r = self.r
        out = []
        for d in range(1, r.n1):
            j = lax.rem(r.me1 + d, r.n1)
            origin = lax.rem(r.me1 - d + r.n1, r.n1) if back else r.me1
            ref = self.total.at[r.q, pl.ds(origin * r.n2, r.n2)]
            out.append(self.copy(ref, ref, 4, d, {r.axis1: j}))
        return out

    def share_copy(self, d, sender):
        r = self.r
        origin = lax.rem(r.me1 - d + r.n1, r.n1)
        ref = self.total.at[r.q, pl.ds(origin * r.n2, r.n2)]
        return self.copy(ref, ref, 5, d, self.partner)

    def step1(self):
        self.pair_copy().wait_recv()
        self.pacc[...] = self.mine[...] + self.ppair[...]
        for c in self.scatter1():
            c.start()

    def step2(self):
        r = self.r
        mine = self.pacc[pl.ds(r.me1 * r.n2, r.n2)]
        for d, c in enumerate(self.scatter1(), 1):
            c.wait_recv()
            mine = mine + self.pr1[d * r.n2 : (d + 1) * r.n2]
        self.p1[0 : r.n2] = mine
        for c in self.scatter2():
            c.start()

    def step3(self):
        r = self.r
        one = self.p1[pl.ds(r.me2, 1)]
        for d, c in enumerate(self.scatter2(), 1):
            c.wait_recv()
            one = one + self.pr2[d : d + 1]
        self.total[r.q, pl.ds(r.me1 * r.n2 + r.me2, 1)] = one
        for c in self.gather2(0):
            c.start()

    def step4(self):
        for c in self.gather2(1):
            c.wait_recv()
        for c in self.gather1(0):
            c.start()
        self.share_copy(0, True).start()

    def step5(self):
        for d, c in enumerate(self.gather1(1), 1):
            c.wait_recv()
            self.share_copy(d, True).start()

    def arrive(self):
        for d in range(self.r.n1):
            self.share_copy(d, False).wait_recv()

    def finish(self):
        self.pair_copy().wait_send()
        for c in self.scatter1() + self.scatter2() + self.gather2(0) + self.gather1(0):
            c.wait_send()
        for d in range(self.r.n1):
            self.share_copy(d, True).wait_send()


def line_greet(nx, ny, partner):
    mx, my = lax.axis_index("scanx"), lax.axis_index("scany")
    greet(
        [(True, partner)]
        + [(True, {"scanx": lax.rem(mx + d, nx)}) for d in range(1, nx)]
        + [(True, {"scany": lax.rem(my + d, ny)}) for d in range(1, ny)]
    )


def each(step):
    p = lax.axis_index("pos")
    for q in range(2):
        pl.when(p == q)(functools.partial(step, q))


class Placer:
    def __init__(self, offsets, bufs, m, positions):
        self.bufs, self.m = bufs, m
        self.tall, self.span = m + 8, m + 128
        self.top = (bufs.shape[2] - self.tall // 8) // 2
        self.spots = []
        for j in range(positions):
            row, col = offsets[j, 0], offsets[j, 1]
            self.spots.append((lax.rem(row, 8), lax.rem(col, 128), lax.div(row, 8), lax.div(col, 128)))

    def clear(self):
        n, k, rows = self.bufs.shape[:3]
        bottom = self.top + self.tall // 8
        for j in range(n):
            for c in range(k):
                self.bufs[j, c, 0 : self.top] = jnp.zeros((self.top, *self.bufs.shape[3:]), jnp.float32)
                self.bufs[j, c, bottom:rows] = jnp.zeros((rows - bottom, *self.bufs.shape[3:]), jnp.float32)

    def put(self, j, k, term):
        row_in, col_in, _, step = self.spots[j]
        m, wide = self.m, self.bufs.shape[4]
        blank_rows = jnp.zeros((self.tall - m, m), jnp.float32)
        blank_cols = jnp.zeros((self.tall, self.span - m), jnp.float32)
        moved = pltpu.roll(jnp.concatenate([term, blank_rows], 0), row_in, 0)
        moved = pltpu.roll(jnp.concatenate([moved, blank_cols], 1), col_in, 1)
        out = None
        for d in range((wide - self.span) // 128 + 1):
            parts = [jnp.zeros((self.tall, w), jnp.float32) for w in (128 * d, wide - self.span - 128 * d)]
            here = jnp.concatenate([x for x in (parts[0], moved, parts[1]) if x.shape[1]], 1)
            out = here if out is None else jnp.where(step == d, here, out)
        self.bufs[j, k, self.top : self.top + self.tall // 8] = out.reshape(self.tall // 8, 8, wide)

    def rows(self, k, r0, count):
        out = None
        for j, (_, _, row, _) in enumerate(self.spots):
            part = self.bufs[j, k, pl.ds(self.top - row + r0 // 8, count // 8)]
            out = part if out is None else out + part
        return out.reshape(count, self.bufs.shape[4])

    def window(self, j, pad, k):
        row_in, col_in, row, step = self.spots[j]
        wide = pad.shape[3]
        block = pad[k, pl.ds(row, self.tall // 8)].reshape(self.tall, wide)
        out = block[:, : self.span]
        for d in range(1, (wide - self.span) // 128 + 1):
            out = jnp.where(step == d, block[:, 128 * d : 128 * d + self.span], out)
        out = pltpu.roll(out, lax.rem(self.span - col_in, self.span), 1)[:, : self.m]
        return pltpu.roll(out, lax.rem(self.tall - row_in, self.tall), 0)[: self.m]


def project(window, pr, pi, amplitude, table_a, table_b):
    m = pr.shape[0]
    bf = jnp.bfloat16
    ar, ai = window
    er = pr * ar - pi * ai
    ei = pr * ai + pi * ar
    left = dot(table_a[...], jnp.concatenate([er.astype(bf), ei.astype(bf)], 0)).astype(bf)
    far = dot(jnp.concatenate([left[:m], left[m:]], 1), table_b[...])
    fr, fi = far[:, :m], far[:, m:]
    ratio = amplitude.astype(jnp.float32) / jnp.maximum(jnp.sqrt(fr * fr + fi * fi), 0.2)
    projected = jnp.concatenate([(fr * ratio).astype(bf), (fi * ratio).astype(bf)], 0)
    back_half = dot(table_b[...], projected).astype(bf)
    back = dot(jnp.concatenate([back_half[:m], back_half[m:]], 1), table_a[...])
    return back[:, :m] - er, back[:, m:] - ei


def whole_kernel(nx, ny, step_size, *refs):
    offsets, spec, *given = refs[:6]
    new_spec, new_probe = refs[6:8]
    pad, probe, amplitudes, table_a, table_b, bufs, grad, prob, total, light_all = refs[8:18]
    (pair, acc, xr1, xr2, zr1, zr2, ipair, iacc, ixr1, ixr2, izr1, izr2) = refs[18:30]
    (ppair, pacc, p1, pr1, pr2) = refs[30:35]
    (hsend, hrecv, local, gsend, grecv, isend, irecv, psend, precv) = refs[35:]
    tile, m = spec.shape[3], probe.shape[1]
    wide = pad.shape[3]
    half = (wide - tile) // 2
    h = grad.shape[3]
    positions = amplitudes.shape[0]
    p = lax.axis_index("pos")
    partner = {"pos": 1 - p}
    loads = [pltpu.make_async_copy(spec, pad.at[:, pl.ds(half // 8, tile // 8), :, pl.ds(half, tile)], local.at[0])]
    for i, (src, dst) in enumerate(zip(given, (probe, amplitudes, table_a, table_b)), 1):
        loads.append(pltpu.make_async_copy(src, dst, local.at[i]))
    for c in loads:
        c.start()
    line_greet(nx, ny, partner)
    roles = [Role(q, nx, ny) for q in range(2)]
    sides = roles[1].sides1 + roles[0].sides1
    halos = [Halo(r, spec, pad, hsend, hrecv, partner) for r in roles]
    folds = [
        Fold(r, grad.at[r.q], grad.at[r.o], pair, acc, (xr1, xr2, zr1, zr2), None, gsend, grecv, partner)
        for r in roles
    ]
    lights = [
        Fold(
            r,
            grad.at[2, :, pl.ds(r.q, 1)],
            grad.at[2, :, pl.ds(r.o, 1)],
            ipair,
            iacc,
            (ixr1, ixr2, izr1, izr2),
            light_all,
            isend,
            irecv,
            partner,
        )
        for r in roles
    ]
    probes = [
        ProbeSum(r, prob.at[r.q], prob.at[r.o], ppair, pacc, p1, pr1, pr2, total, psend, precv, partner)
        for r in roles
    ]
    placer = Placer(offsets, bufs, m, positions)

    def gather(k):
        for g in range(4):
            for b in range(2):
                grad[k, g, b] = placer.rows(k, (2 * g + b) * h, h)

    each(lambda q: halos[q].begin())
    for i, at in enumerate(
        (
            (slice(None), pl.ds(0, half // 8)),
            (slice(None), pl.ds((half + tile) // 8, half // 8)),
            (slice(None), slice(None), slice(None), pl.ds(0, half)),
            (slice(None), slice(None), slice(None), pl.ds(half + tile, half)),
        )
    ):

        @pl.when(jnp.logical_not(sides[i].has))
        def _(at=at):
            pad[at] = jnp.zeros(pad.at[at].shape, pad.dtype)

    placer.clear()
    loads[1].wait()
    power = probe[0] * probe[0] + probe[1] * probe[1]
    for j in range(positions):
        placer.put(j, 2, power)
    gather(2)
    each(lambda q: lights[q].begin())

    def rest(q):
        halos[q].relay()
        halos[1 - q].arrive()
        lights[q].add(0)
        lights[q].add(1)
        lights[q].send_rims(0)
        lights[q].add(2)

    each(rest)
    for c in loads[:1] + loads[2:]:
        c.wait()
    sums = [None, None]
    for j in range(positions):
        ar, ai = placer.window(j, pad, 0), placer.window(j, pad, 1)
        pr, pi = probe[0], probe[1]
        dr, di = project((ar, ai), pr, pi, amplitudes[j], table_a, table_b)
        for k, t in enumerate((ar * dr + ai * di, ar * di - ai * dr)):
            sums[k] = t if sums[k] is None else sums[k] + t
        placer.put(j, 0, pr * dr + pi * di)
        placer.put(j, 1, pr * di - pi * dr)
        if j == 0:

            def light_mid(q):
                lights[q].fold(0)
                lights[q].send_rims(1)

            each(light_mid)
    n, s, lanes = prob.shape[1:]
    for k in range(2):
        for c in range(n):
            r0, l0 = c * s % m, c * s // m * lanes
            prob[k, c] = sums[k][r0 : r0 + s, l0 : l0 + lanes]
    each(lambda q: probes[q].begin())
    gather(0)
    gather(1)

    def update(q):
        q4 = folds[q].q4
        for g in range(2):
            for b in range(2):
                r0 = (2 * g + b) * h
                old = pad[q, (half + r0) // 8 : (half + r0 + h) // 8, :, half : half + tile].reshape(h, tile)
                new_spec[q, r0 : r0 + h] = old + acc[1 + g, b, :, q4 : 3 * q4] / (light_all[b, g, 0] + 1.0)

    def share_copy(q):
        return remote(new_spec.at[q], new_spec.at[q], gsend.at[7], grecv.at[7], partner)

    def objects(q):
        probe_sum, fold, light = probes[q], folds[q], lights[q]
        fold.begin()
        light.fold(1)
        light.share()
        probe_sum.step1()
        fold.add(0)
        fold.add(1)
        fold.send_rims(0)
        fold.add(2)
        probe_sum.step2()
        fold.fold(0)
        fold.send_rims(1)
        probe_sum.step3()
        light.arrive()
        fold.fold(1)
        update(q)
        share_copy(q).start()
        probe_sum.step4()

    each(objects)

    def closing(q):
        probes[q].step5()
        probes[1 - q].arrive()
        share_copy(1 - q).wait_recv()
        share_copy(q).wait_send()
        lights[q].finish()
        folds[q].finish()
        probes[q].finish()
        halos[q].finish()

    each(closing)
    for k in range(2):
        for c in range(n):
            rows = slice(c * s % m, c * s % m + s)
            cols = slice(c * s // m * lanes, c * s // m * lanes + lanes)
            new_probe[k, rows, cols] = probe[k, rows, cols] + total[k, c] * step_size


def tables(length):
    index = np.arange(length)
    angle = ((index[:, None] * index[None, :]) % length).astype(np.float32) * np.float32(2.0 * math.pi / length)
    scale = np.float32(1.0 / math.sqrt(length))
    c = np.cos(angle) * scale
    s = np.sin(angle) * scale
    a = np.block([[c, s], [-s, c]]).astype(jnp.bfloat16)
    b = np.block([[c, -s], [s, c]]).astype(jnp.bfloat16)
    return a, b


def shards(nx, ny, consts, specimen, probe_wave, amplitudes, offsets):
    m = probe_wave.shape[1]
    tile = specimen.shape[1]
    wide = tile + m
    f32 = jnp.float32
    vm = pl.BlockSpec(memory_space=VMEM)
    sm = pl.BlockSpec(memory_space=pltpu.SMEM)
    hbm = pl.BlockSpec(memory_space=pltpu.HBM)
    dma = pltpu.SemaphoreType.DMA
    lanes = 128
    n = nx * ny
    s = m * m // lanes // n
    h = wide // 8
    most = max(nx, ny)
    positions = offsets.shape[0]
    held = (probe_wave, amplitudes, consts[0], consts[1])

    def field(size):
        return [
            VMEM((4, size, h, wide), f32),
            VMEM((4, size, h, wide), f32),
            VMEM((2, 4, size, h, wide // 4), f32),
            VMEM((2, 2, size, h, wide // 4), f32),
            VMEM((2, size, h, wide), f32),
            VMEM((2, size, h, wide // 2), f32),
        ]

    step_size = 1.0 / math.sqrt(positions * n * 2)
    return pl.pallas_call(
        functools.partial(whole_kernel, nx, ny, step_size),
        out_shape=[VMEM(specimen.shape, f32), VMEM(probe_wave.shape, f32)],
        in_specs=[sm] + [hbm] * 5,
        out_specs=[vm, vm],
        scratch_shapes=[
            VMEM((2, wide // 8, 8, wide), f32),
            *[VMEM(x.shape, x.dtype) for x in held],
            VMEM((positions, 3, (2 * (tile - 8) + m + 8) // 8, 8, wide), f32),
            VMEM((3, 4, 2, h, wide), f32),
            VMEM((2, n, s, lanes), f32),
            VMEM((2, n, s, lanes), f32),
            VMEM((2, 2, 1, h, wide // 2), f32),
            *field(2),
            *field(1),
            VMEM((n, s, lanes), f32),
            VMEM((n, s, lanes), f32),
            VMEM((most, s, lanes), f32),
            VMEM((n, s, lanes), f32),
            VMEM((most, s, lanes), f32),
            dma((16,)),
            dma((16,)),
            dma((5,)),
            dma((8,)),
            dma((8,)),
            dma((8,)),
            dma((8,)),
            dma((6, most)),
            dma((6, most)),
        ],
        compiler_params=pltpu.CompilerParams(vmem_limit_bytes=56 * 2**20, collective_id=0, has_side_effects=True),
        name="whole",
    )(offsets, *[pltpu.with_memory_space_constraint(x, pltpu.HBM) for x in (specimen.reshape(2, tile // 8, 8, tile), *held)])


def solution(mesh):
    nx, ny = mesh.shape["scanx"], mesh.shape["scany"]

    def run(specimen, probe_wave, amplitudes, offsets):
        consts = tables(probe_wave.shape[2])
        return jax.shard_map(
            lambda *args: shards(nx, ny, [jnp.asarray(t) for t in consts], *args),
            mesh=mesh,
            in_specs=(
                P(None, ("groups", "scanx"), "scany"),
                P(None, "groups", None),
                P(("groups", "scanx", "scany", "pos"), None, None),
                P(("groups", "scanx", "scany", "pos"), None),
            ),
            out_specs=(P(None, ("groups", "scanx"), "scany"), P(None, "groups", None)),
            check_vma=False,
        )(specimen, probe_wave, amplitudes, offsets)

    return run
```

```python
import functools
import math

import jax
import jax.numpy as jnp
import numpy as np
from jax import lax
from jax.experimental import pallas as pl
from jax.experimental.pallas import tpu as pltpu
from jax.sharding import PartitionSpec as P

MESH = pl.DeviceIdType.MESH
VMEM = pltpu.VMEM


def remote(src, dst, send, recv, where):
    return pltpu.make_async_remote_copy(
        src_ref=src, dst_ref=dst, send_sem=send, recv_sem=recv, device_id=where, device_id_type=MESH
    )


def greet(conditions_devices):
    barrier = pltpu.get_barrier_semaphore()
    for present, where in conditions_devices:
        if present is True:
            pl.semaphore_signal(barrier, inc=1, device_id=where, device_id_type=MESH)
        else:

            @pl.when(present)
            def _(where=where):
                pl.semaphore_signal(barrier, inc=1, device_id=where, device_id_type=MESH)

    fixed = sum(1 for present, _ in conditions_devices if present is True)
    peers = [present.astype(jnp.int32) for present, _ in conditions_devices if present is not True]
    pl.semaphore_wait(barrier, sum(peers, fixed))


class Side:
    def __init__(self, axis, count, step):
        me = lax.axis_index(axis)
        self.has = me > 0 if step < 0 else me < count - 1
        self.where = {axis: me + step}


class Role:
    def __init__(self, q, nx, ny, order=None):
        order = q if order is None else order
        along_x = ("scanx", nx, Side("scanx", nx, -1), Side("scanx", nx, 1))
        along_y = ("scany", ny, Side("scany", ny, -1), Side("scany", ny, 1))
        one, two = (along_y, along_x) if order == 0 else (along_x, along_y)
        self.q, self.o, self.rows_first = q, 1 - q, order == 1
        self.axis1, self.n1, self.sides1 = one[0], one[1], one[2:]
        self.axis2, self.n2, self.sides2 = two[0], two[1], two[2:]
        self.me1, self.me2 = lax.axis_index(self.axis1), lax.axis_index(self.axis2)


def when(*conditions):
    return pl.when(functools.reduce(jnp.logical_and, conditions))


def dot(a, b):
    return jnp.dot(a, b, preferred_element_type=jnp.float32)


class Halo:
    def __init__(self, role, spec, pad, send, recv, partner):
        self.r, self.spec, self.pad, self.partner = role, spec, pad, partner
        self.send, self.recv = send, recv
        tile = spec.shape[3]
        half = (pad.shape[3] - tile) // 2
        self.own = (half, tile)
        self.margins = ((0, half), (half + tile, half))
        self.edges = ((0, half), (tile - half, half))
        self.pad_edges = ((half, half), (tile, half))
        self.whole = (0, tile)

    def at(self, one, two):
        rows, cols = (one, two) if self.r.rows_first else (two, one)
        return (self.r.q, pl.ds(rows[0] // 8, rows[1] // 8), slice(None), pl.ds(*cols))

    def copy(self, src, dst, i, where):
        return remote(src, dst, self.send.at[i], self.recv.at[i], where)

    def strip1(self, m, e):
        return self.copy(
            self.spec.at[self.at(self.edges[1 - m], self.edges[e])],
            self.pad.at[self.at(self.margins[m], self.pad_edges[e])],
            2 * m + e,
            self.r.sides1[1 - m].where,
        )

    def strip2(self, m):
        return self.copy(
            self.spec.at[self.at(self.whole, self.edges[1 - m])],
            self.pad.at[self.at(self.own, self.margins[m])],
            4 + m,
            self.r.sides2[1 - m].where,
        )

    def corner(self, m1, m2):
        return self.copy(
            self.pad.at[self.at(self.margins[m1], self.pad_edges[1 - m2])],
            self.pad.at[self.at(self.margins[m1], self.margins[m2])],
            6 + 2 * m1 + m2,
            self.r.sides2[1 - m2].where,
        )

    def share(self, i, one, two):
        ref = self.pad.at[self.at(one, two)]
        return self.copy(ref, ref, 10 + i, self.partner)

    def share1(self, m, e):
        return self.share(2 * m + e, self.margins[m], self.pad_edges[e])

    def share2(self, m):
        return self.share(4 + m, self.own, self.margins[m])

    def share_corner(self, m1, m2):
        return self.share(6 + 2 * m1 + m2, self.margins[m1], self.margins[m2])

    def begin(self):
        r = self.r
        for m in range(2):
            for e in range(2):
                when(r.sides1[1 - m].has, r.sides2[e].has)(self.strip1(m, e).start)
        for m in range(2):
            when(r.sides2[1 - m].has)(self.strip2(m).start)
        for m in range(2):
            for e in range(2):
                when(r.sides1[1 - m].has, jnp.logical_not(r.sides2[e].has))(self.strip1(m, e).start)

    def relay(self):
        r = self.r
        for m1 in range(2):
            for e in range(2):

                @when(r.sides1[m1].has, r.sides2[e].has)
                def _():
                    self.strip1(m1, e).wait_recv()
                    self.corner(m1, 1 - e).start()
                    self.share1(m1, e).start()

        for m in range(2):

            @when(r.sides2[m].has)
            def _():
                self.strip2(m).wait_recv()
                self.share2(m).start()

        for m1 in range(2):
            for e in range(2):

                @when(r.sides1[m1].has, jnp.logical_not(r.sides2[e].has))
                def _():
                    self.strip1(m1, e).wait_recv()
                    self.share1(m1, e).start()

    def relay_corners(self):
        r = self.r
        for m1 in range(2):
            for m2 in range(2):

                @when(r.sides1[m1].has, r.sides2[m2].has)
                def _():
                    self.corner(m1, m2).wait_recv()
                    self.share_corner(m1, m2).start()

    def arrive(self):
        r = self.r
        for m in range(2):
            for e in range(2):
                when(r.sides1[m].has)(self.share1(m, e).wait_recv)
            when(r.sides2[m].has)(self.share2(m).wait_recv)
        for m1 in range(2):
            for m2 in range(2):
                when(r.sides1[m1].has, r.sides2[m2].has)(self.share_corner(m1, m2).wait_recv)

    def finish(self):
        r = self.r
        for m in range(2):
            for e in range(2):
                when(r.sides1[1 - m].has)(self.strip1(m, e).wait_send)
                when(r.sides1[m].has)(self.share1(m, e).wait_send)
            when(r.sides2[1 - m].has)(self.strip2(m).wait_send)
            when(r.sides2[m].has)(self.share2(m).wait_send)
        for m1 in range(2):
            for m2 in range(2):
                when(r.sides1[m1].has, r.sides2[1 - m2].has)(self.corner(m1, m2).wait_send)
                when(r.sides1[m1].has, r.sides2[m2].has)(self.share_corner(m1, m2).wait_send)


class Fold:
    def __init__(self, role, mine, theirs, pair, acc, rims, core, send, recv, partner):
        self.r, self.mine, self.theirs, self.pair, self.acc = role, mine, theirs, pair, acc
        self.rims = rims
        self.core, self.send, self.recv, self.partner = core, send, recv, partner
        w = acc.shape[-1]
        self.w, self.q4 = w, w // 4

    def piece(self, i):
        q4, cols = self.q4, (slice(None),) * 3
        if self.r.rows_first:
            return ((pl.ds(0, 1),), (pl.ds(3, 1),), (pl.ds(1, 2),))[i]
        return cols + ((pl.ds(0, q4),), (pl.ds(3 * q4, q4),), (pl.ds(q4, 2 * q4),))[i]

    def needed(self, i):
        return pl.when(self.r.sides1[i].has) if i < 2 else lambda f: f()

    def pair_copy(self, i):
        at = self.piece(i)
        return remote(self.theirs.at[at], self.pair.at[at], self.send.at[i], self.recv.at[i], self.partner)

    def begin(self):
        for i in range(3):
            self.needed(i)(self.pair_copy(i).start)

    def add(self, i):
        @self.needed(i)
        def _():
            self.pair_copy(i).wait_recv()
            at = self.piece(i)
            self.acc[at] = self.mine[at] + self.pair[at]

    def rim_copy(self, stage, m):
        r, q4, w = self.r, self.q4, self.w
        rows = r.rows_first == (stage == 0)
        k = 1 - m
        if rows:
            cols = pl.ds(0, w) if stage == 0 else pl.ds(q4, 2 * q4)
            src = self.acc.at[3 * k, :, :, cols]
        else:
            groups = pl.ds(0, 4) if stage == 0 else pl.ds(1, 2)
            src = self.acc.at[groups, :, :, pl.ds(3 * k * q4, q4)]
        rim = self.rims[stage]
        sides = r.sides1 if stage == 0 else r.sides2
        i = 3 + 2 * stage + m
        return remote(src, rim.at[m], self.send.at[i], self.recv.at[i], sides[k].where)

    def send_rims(self, stage):
        sides = self.r.sides1 if stage == 0 else self.r.sides2
        for m in range(2):
            when(sides[1 - m].has)(self.rim_copy(stage, m).start)

    def fold(self, stage):
        r, q4, w, acc = self.r, self.q4, self.w, self.acc
        rows = r.rows_first == (stage == 0)
        sides = r.sides1 if stage == 0 else r.sides2
        for m in range(2):

            @when(sides[m].has)
            def _():
                self.rim_copy(stage, m).wait_recv()
                if rows:
                    cols = pl.ds(0, w) if stage == 0 else pl.ds(q4, 2 * q4)
                    rim = self.rims[stage]
                    acc[1 + m, :, :, cols] = acc[1 + m, :, :, cols] + rim[m]
                else:
                    groups = pl.ds(0, 4) if stage == 0 else pl.ds(1, 2)
                    cols = pl.ds((1 + m) * q4, q4)
                    rim = self.rims[stage]
                    acc[groups, :, :, cols] = acc[groups, :, :, cols] + rim[m]

    def share_copy(self, q):
        return remote(self.core.at[q], self.core.at[q], self.send.at[7], self.recv.at[7], self.partner)

    def share(self):
        q4 = self.q4
        self.core[self.r.q] = self.acc[1:3, :, :, q4 : 3 * q4]
        self.share_copy(self.r.q).start()

    def arrive(self):
        self.share_copy(self.r.o).wait_recv()

    def finish(self):
        r = self.r
        for i in range(3):
            self.needed(i)(self.pair_copy(i).wait_send)
        for m in range(2):
            when(r.sides1[1 - m].has)(self.rim_copy(0, m).wait_send)
            when(r.sides2[1 - m].has)(self.rim_copy(1, m).wait_send)
        if self.core is not None:
            self.share_copy(r.q).wait_send()


class ProbeSum:
    def __init__(self, q, nx, ny, prob, ppair, held, inner, hub, part, total, send, recv, partner):
        self.q, self.ny = q, ny
        self.prob, self.ppair, self.held = prob, ppair, held
        self.inner, self.hub, self.part, self.total = inner, hub, part, total
        self.send, self.recv, self.partner = send, recv, partner
        self.chunks = send.shape[1]
        self.rows = prob.shape[1] // self.chunks
        me, mid = lax.axis_index("scanx"), nx // 2
        step = 2 * (me < mid).astype(jnp.int32) - 1
        self.to_inner, self.to_outer = {"scanx": me + step}, {"scanx": me - step}
        self.has_outer = jnp.logical_and(me > 0, me < nx - 1)
        self.no_outer = jnp.logical_not(self.has_outer)
        self.is_hub = jnp.logical_or(me == mid - 1, me == mid)
        self.not_hub = jnp.logical_not(self.is_hub)
        self.mine = lax.axis_index("scany")

    def at(self, c):
        return pl.ds(c * self.rows, self.rows)

    def copy(self, src, dst, s, r, c, where):
        return remote(src.at[self.at(c)], dst.at[self.at(c)], self.send.at[s, c], self.recv.at[r, c], where)

    def pair(self, c):
        return self.copy(self.prob.at[1 - self.q], self.ppair, 0, 0, c, self.partner)

    def inward(self, c):
        return self.copy(self.part, self.inner, 1, 1, c, self.to_inner)

    def across(self, c):
        return self.copy(self.part, self.hub, 1, 2, c, self.to_inner)

    def outward(self, c, src):
        return self.copy(src, self.hub, 2, 2, c, self.to_outer)

    def share(self, c, q):
        return self.copy(self.total.at[q], self.total.at[q], 3, 3, c, self.partner)

    def sides(self, c):
        out = []
        for d in range(1, self.ny):
            slot = self.held.at[self.mine]
            out.append(self.copy(slot, slot, 3 + d, 3 + d, c, {"scany": lax.rem(self.mine + d, self.ny)}))
        return out

    def side_arrive(self, c):
        for d in range(1, self.ny):
            slot = self.held.at[lax.rem(self.mine - d + self.ny, self.ny)]
            self.copy(slot, slot, 3 + d, 3 + d, c, self.partner).wait_recv()

    def side_sum(self, c):
        self.side_arrive(c)
        out = self.held[0, self.at(c)]
        for i in range(1, self.ny):
            out = out + self.held[i, self.at(c)]
        return out

    def pair_sum(self, c):
        self.pair(c).wait_recv()
        return self.prob[self.q, self.at(c)] + self.ppair[self.at(c)]

    def send_sides(self, c, value):
        self.held[self.mine, self.at(c)] = value
        for copy in self.sides(c):
            copy.start()

    def send_inward(self, c):
        when(self.not_hub)(self.inward(c).start)
        when(self.is_hub)(self.across(c).start)

    def collect(self):
        @pl.when(self.has_outer)
        def _():
            for c in range(self.chunks):
                self.inward(c).wait_recv()
                self.part[self.at(c)] = self.part[self.at(c)] + self.inner[self.at(c)]
                self.send_inward(c)

    def start_part(self, c, value):
        self.part[self.at(c)] = value
        when(self.no_outer)(functools.partial(self.send_inward, c))

    def from_hub(self, hubs, after, chunks=None):
        @pl.when(self.is_hub if hubs else self.not_hub)
        def _():
            for c in chunks or range(self.chunks):
                self.across(c).wait_recv()
                value = self.hub[self.at(c)]
                after(c, self.part[self.at(c)] + value if hubs else value)

    def finish(self, src):
        for c in range(self.chunks):
            self.pair(c).wait_send()
            self.inward(c).wait_send()
            when(self.has_outer)(self.outward(c, src).wait_send)
            self.share(c, self.q).wait_send()
            for copy in self.sides(c):
                copy.wait_send()


class SideFirst(ProbeSum):
    def one(self):
        for c in range(self.chunks):
            self.send_sides(c, self.pair_sum(c))

    def two(self):
        for c in range(self.chunks):
            self.start_part(c, self.side_sum(c))
        self.collect()

    def done(self, c, value):
        self.total[self.q, self.at(c)] = value
        when(self.has_outer)(self.outward(c, self.total.at[self.q]).start)
        self.share(c, self.q).start()

    def three(self, chunks=None):
        self.from_hub(True, self.done, chunks)

    def four(self):
        self.from_hub(False, self.done)

    def five(self):
        pass

    def end(self):
        self.finish(self.total.at[self.q])


class ChainFirst(ProbeSum):
    def one(self):
        for c in range(self.chunks):
            self.start_part(c, self.pair_sum(c))

    def two(self):
        self.collect()

    def done(self, c, value):
        self.send_sides(c, value)
        when(self.has_outer)(self.outward(c, self.held.at[self.mine]).start)

    def three(self, chunks=None):
        self.from_hub(True, self.done, chunks)

    def four(self):
        self.from_hub(False, self.done)

    def five(self):
        for c in range(self.chunks):
            self.total[self.q, self.at(c)] = self.side_sum(c)
            self.share(c, self.q).start()

    def end(self):
        self.finish(self.held.at[self.mine])


def near_greet(ny, partner, sides):
    my = lax.axis_index("scany")
    greet(
        [(True, partner)]
        + [(True, {"scany": lax.rem(my + d, ny)}) for d in range(1, ny)]
        + [(side.has, side.where) for side in sides]
    )


def each(step):
    p = lax.axis_index("pos")
    for q in range(2):
        pl.when(p == q)(functools.partial(step, q))


class Placer:
    def __init__(self, offsets, bufs, m, positions):
        self.bufs, self.m = bufs, m
        self.tall, self.span = m + 8, m + 128
        self.top = (bufs.shape[2] - self.tall // 8) // 2
        self.spots = []
        for j in range(positions):
            row, col = offsets[j, 0], offsets[j, 1]
            self.spots.append((lax.rem(row, 8), lax.rem(col, 128), lax.div(row, 8), lax.div(col, 128)))

    def clear(self):
        n, k, rows = self.bufs.shape[:3]
        bottom = self.top + self.tall // 8
        for j in range(n):
            for c in range(k):
                self.bufs[j, c, 0 : self.top] = jnp.zeros((self.top, *self.bufs.shape[3:]), jnp.float32)
                self.bufs[j, c, bottom:rows] = jnp.zeros((rows - bottom, *self.bufs.shape[3:]), jnp.float32)

    def put(self, j, k, term):
        row_in, col_in, _, step = self.spots[j]
        m, wide = self.m, self.bufs.shape[4]
        blank_rows = jnp.zeros((self.tall - m, m), jnp.float32)
        blank_cols = jnp.zeros((self.tall, self.span - m), jnp.float32)
        moved = pltpu.roll(jnp.concatenate([term, blank_rows], 0), row_in, 0)
        moved = pltpu.roll(jnp.concatenate([moved, blank_cols], 1), col_in, 1)
        out = None
        for d in range((wide - self.span) // 128 + 1):
            parts = [jnp.zeros((self.tall, w), jnp.float32) for w in (128 * d, wide - self.span - 128 * d)]
            here = jnp.concatenate([x for x in (parts[0], moved, parts[1]) if x.shape[1]], 1)
            out = here if out is None else jnp.where(step == d, here, out)
        self.bufs[j, k, self.top : self.top + self.tall // 8] = out.reshape(self.tall // 8, 8, wide)

    def rows(self, k, r0, count):
        out = None
        for j, (_, _, row, _) in enumerate(self.spots):
            part = self.bufs[j, k, pl.ds(self.top - row + r0 // 8, count // 8)]
            out = part if out is None else out + part
        return out.reshape(count, self.bufs.shape[4])

    def window(self, j, pad, k):
        row_in, col_in, row, step = self.spots[j]
        wide = pad.shape[3]
        block = pad[k, pl.ds(row, self.tall // 8)].reshape(self.tall, wide)
        out = block[:, : self.span]
        for d in range(1, (wide - self.span) // 128 + 1):
            out = jnp.where(step == d, block[:, 128 * d : 128 * d + self.span], out)
        out = pltpu.roll(out, lax.rem(self.span - col_in, self.span), 1)[:, : self.m]
        return pltpu.roll(out, lax.rem(self.tall - row_in, self.tall), 0)[: self.m]


def forward(window, pr, pi, table_a, table_b):
    m = pr.shape[0]
    bf = jnp.bfloat16
    ar, ai = window
    er = pr * ar - pi * ai
    ei = pr * ai + pi * ar
    left = dot(table_a[...], jnp.concatenate([er.astype(bf), ei.astype(bf)], 0)).astype(bf)
    return er, ei, dot(jnp.concatenate([left[:m], left[m:]], 1), table_b[...])


def backward(er, ei, far, amplitude, table_a, table_b):
    m = er.shape[0]
    bf = jnp.bfloat16
    fr, fi = far[:, :m], far[:, m:]
    ratio = amplitude.astype(jnp.float32) / jnp.maximum(jnp.sqrt(fr * fr + fi * fi), 0.2)
    projected = jnp.concatenate([(fr * ratio).astype(bf), (fi * ratio).astype(bf)], 0)
    back_half = dot(table_b[...], projected).astype(bf)
    back = dot(jnp.concatenate([back_half[:m], back_half[m:]], 1), table_a[...])
    return back[:, :m] - er, back[:, m:] - ei


def whole_kernel(nx, ny, step_size, *refs):
    offsets, spec, *given = refs[:6]
    new_spec, new_probe = refs[6:8]
    pad, probe, amplitudes, table_a, table_b, bufs, grad, prob, total, light_all = refs[8:18]
    pair, acc, xr, zr, ipair, iacc, ixr, izr, ppair, held, inner, hub, part = refs[18:31]
    hsend, hrecv, local, gsend, grecv, isend, irecv, psend, precv = refs[31:]
    tile, m = spec.shape[3], probe.shape[1]
    wide = pad.shape[3]
    half = (wide - tile) // 2
    h = grad.shape[3]
    positions, chunks = amplitudes.shape[0], psend.shape[1]
    p = lax.axis_index("pos")
    partner = {"pos": 1 - p}
    loads = [pltpu.make_async_copy(spec, pad.at[:, pl.ds(half // 8, tile // 8), :, pl.ds(half, tile)], local.at[0])]
    for i, (src, dst) in enumerate(zip(given, (probe, amplitudes, table_a, table_b)), 1):
        loads.append(pltpu.make_async_copy(src, dst, local.at[i]))
    for c in loads:
        c.start()
    roles = [Role(q, nx, ny) for q in range(2)]
    sides = roles[1].sides1 + roles[0].sides1
    near_greet(ny, partner, roles[1].sides1)
    halos = [Halo(r, spec, pad, hsend, hrecv, partner) for r in roles]
    role = Role(p, nx, ny, 0)
    fold = Fold(role, grad.at[p], grad.at[1 - p], pair, acc, (xr, zr), None, gsend, grecv, partner)
    light = Fold(
        role,
        grad.at[2, :, pl.ds(p, 1)],
        grad.at[2, :, pl.ds(1 - p, 1)],
        ipair,
        iacc,
        (ixr, izr),
        light_all,
        isend,
        irecv,
        partner,
    )
    probes = [
        kind(q, nx, ny, prob, ppair, held, inner, hub, part, total, psend, precv, partner)
        for q, kind in enumerate((SideFirst, ChainFirst))
    ]
    placer = Placer(offsets, bufs, m, positions)

    def gather(k):
        for g in range(4):
            for b in range(2):
                grad[k, g, b] = placer.rows(k, (2 * g + b) * h, h)

    each(lambda q: halos[q].begin())
    for i, at in enumerate(
        (
            (slice(None), pl.ds(0, half // 8)),
            (slice(None), pl.ds((half + tile) // 8, half // 8)),
            (slice(None), slice(None), slice(None), pl.ds(0, half)),
            (slice(None), slice(None), slice(None), pl.ds(half + tile, half)),
        )
    ):

        @pl.when(jnp.logical_not(sides[i].has))
        def _(at=at):
            pad[at] = jnp.zeros(pad.at[at].shape, pad.dtype)

    placer.clear()
    loads[1].wait()
    power = probe[0] * probe[0] + probe[1] * probe[1]
    for j in range(positions):
        placer.put(j, 2, power)
    gather(2)
    light.begin()

    def strips(q):
        halos[q].relay()

    def corners(q):
        halos[q].relay_corners()
        halos[1 - q].arrive()

    each(strips)
    for i in range(3):
        light.add(i)
    light.send_rims(0)
    each(corners)
    for c in loads[:1] + loads[2:]:
        c.wait()
    pr, pi = probe[0], probe[1]
    windows = [[placer.window(j, pad, k) for k in range(2)] for j in range(positions)]
    fields = [forward(windows[j], pr, pi, table_a, table_b) for j in range(positions)]
    light.fold(0)
    light.send_rims(1)
    diffs = [backward(*fields[j], amplitudes[j], table_a, table_b) for j in range(positions)]
    sums = [None, None]
    for (ar, ai), (dr, di) in zip(windows, diffs):
        for k, t in enumerate((ar * dr + ai * di, ar * di - ai * dr)):
            sums[k] = t if sums[k] is None else sums[k] + t
    rows = m // chunks
    for c in range(chunks):
        at = pl.ds(c * rows, rows)
        for k in range(2):
            prob[k, at] = sums[k][c * rows : (c + 1) * rows]
        remote(prob.at[1 - p, at], ppair.at[at], psend.at[0, c], precv.at[0, c], partner).start()
    for j, (dr, di) in enumerate(diffs):
        placer.put(j, 0, pr * dr + pi * di)
        placer.put(j, 1, pr * di - pi * dr)
    gather(1 - p)
    fold.begin()
    gather(p)

    def update(q):
        q4 = fold.q4
        for g in range(2):
            for b in range(2):
                r0 = (2 * g + b) * h
                old = pad[q, (half + r0) // 8 : (half + r0 + h) // 8, :, half : half + tile].reshape(h, tile)
                new_spec[q, r0 : r0 + h] = old + acc[1 + g, b, :, q4 : 3 * q4] / (light_all[b, g, 0] + 1.0)

    def share_copy(q):
        return remote(new_spec.at[q], new_spec.at[q], gsend.at[7], grecv.at[7], partner)

    def object_last(q):
        light.arrive()
        fold.fold(1)
        update(q)
        share_copy(q).start()

    def objects(q):
        probe_sum = probes[q]
        probe_sum.one()
        fold.add(0)
        fold.add(1)
        fold.send_rims(0)
        fold.add(2)
        light.fold(1)
        light.share()
        probe_sum.two()
        if q == 0:
            probe_sum.three(range(chunks // 2))
            fold.fold(0)
            fold.send_rims(1)
            probe_sum.three(range(chunks // 2, chunks))
            probe_sum.four()
            object_last(q)
        else:
            probe_sum.three()
            probe_sum.four()
            fold.fold(0)
            fold.send_rims(1)
            probe_sum.five()
            object_last(q)

    each(objects)

    def closing(q):
        for c in range(chunks):
            probes[q].share(c, 1 - q).wait_recv()
        share_copy(1 - q).wait_recv()
        share_copy(q).wait_send()
        light.finish()
        fold.finish()
        probes[q].end()
        halos[q].finish()

    each(closing)
    for k in range(2):
        new_probe[k] = probe[k] + total[k] * step_size


def emit_kernel(spec, probe, new_spec, new_probe, sem):
    copies = [
        pltpu.make_async_copy(src.at[k], dst.at[k], sem.at[i, k])
        for i, (src, dst) in enumerate(((spec, new_spec), (probe, new_probe)))
        for k in range(2)
    ]
    for c in copies:
        c.start()
    for c in copies:
        c.wait()


def tables(length):
    index = np.arange(length)
    angle = ((index[:, None] * index[None, :]) % length).astype(np.float32) * np.float32(2.0 * math.pi / length)
    scale = np.float32(1.0 / math.sqrt(length))
    c = np.cos(angle) * scale
    s = np.sin(angle) * scale
    a = np.block([[c, s], [-s, c]]).astype(jnp.bfloat16)
    b = np.block([[c, -s], [s, c]]).astype(jnp.bfloat16)
    return a, b


def shards(nx, ny, consts, specimen, probe_wave, amplitudes, offsets):
    m = probe_wave.shape[1]
    tile = specimen.shape[1]
    wide = tile + m
    f32 = jnp.float32
    vm = pl.BlockSpec(memory_space=VMEM)
    sm = pl.BlockSpec(memory_space=pltpu.SMEM)
    hbm = pl.BlockSpec(memory_space=pltpu.HBM)
    dma = pltpu.SemaphoreType.DMA
    n = nx * ny
    h = wide // 8
    chunks = 4
    positions = offsets.shape[0]
    held = (probe_wave, amplitudes, consts[0], consts[1])

    def field(size):
        return [
            VMEM((4, size, h, wide), f32),
            VMEM((4, size, h, wide), f32),
            VMEM((2, 4, size, h, wide // 4), f32),
            VMEM((2, size, h, wide // 2), f32),
        ]

    step_size = 1.0 / math.sqrt(positions * n * 2)
    results = pl.pallas_call(
        functools.partial(whole_kernel, nx, ny, step_size),
        out_shape=[VMEM(specimen.shape, f32), VMEM(probe_wave.shape, f32)],
        in_specs=[sm] + [hbm] * 5,
        out_specs=[vm, vm],
        scratch_shapes=[
            VMEM((2, wide // 8, 8, wide), f32),
            *[VMEM(x.shape, x.dtype) for x in held],
            VMEM((positions, 3, (2 * (tile - 8) + m + 8) // 8, 8, wide), f32),
            VMEM((3, 4, 2, h, wide), f32),
            VMEM((2, m, m), f32),
            VMEM((2, m, m), f32),
            VMEM((2, 2, 1, h, wide // 2), f32),
            *field(2),
            *field(1),
            VMEM((m, m), f32),
            VMEM((ny, m, m), f32),
            VMEM((m, m), f32),
            VMEM((m, m), f32),
            VMEM((m, m), f32),
            dma((20,)),
            dma((20,)),
            dma((5,)),
            dma((8,)),
            dma((8,)),
            dma((8,)),
            dma((8,)),
            dma((3 + ny, chunks)),
            dma((3 + ny, chunks)),
        ],
        compiler_params=pltpu.CompilerParams(vmem_limit_bytes=56 * 2**20, collective_id=0, has_side_effects=True),
        name="whole",
    )(offsets, *[pltpu.with_memory_space_constraint(x, pltpu.HBM) for x in (specimen.reshape(2, tile // 8, 8, tile), *held)])
    return pl.pallas_call(
        emit_kernel,
        out_shape=[jax.ShapeDtypeStruct(specimen.shape, f32), jax.ShapeDtypeStruct(probe_wave.shape, f32)],
        in_specs=[vm] * 2,
        out_specs=[pl.BlockSpec(memory_space=pl.ANY)] * 2,
        scratch_shapes=[dma((2, 2))],
        compiler_params=pltpu.CompilerParams(vmem_limit_bytes=2 * 2**20),
        name="emit",
    )(*results)


def solution(mesh):
    nx, ny = mesh.shape["scanx"], mesh.shape["scany"]

    def run(specimen, probe_wave, amplitudes, offsets):
        consts = tables(probe_wave.shape[2])
        return jax.shard_map(
            lambda *args: shards(nx, ny, [jnp.asarray(t) for t in consts], *args),
            mesh=mesh,
            in_specs=(
                P(None, ("groups", "scanx"), "scany"),
                P(None, "groups", None),
                P(("groups", "scanx", "scany", "pos"), None, None),
                P(("groups", "scanx", "scany", "pos"), None),
            ),
            out_specs=(P(None, ("groups", "scanx"), "scany"), P(None, "groups", None)),
            check_vma=False,
        )(specimen, probe_wave, amplitudes, offsets)

    return run
```

```python
import functools
import math

import jax
import jax.numpy as jnp
import numpy as np
from jax import lax
from jax.experimental import pallas as pl
from jax.experimental.pallas import tpu as pltpu
from jax.sharding import PartitionSpec as P

MESH = pl.DeviceIdType.MESH
VMEM = pltpu.VMEM


def remote(src, dst, send, recv, where):
    return pltpu.make_async_remote_copy(
        src_ref=src, dst_ref=dst, send_sem=send, recv_sem=recv, device_id=where, device_id_type=MESH
    )


def greet(conditions_devices):
    barrier = pltpu.get_barrier_semaphore()
    for present, where in conditions_devices:
        if present is True:
            pl.semaphore_signal(barrier, inc=1, device_id=where, device_id_type=MESH)
        else:

            @pl.when(present)
            def _(where=where):
                pl.semaphore_signal(barrier, inc=1, device_id=where, device_id_type=MESH)

    fixed = sum(1 for present, _ in conditions_devices if present is True)
    peers = [present.astype(jnp.int32) for present, _ in conditions_devices if present is not True]
    pl.semaphore_wait(barrier, sum(peers, fixed))


class Side:
    def __init__(self, axis, count, step):
        me = lax.axis_index(axis)
        self.has = me > 0 if step < 0 else me < count - 1
        self.where = {axis: me + step}


class Role:
    def __init__(self, q, nx, ny, order=None):
        order = q if order is None else order
        along_x = ("scanx", nx, Side("scanx", nx, -1), Side("scanx", nx, 1))
        along_y = ("scany", ny, Side("scany", ny, -1), Side("scany", ny, 1))
        one, two = (along_y, along_x) if order == 0 else (along_x, along_y)
        self.q, self.o, self.rows_first = q, 1 - q, order == 1
        self.axis1, self.n1, self.sides1 = one[0], one[1], one[2:]
        self.axis2, self.n2, self.sides2 = two[0], two[1], two[2:]
        self.me1, self.me2 = lax.axis_index(self.axis1), lax.axis_index(self.axis2)


def when(*conditions):
    return pl.when(functools.reduce(jnp.logical_and, conditions))


def dot(a, b):
    return jnp.dot(a, b, preferred_element_type=jnp.float32)


class Halo:
    def __init__(self, role, spec, pad, send, recv, partner):
        self.r, self.spec, self.pad, self.partner = role, spec, pad, partner
        self.send, self.recv = send, recv
        tile = spec.shape[3]
        half = (pad.shape[3] - tile) // 2
        self.own = (half, tile)
        self.margins = ((0, half), (half + tile, half))
        self.edges = ((0, half), (tile - half, half))
        self.pad_edges = ((half, half), (tile, half))
        self.whole = (0, tile)

    def at(self, one, two):
        rows, cols = (one, two) if self.r.rows_first else (two, one)
        return (self.r.q, pl.ds(rows[0] // 8, rows[1] // 8), slice(None), pl.ds(*cols))

    def copy(self, src, dst, i, where):
        return remote(src, dst, self.send.at[i], self.recv.at[i], where)

    def strip1(self, m, e):
        return self.copy(
            self.spec.at[self.at(self.edges[1 - m], self.edges[e])],
            self.pad.at[self.at(self.margins[m], self.pad_edges[e])],
            2 * m + e,
            self.r.sides1[1 - m].where,
        )

    def strip2(self, m):
        return self.copy(
            self.spec.at[self.at(self.whole, self.edges[1 - m])],
            self.pad.at[self.at(self.own, self.margins[m])],
            4 + m,
            self.r.sides2[1 - m].where,
        )

    def corner(self, m1, m2):
        return self.copy(
            self.pad.at[self.at(self.margins[m1], self.pad_edges[1 - m2])],
            self.pad.at[self.at(self.margins[m1], self.margins[m2])],
            6 + 2 * m1 + m2,
            self.r.sides2[1 - m2].where,
        )

    def share(self, i, one, two):
        ref = self.pad.at[self.at(one, two)]
        return self.copy(ref, ref, 10 + i, self.partner)

    def share1(self, m, e):
        return self.share(2 * m + e, self.margins[m], self.pad_edges[e])

    def share2(self, m):
        return self.share(4 + m, self.own, self.margins[m])

    def share_corner(self, m1, m2):
        return self.share(6 + 2 * m1 + m2, self.margins[m1], self.margins[m2])

    def begin(self):
        r = self.r
        for m in range(2):
            for e in range(2):
                when(r.sides1[1 - m].has, r.sides2[e].has)(self.strip1(m, e).start)
        for m in range(2):
            when(r.sides2[1 - m].has)(self.strip2(m).start)
        for m in range(2):
            for e in range(2):
                when(r.sides1[1 - m].has, jnp.logical_not(r.sides2[e].has))(self.strip1(m, e).start)

    def relay(self):
        r = self.r
        for m1 in range(2):
            for e in range(2):

                @when(r.sides1[m1].has, r.sides2[e].has)
                def _():
                    self.strip1(m1, e).wait_recv()
                    self.corner(m1, 1 - e).start()
                    self.share1(m1, e).start()

        for m in range(2):

            @when(r.sides2[m].has)
            def _():
                self.strip2(m).wait_recv()
                self.share2(m).start()

        for m1 in range(2):
            for e in range(2):

                @when(r.sides1[m1].has, jnp.logical_not(r.sides2[e].has))
                def _():
                    self.strip1(m1, e).wait_recv()
                    self.share1(m1, e).start()

    def relay_corners(self):
        r = self.r
        for m1 in range(2):
            for m2 in range(2):

                @when(r.sides1[m1].has, r.sides2[m2].has)
                def _():
                    self.corner(m1, m2).wait_recv()
                    self.share_corner(m1, m2).start()

    def arrive(self):
        r = self.r
        for m in range(2):
            for e in range(2):
                when(r.sides1[m].has)(self.share1(m, e).wait_recv)
            when(r.sides2[m].has)(self.share2(m).wait_recv)
        for m1 in range(2):
            for m2 in range(2):
                when(r.sides1[m1].has, r.sides2[m2].has)(self.share_corner(m1, m2).wait_recv)

    def finish(self):
        r = self.r
        for m in range(2):
            for e in range(2):
                when(r.sides1[1 - m].has)(self.strip1(m, e).wait_send)
                when(r.sides1[m].has)(self.share1(m, e).wait_send)
            when(r.sides2[1 - m].has)(self.strip2(m).wait_send)
            when(r.sides2[m].has)(self.share2(m).wait_send)
        for m1 in range(2):
            for m2 in range(2):
                when(r.sides1[m1].has, r.sides2[1 - m2].has)(self.corner(m1, m2).wait_send)
                when(r.sides1[m1].has, r.sides2[m2].has)(self.share_corner(m1, m2).wait_send)


class Fold:
    def __init__(self, role, other, mine, theirs, pair, acc, rims, core, send, recv, partner):
        self.r, self.other, self.mine, self.theirs, self.pair, self.acc = role, other, mine, theirs, pair, acc
        self.rows1, self.cols1, self.rows2, self.cols2 = rims
        self.core, self.send, self.recv, self.partner = core, send, recv, partner
        w = acc.shape[-1]
        self.w, self.q4 = w, w // 4

    def piece(self, i, r):
        q4, cols = self.q4, (slice(None),) * 3
        if r.rows_first:
            return ((pl.ds(0, 1),), (pl.ds(3, 1),), (pl.ds(1, 2),))[i]
        return cols + ((pl.ds(0, q4),), (pl.ds(3 * q4, q4),), (pl.ds(q4, 2 * q4),))[i]

    def needed(self, i, r):
        return pl.when(r.sides1[i].has) if i < 2 else lambda f: f()

    def pair_copy(self, i, r):
        at = self.piece(i, r)
        return remote(self.theirs.at[at], self.pair.at[at], self.send.at[i], self.recv.at[i], self.partner)

    def begin(self):
        for i in range(3):
            self.needed(i, self.other)(self.pair_copy(i, self.other).start)

    def add(self, i):
        @self.needed(i, self.r)
        def _():
            self.pair_copy(i, self.r).wait_recv()
            at = self.piece(i, self.r)
            self.acc[at] = self.mine[at] + self.pair[at]

    def spot(self, stage, i, m):
        r, q4, w = self.r, self.q4, self.w
        if r.rows_first == (stage == 0):
            if stage == 1:
                return (i, slice(None), slice(None), pl.ds(q4, 2 * q4)), self.rows2.at[m]
            cols = pl.ds(0, w)
            if r.n2 == 2:
                cols = pl.ds(pl.multiple_of((1 - r.me2) * q4, q4), 3 * q4)
            return (i, slice(None), slice(None), cols), self.rows1.at[m, :, :, cols]
        groups = pl.ds(0, 4) if stage == 0 else pl.ds(1, 2)
        return (groups, slice(None), slice(None), pl.ds(i * q4, q4)), (self.cols1 if stage == 0 else self.cols2).at[m]

    def rim_copy(self, stage, m):
        sides = self.r.sides1 if stage == 0 else self.r.sides2
        at, rim = self.spot(stage, 3 * (1 - m), m)
        i = 3 + 2 * stage + m
        return remote(self.acc.at[at], rim, self.send.at[i], self.recv.at[i], sides[1 - m].where)

    def send_rims(self, stage):
        sides = self.r.sides1 if stage == 0 else self.r.sides2
        for m in range(2):
            when(sides[1 - m].has)(self.rim_copy(stage, m).start)

    def fold(self, stage):
        sides = self.r.sides1 if stage == 0 else self.r.sides2
        for m in range(2):

            @when(sides[m].has)
            def _():
                self.rim_copy(stage, m).wait_recv()
                at, rim = self.spot(stage, 1 + m, m)
                self.acc[at] = self.acc[at] + rim[...]

    def share_copy(self, q):
        return remote(self.core.at[q], self.core.at[q], self.send.at[7], self.recv.at[7], self.partner)

    def share(self):
        q4 = self.q4
        self.core[self.r.q] = self.acc[1:3, :, :, q4 : 3 * q4]
        self.share_copy(self.r.q).start()

    def arrive(self):
        self.share_copy(self.r.o).wait_recv()

    def finish(self):
        r = self.r
        for i in range(3):
            self.needed(i, self.other)(self.pair_copy(i, self.other).wait_send)
        for m in range(2):
            when(r.sides1[1 - m].has)(self.rim_copy(0, m).wait_send)
            when(r.sides2[1 - m].has)(self.rim_copy(1, m).wait_send)
        if self.core is not None:
            self.share_copy(r.q).wait_send()


class ProbeSum:
    def __init__(self, q, nx, ny, prob, ppair, held, inner, hub, part, total, send, recv, partner):
        self.q, self.ny = q, ny
        self.prob, self.ppair, self.held = prob, ppair, held
        self.inner, self.hub, self.part, self.total = inner, hub, part, total
        self.send, self.recv, self.partner = send, recv, partner
        self.chunks = send.shape[1]
        self.rows = prob.shape[1] // self.chunks
        me, mid = lax.axis_index("scanx"), nx // 2
        step = 2 * (me < mid).astype(jnp.int32) - 1
        self.to_inner, self.to_outer = {"scanx": me + step}, {"scanx": me - step}
        self.has_outer = jnp.logical_and(me > 0, me < nx - 1)
        self.no_outer = jnp.logical_not(self.has_outer)
        self.is_hub = jnp.logical_or(me == mid - 1, me == mid)
        self.not_hub = jnp.logical_not(self.is_hub)
        self.mine = lax.axis_index("scany")

    def at(self, c):
        return pl.ds(c * self.rows, self.rows)

    def copy(self, src, dst, s, r, c, where):
        return remote(src.at[self.at(c)], dst.at[self.at(c)], self.send.at[s, c], self.recv.at[r, c], where)

    def pair(self, c):
        return self.copy(self.prob.at[1 - self.q], self.ppair, 0, 0, c, self.partner)

    def inward(self, c):
        return self.copy(self.part, self.inner, 1, 1, c, self.to_inner)

    def across(self, c):
        return self.copy(self.part, self.hub, 1, 2, c, self.to_inner)

    def outward(self, c, src):
        return self.copy(src, self.hub, 2, 2, c, self.to_outer)

    def share(self, c, q):
        return self.copy(self.total.at[q], self.total.at[q], 3, 3, c, self.partner)

    def sides(self, c):
        out = []
        for d in range(1, self.ny):
            slot = self.held.at[self.mine]
            out.append(self.copy(slot, slot, 3 + d, 3 + d, c, {"scany": lax.rem(self.mine + d, self.ny)}))
        return out

    def side_arrive(self, c):
        for d in range(1, self.ny):
            slot = self.held.at[lax.rem(self.mine - d + self.ny, self.ny)]
            self.copy(slot, slot, 3 + d, 3 + d, c, self.partner).wait_recv()

    def side_sum(self, c):
        self.side_arrive(c)
        out = self.held[0, self.at(c)]
        for i in range(1, self.ny):
            out = out + self.held[i, self.at(c)]
        return out

    def pair_sum(self, c):
        self.pair(c).wait_recv()
        return self.prob[self.q, self.at(c)] + self.ppair[self.at(c)]

    def send_sides(self, c, value):
        self.held[self.mine, self.at(c)] = value
        for copy in self.sides(c):
            copy.start()

    def send_inward(self, c):
        when(self.not_hub)(self.inward(c).start)
        when(self.is_hub)(self.across(c).start)

    def collect(self):
        @pl.when(self.has_outer)
        def _():
            for c in range(self.chunks):
                self.inward(c).wait_recv()
                self.part[self.at(c)] = self.part[self.at(c)] + self.inner[self.at(c)]
                self.send_inward(c)

    def start_part(self, c, value):
        self.part[self.at(c)] = value
        when(self.no_outer)(functools.partial(self.send_inward, c))

    def from_hub(self, hubs, after, chunks=None):
        @pl.when(self.is_hub if hubs else self.not_hub)
        def _():
            for c in chunks or range(self.chunks):
                self.across(c).wait_recv()
                value = self.hub[self.at(c)]
                after(c, self.part[self.at(c)] + value if hubs else value)

    def finish(self, src):
        for c in range(self.chunks):
            self.pair(c).wait_send()
            self.inward(c).wait_send()
            when(self.has_outer)(self.outward(c, src).wait_send)
            self.share(c, self.q).wait_send()
            for copy in self.sides(c):
                copy.wait_send()


class SideFirst(ProbeSum):
    def one(self):
        for c in range(self.chunks):
            self.send_sides(c, self.pair_sum(c))

    def two(self):
        for c in range(self.chunks):
            self.start_part(c, self.side_sum(c))
        self.collect()

    def done(self, c, value):
        self.total[self.q, self.at(c)] = value
        when(self.has_outer)(self.outward(c, self.total.at[self.q]).start)
        self.share(c, self.q).start()

    def three(self, chunks=None):
        self.from_hub(True, self.done, chunks)

    def four(self):
        self.from_hub(False, self.done)

    def five(self):
        pass

    def end(self):
        self.finish(self.total.at[self.q])


class ChainFirst(ProbeSum):
    def one(self):
        for c in range(self.chunks):
            self.start_part(c, self.pair_sum(c))

    def two(self):
        self.collect()

    def done(self, c, value):
        self.send_sides(c, value)
        when(self.has_outer)(self.outward(c, self.held.at[self.mine]).start)

    def three(self, chunks=None):
        self.from_hub(True, self.done, chunks)

    def four(self):
        self.from_hub(False, self.done)

    def five(self):
        for c in range(self.chunks):
            self.total[self.q, self.at(c)] = self.side_sum(c)
            self.share(c, self.q).start()

    def end(self):
        self.finish(self.held.at[self.mine])


def near_greet(ny, partner, sides):
    my = lax.axis_index("scany")
    greet(
        [(True, partner)]
        + [(True, {"scany": lax.rem(my + d, ny)}) for d in range(1, ny)]
        + [(side.has, side.where) for side in sides]
    )


def each(step):
    p = lax.axis_index("pos")
    for q in range(2):
        pl.when(p == q)(functools.partial(step, q))


class Placer:
    def __init__(self, offsets, bufs, m, positions):
        self.bufs, self.m = bufs, m
        self.tall, self.span = m + 8, m + 128
        self.top = (bufs.shape[2] - self.tall // 8) // 2
        self.spots = []
        for j in range(positions):
            row, col = offsets[j, 0], offsets[j, 1]
            self.spots.append((lax.rem(row, 8), lax.rem(col, 128), lax.div(row, 8), lax.div(col, 128)))

    def clear(self):
        n, k, rows = self.bufs.shape[:3]
        bottom = self.top + self.tall // 8
        for j in range(n):
            for c in range(k):
                self.bufs[j, c, 0 : self.top] = jnp.zeros((self.top, *self.bufs.shape[3:]), jnp.float32)
                self.bufs[j, c, bottom:rows] = jnp.zeros((rows - bottom, *self.bufs.shape[3:]), jnp.float32)

    def put(self, j, k, term):
        row_in, col_in, _, step = self.spots[j]
        m, wide = self.m, self.bufs.shape[4]
        blank_rows = jnp.zeros((self.tall - m, m), jnp.float32)
        blank_cols = jnp.zeros((self.tall, self.span - m), jnp.float32)
        moved = pltpu.roll(jnp.concatenate([term, blank_rows], 0), row_in, 0)
        moved = pltpu.roll(jnp.concatenate([moved, blank_cols], 1), col_in, 1)
        out = None
        for d in range((wide - self.span) // 128 + 1):
            parts = [jnp.zeros((self.tall, w), jnp.float32) for w in (128 * d, wide - self.span - 128 * d)]
            here = jnp.concatenate([x for x in (parts[0], moved, parts[1]) if x.shape[1]], 1)
            out = here if out is None else jnp.where(step == d, here, out)
        self.bufs[j, k, self.top : self.top + self.tall // 8] = out.reshape(self.tall // 8, 8, wide)

    def rows(self, k, r0, count):
        out = None
        for j, (_, _, row, _) in enumerate(self.spots):
            part = self.bufs[j, k, pl.ds(self.top - row + r0 // 8, count // 8)]
            out = part if out is None else out + part
        return out.reshape(count, self.bufs.shape[4])

    def window(self, j, pad, k):
        row_in, col_in, row, step = self.spots[j]
        wide = pad.shape[3]
        block = pad[k, pl.ds(row, self.tall // 8)].reshape(self.tall, wide)
        out = block[:, : self.span]
        for d in range(1, (wide - self.span) // 128 + 1):
            out = jnp.where(step == d, block[:, 128 * d : 128 * d + self.span], out)
        out = pltpu.roll(out, lax.rem(self.span - col_in, self.span), 1)[:, : self.m]
        return pltpu.roll(out, lax.rem(self.tall - row_in, self.tall), 0)[: self.m]


def forward(window, pr, pi, table_a, table_b):
    m = pr.shape[0]
    bf = jnp.bfloat16
    ar, ai = window
    er = pr * ar - pi * ai
    ei = pr * ai + pi * ar
    left = dot(table_a[...], jnp.concatenate([er.astype(bf), ei.astype(bf)], 0)).astype(bf)
    return er, ei, dot(jnp.concatenate([left[:m], left[m:]], 1), table_b[...])


def backward(er, ei, far, amplitude, table_a, table_b):
    m = er.shape[0]
    bf = jnp.bfloat16
    fr, fi = far[:, :m], far[:, m:]
    ratio = amplitude.astype(jnp.float32) / jnp.maximum(jnp.sqrt(fr * fr + fi * fi), 0.2)
    projected = jnp.concatenate([(fr * ratio).astype(bf), (fi * ratio).astype(bf)], 0)
    back_half = dot(table_b[...], projected).astype(bf)
    back = dot(jnp.concatenate([back_half[:m], back_half[m:]], 1), table_a[...])
    return back[:, :m] - er, back[:, m:] - ei


def whole_kernel(nx, ny, step_size, *refs):
    offsets, spec, *given = refs[:6]
    new_spec, new_probe = refs[6:8]
    pad, probe, amplitudes, table_a, table_b, bufs, grad, prob, total, light_all = refs[8:18]
    pair, acc, xr1, xr2, zr1, zr2, ipair, iacc, ixr, izr, ppair, held, inner, hub, part = refs[18:33]
    hsend, hrecv, local, gsend, grecv, isend, irecv, psend, precv = refs[33:]
    tile, m = spec.shape[3], probe.shape[1]
    wide = pad.shape[3]
    half = (wide - tile) // 2
    h = grad.shape[3]
    positions, chunks = amplitudes.shape[0], psend.shape[1]
    p = lax.axis_index("pos")
    partner = {"pos": 1 - p}
    loads = [pltpu.make_async_copy(spec, pad.at[:, pl.ds(half // 8, tile // 8), :, pl.ds(half, tile)], local.at[0])]
    for i, (src, dst) in enumerate(zip(given, (probe, amplitudes, table_a, table_b)), 1):
        loads.append(pltpu.make_async_copy(src, dst, local.at[i]))
    for c in loads:
        c.start()
    roles = [Role(q, nx, ny) for q in range(2)]
    sides = roles[1].sides1 + roles[0].sides1
    near_greet(ny, partner, roles[1].sides1)
    halos = [Halo(r, spec, pad, hsend, hrecv, partner) for r in roles]
    folds = [
        Fold(
            roles[q],
            roles[1 - q],
            grad.at[q],
            grad.at[1 - q],
            pair,
            acc,
            (zr1, xr1, zr2, xr2),
            None,
            gsend,
            grecv,
            partner,
        )
        for q in range(2)
    ]
    role = Role(p, nx, ny, 0)
    light = Fold(
        role,
        role,
        grad.at[2, :, pl.ds(p, 1)],
        grad.at[2, :, pl.ds(1 - p, 1)],
        ipair,
        iacc,
        (None, ixr, izr, None),
        light_all,
        isend,
        irecv,
        partner,
    )
    probes = [
        kind(q, nx, ny, prob, ppair, held, inner, hub, part, total, psend, precv, partner)
        for q, kind in enumerate((SideFirst, ChainFirst))
    ]
    placer = Placer(offsets, bufs, m, positions)

    def gather(k):
        for g in range(4):
            for b in range(2):
                grad[k, g, b] = placer.rows(k, (2 * g + b) * h, h)

    each(lambda q: halos[q].begin())
    for i, at in enumerate(
        (
            (slice(None), pl.ds(0, half // 8)),
            (slice(None), pl.ds((half + tile) // 8, half // 8)),
            (slice(None), slice(None), slice(None), pl.ds(0, half)),
            (slice(None), slice(None), slice(None), pl.ds(half + tile, half)),
        )
    ):

        @pl.when(jnp.logical_not(sides[i].has))
        def _(at=at):
            pad[at] = jnp.zeros(pad.at[at].shape, pad.dtype)

    placer.clear()
    loads[1].wait()
    power = probe[0] * probe[0] + probe[1] * probe[1]
    for j in range(positions):
        placer.put(j, 2, power)
    gather(2)
    light.begin()

    def strips(q):
        halos[q].relay()

    def corners(q):
        halos[q].relay_corners()
        halos[1 - q].arrive()

    each(strips)
    for i in range(3):
        light.add(i)
    light.send_rims(0)
    each(corners)
    for c in loads[:1] + loads[2:]:
        c.wait()
    pr, pi = probe[0], probe[1]
    windows = [[placer.window(j, pad, k) for k in range(2)] for j in range(positions)]
    fields = [forward(windows[j], pr, pi, table_a, table_b) for j in range(positions)]
    light.fold(0)
    light.send_rims(1)
    diffs = [backward(*fields[j], amplitudes[j], table_a, table_b) for j in range(positions)]
    sums = [None, None]
    for (ar, ai), (dr, di) in zip(windows, diffs):
        for k, t in enumerate((ar * dr + ai * di, ar * di - ai * dr)):
            sums[k] = t if sums[k] is None else sums[k] + t
    rows = m // chunks
    for c in range(chunks):
        at = pl.ds(c * rows, rows)
        for k in range(2):
            prob[k, at] = sums[k][c * rows : (c + 1) * rows]
        remote(prob.at[1 - p, at], ppair.at[at], psend.at[0, c], precv.at[0, c], partner).start()
    for j, (dr, di) in enumerate(diffs):
        placer.put(j, 0, pr * dr + pi * di)
        placer.put(j, 1, pr * di - pi * dr)
    gather(1 - p)
    each(lambda q: folds[q].begin())
    gather(p)

    def update(q):
        q4 = folds[q].q4
        for g in range(2):
            for b in range(2):
                r0 = (2 * g + b) * h
                old = pad[q, (half + r0) // 8 : (half + r0 + h) // 8, :, half : half + tile].reshape(h, tile)
                new_spec[q, r0 : r0 + h] = old + acc[1 + g, b, :, q4 : 3 * q4] / (light_all[b, g, 0] + 1.0)

    def share_copy(q):
        return remote(new_spec.at[q], new_spec.at[q], gsend.at[7], grecv.at[7], partner)

    def object_last(q):
        light.arrive()
        folds[q].fold(1)
        update(q)
        share_copy(q).start()

    def objects(q):
        probe_sum, fold = probes[q], folds[q]
        probe_sum.one()
        fold.add(0)
        fold.add(1)
        fold.send_rims(0)
        fold.add(2)
        light.fold(1)
        light.share()
        probe_sum.two()
        if q == 0:
            fold.fold(0)
            fold.send_rims(1)
            probe_sum.three()
            object_last(q)
            probe_sum.four()
        else:
            probe_sum.three()
            fold.fold(0)
            fold.send_rims(1)
            probe_sum.four()
            object_last(q)
            probe_sum.five()

    each(objects)

    def closing(q):
        for c in range(chunks):
            probes[q].share(c, 1 - q).wait_recv()
        share_copy(1 - q).wait_recv()
        share_copy(q).wait_send()
        light.finish()
        folds[q].finish()
        probes[q].end()
        halos[q].finish()

    each(closing)
    for k in range(2):
        new_probe[k] = probe[k] + total[k] * step_size


def emit_kernel(spec, probe, new_spec, new_probe, sem):
    copies = [
        pltpu.make_async_copy(src.at[k], dst.at[k], sem.at[i, k])
        for i, (src, dst) in enumerate(((spec, new_spec), (probe, new_probe)))
        for k in range(2)
    ]
    for c in copies:
        c.start()
    for c in copies:
        c.wait()


def tables(length):
    index = np.arange(length)
    angle = ((index[:, None] * index[None, :]) % length).astype(np.float32) * np.float32(2.0 * math.pi / length)
    scale = np.float32(1.0 / math.sqrt(length))
    c = np.cos(angle) * scale
    s = np.sin(angle) * scale
    a = np.block([[c, s], [-s, c]]).astype(jnp.bfloat16)
    b = np.block([[c, -s], [s, c]]).astype(jnp.bfloat16)
    return a, b


def shards(nx, ny, consts, specimen, probe_wave, amplitudes, offsets):
    m = probe_wave.shape[1]
    tile = specimen.shape[1]
    wide = tile + m
    f32 = jnp.float32
    vm = pl.BlockSpec(memory_space=VMEM)
    sm = pl.BlockSpec(memory_space=pltpu.SMEM)
    hbm = pl.BlockSpec(memory_space=pltpu.HBM)
    dma = pltpu.SemaphoreType.DMA
    n = nx * ny
    h = wide // 8
    chunks = 4
    positions = offsets.shape[0]
    held = (probe_wave, amplitudes, consts[0], consts[1])

    step_size = 1.0 / math.sqrt(positions * n * 2)
    results = pl.pallas_call(
        functools.partial(whole_kernel, nx, ny, step_size),
        out_shape=[VMEM(specimen.shape, f32), VMEM(probe_wave.shape, f32)],
        in_specs=[sm] + [hbm] * 5,
        out_specs=[vm, vm],
        scratch_shapes=[
            VMEM((2, wide // 8, 8, wide), f32),
            *[VMEM(x.shape, x.dtype) for x in held],
            VMEM((positions, 3, (2 * (tile - 8) + m + 8) // 8, 8, wide), f32),
            VMEM((3, 4, 2, h, wide), f32),
            VMEM((2, m, m), f32),
            VMEM((2, m, m), f32),
            VMEM((2, 2, 1, h, wide // 2), f32),
            VMEM((4, 2, h, wide), f32),
            VMEM((4, 2, h, wide), f32),
            VMEM((2, 4, 2, h, wide // 4), f32),
            VMEM((2, 2, 2, h, wide // 4), f32),
            VMEM((2, 2, h, wide), f32),
            VMEM((2, 2, h, wide // 2), f32),
            VMEM((4, 1, h, wide), f32),
            VMEM((4, 1, h, wide), f32),
            VMEM((2, 4, 1, h, wide // 4), f32),
            VMEM((2, 1, h, wide // 2), f32),
            VMEM((m, m), f32),
            VMEM((ny, m, m), f32),
            VMEM((m, m), f32),
            VMEM((m, m), f32),
            VMEM((m, m), f32),
            dma((20,)),
            dma((20,)),
            dma((5,)),
            dma((8,)),
            dma((8,)),
            dma((8,)),
            dma((8,)),
            dma((3 + ny, chunks)),
            dma((3 + ny, chunks)),
        ],
        compiler_params=pltpu.CompilerParams(vmem_limit_bytes=56 * 2**20, collective_id=0, has_side_effects=True),
        name="whole",
    )(offsets, *[pltpu.with_memory_space_constraint(x, pltpu.HBM) for x in (specimen.reshape(2, tile // 8, 8, tile), *held)])
    return pl.pallas_call(
        emit_kernel,
        out_shape=[jax.ShapeDtypeStruct(specimen.shape, f32), jax.ShapeDtypeStruct(probe_wave.shape, f32)],
        in_specs=[vm] * 2,
        out_specs=[pl.BlockSpec(memory_space=pl.ANY)] * 2,
        scratch_shapes=[dma((2, 2))],
        compiler_params=pltpu.CompilerParams(vmem_limit_bytes=2 * 2**20),
        name="emit",
    )(*results)


def solution(mesh):
    nx, ny = mesh.shape["scanx"], mesh.shape["scany"]

    def run(specimen, probe_wave, amplitudes, offsets):
        consts = tables(probe_wave.shape[2])
        return jax.shard_map(
            lambda *args: shards(nx, ny, [jnp.asarray(t) for t in consts], *args),
            mesh=mesh,
            in_specs=(
                P(None, ("groups", "scanx"), "scany"),
                P(None, "groups", None),
                P(("groups", "scanx", "scany", "pos"), None, None),
                P(("groups", "scanx", "scany", "pos"), None),
            ),
            out_specs=(P(None, ("groups", "scanx"), "scany"), P(None, "groups", None)),
            check_vma=False,
        )(specimen, probe_wave, amplitudes, offsets)

    return run
```

```python
import functools
import math

import jax
import jax.numpy as jnp
import numpy as np
from jax import lax
from jax.experimental import pallas as pl
from jax.experimental.pallas import tpu as pltpu
from jax.sharding import PartitionSpec as P

MESH = pl.DeviceIdType.MESH
VMEM = pltpu.VMEM


def remote(src, dst, send, recv, where):
    return pltpu.make_async_remote_copy(
        src_ref=src, dst_ref=dst, send_sem=send, recv_sem=recv, device_id=where, device_id_type=MESH
    )


def greet(conditions_devices):
    barrier = pltpu.get_barrier_semaphore()
    for present, where in conditions_devices:
        if present is True:
            pl.semaphore_signal(barrier, inc=1, device_id=where, device_id_type=MESH)
        else:

            @pl.when(present)
            def _(where=where):
                pl.semaphore_signal(barrier, inc=1, device_id=where, device_id_type=MESH)

    fixed = sum(1 for present, _ in conditions_devices if present is True)
    peers = [present.astype(jnp.int32) for present, _ in conditions_devices if present is not True]
    pl.semaphore_wait(barrier, sum(peers, fixed))


class Side:
    def __init__(self, axis, count, step):
        me = lax.axis_index(axis)
        self.has = me > 0 if step < 0 else me < count - 1
        self.where = {axis: me + step}


class Role:
    def __init__(self, q, nx, ny, order=None):
        order = q if order is None else order
        along_x = ("scanx", nx, Side("scanx", nx, -1), Side("scanx", nx, 1))
        along_y = ("scany", ny, Side("scany", ny, -1), Side("scany", ny, 1))
        one, two = (along_y, along_x) if order == 0 else (along_x, along_y)
        self.q, self.o, self.rows_first = q, 1 - q, order == 1
        self.axis1, self.n1, self.sides1 = one[0], one[1], one[2:]
        self.axis2, self.n2, self.sides2 = two[0], two[1], two[2:]
        self.me1, self.me2 = lax.axis_index(self.axis1), lax.axis_index(self.axis2)


def when(*conditions):
    return pl.when(functools.reduce(jnp.logical_and, [c for c in conditions if c is not True]))


def dot(a, b):
    return jnp.dot(a, b, preferred_element_type=jnp.float32)


class Halo:
    def __init__(self, role, spec, pad, send, recv, partner):
        self.r, self.spec, self.pad, self.partner = role, spec, pad, partner
        self.send, self.recv = send, recv
        self.direct = not role.rows_first
        tile = spec.shape[3]
        half = (pad.shape[3] - tile) // 2
        self.own = (half, tile)
        self.margins = ((0, half), (half + tile, half))
        self.edges = ((0, half), (tile - half, half))
        self.pad_edges = ((half, half), (tile, half))
        self.whole = (0, tile)

    def at(self, one, two):
        rows, cols = (one, two) if self.r.rows_first else (two, one)
        return (self.r.q, pl.ds(rows[0] // 8, rows[1] // 8), slice(None), pl.ds(*cols))

    def copy(self, src, dst, i, where):
        return remote(src, dst, self.send.at[i], self.recv.at[i], where)

    def strip1(self, m, e):
        return self.copy(
            self.spec.at[self.at(self.edges[1 - m], self.edges[e])],
            self.pad.at[self.at(self.margins[m], self.pad_edges[e])],
            2 * m + e,
            self.r.sides1[1 - m].where,
        )

    def strip2(self, m):
        return self.copy(
            self.spec.at[self.at(self.whole, self.edges[1 - m])],
            self.pad.at[self.at(self.own, self.margins[m])],
            4 + m,
            self.r.sides2[1 - m].where,
        )

    def corner(self, m1, m2):
        if self.direct:
            return self.copy(
                self.spec.at[self.at(self.edges[1 - m1], self.edges[1 - m2])],
                self.pad.at[self.at(self.margins[m1], self.margins[m2])],
                6 + 2 * m1 + m2,
                {**self.r.sides1[1 - m1].where, **self.r.sides2[1 - m2].where},
            )
        return self.copy(
            self.pad.at[self.at(self.margins[m1], self.pad_edges[1 - m2])],
            self.pad.at[self.at(self.margins[m1], self.margins[m2])],
            6 + 2 * m1 + m2,
            self.r.sides2[1 - m2].where,
        )

    def share(self, i, one, two):
        ref = self.pad.at[self.at(one, two)]
        return self.copy(ref, ref, 10 + i, self.partner)

    def share1(self, m, e):
        return self.share(2 * m + e, self.margins[m], self.pad_edges[e])

    def share2(self, m):
        return self.share(4 + m, self.own, self.margins[m])

    def share_corner(self, m1, m2):
        return self.share(6 + 2 * m1 + m2, self.margins[m1], self.margins[m2])

    def begin(self):
        r = self.r
        if self.direct:
            for m1 in range(2):
                for m2 in range(2):
                    when(r.sides1[1 - m1].has, r.sides2[1 - m2].has)(self.corner(m1, m2).start)
        for m in range(2):
            for e in range(2):
                when(r.sides1[1 - m].has, r.sides2[e].has)(self.strip1(m, e).start)
        for m in range(2):
            when(r.sides2[1 - m].has)(self.strip2(m).start)
        for m in range(2):
            for e in range(2):
                when(r.sides1[1 - m].has, jnp.logical_not(r.sides2[e].has))(self.strip1(m, e).start)

    def relay(self):
        r = self.r
        for m1 in range(2):
            for e in range(2):

                @when(r.sides1[m1].has, r.sides2[e].has)
                def _():
                    self.strip1(m1, e).wait_recv()
                    if not self.direct:
                        self.corner(m1, 1 - e).start()
                    self.share1(m1, e).start()

        for m in range(2):

            @when(r.sides2[m].has)
            def _():
                self.strip2(m).wait_recv()
                self.share2(m).start()

        for m1 in range(2):
            for e in range(2):

                @when(r.sides1[m1].has, jnp.logical_not(r.sides2[e].has))
                def _():
                    self.strip1(m1, e).wait_recv()
                    self.share1(m1, e).start()

    def relay_corners(self):
        r = self.r
        for m1 in range(2):
            for m2 in range(2):

                @when(r.sides1[m1].has, r.sides2[m2].has)
                def _():
                    self.corner(m1, m2).wait_recv()
                    self.share_corner(m1, m2).start()

    def arrive(self):
        r = self.r
        for m in range(2):
            for e in range(2):
                when(r.sides1[m].has)(self.share1(m, e).wait_recv)
            when(r.sides2[m].has)(self.share2(m).wait_recv)
        for m1 in range(2):
            for m2 in range(2):
                when(r.sides1[m1].has, r.sides2[m2].has)(self.share_corner(m1, m2).wait_recv)

    def finish(self):
        r = self.r
        for m in range(2):
            for e in range(2):
                when(r.sides1[1 - m].has)(self.strip1(m, e).wait_send)
                when(r.sides1[m].has)(self.share1(m, e).wait_send)
            when(r.sides2[1 - m].has)(self.strip2(m).wait_send)
            when(r.sides2[m].has)(self.share2(m).wait_send)
        for m1 in range(2):
            for m2 in range(2):
                sent = r.sides1[1 - m1].has if self.direct else r.sides1[m1].has
                when(sent, r.sides2[1 - m2].has)(self.corner(m1, m2).wait_send)
                when(r.sides1[m1].has, r.sides2[m2].has)(self.share_corner(m1, m2).wait_send)


class Fold:
    def __init__(self, role, other, mine, theirs, pair, acc, rims, core, send, recv, partner):
        self.r, self.other, self.mine, self.theirs, self.pair, self.acc = role, other, mine, theirs, pair, acc
        self.rows1, self.cols1, self.rows2, self.cols2 = rims
        self.core, self.send, self.recv, self.partner = core, send, recv, partner
        w = acc.shape[-1]
        self.w, self.q4 = w, w // 4

    def piece(self, i, r):
        q4, cols = self.q4, (slice(None),) * 3
        if r.rows_first:
            return ((pl.ds(0, 1),), (pl.ds(3, 1),), (pl.ds(1, 2),))[i]
        return cols + ((pl.ds(0, q4),), (pl.ds(3 * q4, q4),), (pl.ds(q4, 2 * q4),))[i]

    def needed(self, i, r):
        return pl.when(r.sides1[i].has) if i < 2 else lambda f: f()

    def pair_copy(self, i, r):
        at = self.piece(i, r)
        return remote(self.theirs.at[at], self.pair.at[at], self.send.at[i], self.recv.at[i], self.partner)

    def begin(self):
        for i in range(3):
            self.needed(i, self.other)(self.pair_copy(i, self.other).start)

    def add(self, i):
        @self.needed(i, self.r)
        def _():
            self.pair_copy(i, self.r).wait_recv()
            at = self.piece(i, self.r)
            self.acc[at] = self.mine[at] + self.pair[at]

    def spot(self, stage, i, m):
        r, q4, w = self.r, self.q4, self.w
        if r.rows_first == (stage == 0):
            if stage == 1:
                return (i, slice(None), slice(None), pl.ds(q4, 2 * q4)), self.rows2.at[m]
            cols = pl.ds(0, w)
            if r.n2 == 2:
                cols = pl.ds(pl.multiple_of((1 - r.me2) * q4, q4), 3 * q4)
            return (i, slice(None), slice(None), cols), self.rows1.at[m, :, :, cols]
        groups = pl.ds(0, 4) if stage == 0 else pl.ds(1, 2)
        return (groups, slice(None), slice(None), pl.ds(i * q4, q4)), (self.cols1 if stage == 0 else self.cols2).at[m]

    def rim_copy(self, stage, m):
        sides = self.r.sides1 if stage == 0 else self.r.sides2
        at, rim = self.spot(stage, 3 * (1 - m), m)
        i = 3 + 2 * stage + m
        return remote(self.acc.at[at], rim, self.send.at[i], self.recv.at[i], sides[1 - m].where)

    def send_rims(self, stage, only=lambda k: True):
        sides = self.r.sides1 if stage == 0 else self.r.sides2
        for m in range(2):
            when(sides[1 - m].has, only(1 - m))(self.rim_copy(stage, m).start)

    def fold(self, stage, only=lambda k: True):
        sides = self.r.sides1 if stage == 0 else self.r.sides2
        for m in range(2):

            @when(sides[m].has, only(m))
            def _():
                self.rim_copy(stage, m).wait_recv()
                at, rim = self.spot(stage, 1 + m, m)
                self.acc[at] = self.acc[at] + rim[...]

    def share_copy(self, q):
        return remote(self.core.at[q], self.core.at[q], self.send.at[7], self.recv.at[7], self.partner)

    def share(self):
        q4 = self.q4
        self.core[self.r.q] = self.acc[1:3, :, :, q4 : 3 * q4]
        self.share_copy(self.r.q).start()

    def arrive(self):
        self.share_copy(self.r.o).wait_recv()

    def finish(self):
        r = self.r
        for i in range(3):
            self.needed(i, self.other)(self.pair_copy(i, self.other).wait_send)
        for m in range(2):
            when(r.sides1[1 - m].has)(self.rim_copy(0, m).wait_send)
            when(r.sides2[1 - m].has)(self.rim_copy(1, m).wait_send)
        if self.core is not None:
            self.share_copy(r.q).wait_send()


class ProbeSum:
    def __init__(self, q, nx, ny, prob, ppair, held, inner, hub, part, total, send, recv, partner):
        self.q, self.ny = q, ny
        self.prob, self.ppair, self.held = prob, ppair, held
        self.inner, self.hub, self.part, self.total = inner, hub, part, total
        self.send, self.recv, self.partner = send, recv, partner
        self.chunks = send.shape[1]
        self.rows = prob.shape[1] // self.chunks
        me, mid = lax.axis_index("scanx"), nx // 2
        self.lower, self.upper = me < mid, me >= mid
        step = 2 * self.lower.astype(jnp.int32) - 1
        self.to_inner, self.to_outer = {"scanx": me + step}, {"scanx": me - step}
        self.has_outer = jnp.logical_and(me > 0, me < nx - 1)
        self.no_outer = jnp.logical_not(self.has_outer)
        self.is_hub = jnp.logical_or(me == mid - 1, me == mid)
        self.not_hub = jnp.logical_not(self.is_hub)
        self.mine = lax.axis_index("scany")

    def parts(self):
        inner = (self.upper, self.lower)
        return (
            lambda k: inner[k],
            lambda k: inner[1 - k],
            lambda k: jnp.logical_and(inner[k], self.not_hub),
            lambda k: jnp.logical_or(inner[1 - k], self.is_hub),
        )

    def at(self, c):
        return pl.ds(c * self.rows, self.rows)

    def copy(self, src, dst, s, r, c, where):
        return remote(src.at[self.at(c)], dst.at[self.at(c)], self.send.at[s, c], self.recv.at[r, c], where)

    def pair(self, c):
        return self.copy(self.prob.at[1 - self.q], self.ppair, 0, 0, c, self.partner)

    def inward(self, c):
        return self.copy(self.part, self.inner, 1, 1, c, self.to_inner)

    def across(self, c):
        return self.copy(self.part, self.hub, 1, 2, c, self.to_inner)

    def outward(self, c, src):
        return self.copy(src, self.hub, 2, 2, c, self.to_outer)

    def share(self, c, q):
        return self.copy(self.total.at[q], self.total.at[q], 3, 3, c, self.partner)

    def sides(self, c):
        out = []
        for d in range(1, self.ny):
            slot = self.held.at[self.mine]
            out.append(self.copy(slot, slot, 3 + d, 3 + d, c, {"scany": lax.rem(self.mine + d, self.ny)}))
        return out

    def side_arrive(self, c):
        for d in range(1, self.ny):
            slot = self.held.at[lax.rem(self.mine - d + self.ny, self.ny)]
            self.copy(slot, slot, 3 + d, 3 + d, c, self.partner).wait_recv()

    def side_sum(self, c):
        self.side_arrive(c)
        out = self.held[0, self.at(c)]
        for i in range(1, self.ny):
            out = out + self.held[i, self.at(c)]
        return out

    def pair_sum(self, c):
        self.pair(c).wait_recv()
        return self.prob[self.q, self.at(c)] + self.ppair[self.at(c)]

    def send_sides(self, c, value):
        self.held[self.mine, self.at(c)] = value
        for copy in self.sides(c):
            copy.start()

    def send_inward(self, c):
        when(self.not_hub)(self.inward(c).start)
        when(self.is_hub)(self.across(c).start)

    def collect(self):
        @pl.when(self.has_outer)
        def _():
            for c in range(self.chunks):
                self.inward(c).wait_recv()
                self.part[self.at(c)] = self.part[self.at(c)] + self.inner[self.at(c)]
                self.send_inward(c)

    def start_part(self, c, value):
        self.part[self.at(c)] = value
        when(self.no_outer)(functools.partial(self.send_inward, c))

    def from_hub(self, hubs, after, chunks=None):
        @pl.when(self.is_hub if hubs else self.not_hub)
        def _():
            for c in chunks or range(self.chunks):
                self.across(c).wait_recv()
                value = self.hub[self.at(c)]
                after(c, self.part[self.at(c)] + value if hubs else value)

    def finish(self, src):
        for c in range(self.chunks):
            self.pair(c).wait_send()
            self.inward(c).wait_send()
            when(self.has_outer)(self.outward(c, src).wait_send)
            self.share(c, self.q).wait_send()
            for copy in self.sides(c):
                copy.wait_send()


class SideFirst(ProbeSum):
    def one(self):
        for c in range(self.chunks):
            self.send_sides(c, self.pair_sum(c))

    def two(self):
        for c in range(self.chunks):
            self.start_part(c, self.side_sum(c))
        self.collect()

    def done(self, c, value):
        self.total[self.q, self.at(c)] = value
        when(self.has_outer)(self.outward(c, self.total.at[self.q]).start)
        self.share(c, self.q).start()

    def three(self, chunks=None):
        self.from_hub(True, self.done, chunks)

    def four(self):
        self.from_hub(False, self.done)

    def five(self):
        pass

    def end(self):
        self.finish(self.total.at[self.q])


class ChainFirst(ProbeSum):
    def one(self):
        for c in range(self.chunks):
            self.start_part(c, self.pair_sum(c))

    def two(self):
        self.collect()

    def done(self, c, value):
        self.send_sides(c, value)
        when(self.has_outer)(self.outward(c, self.held.at[self.mine]).start)

    def three(self, chunks=None):
        self.from_hub(True, self.done, chunks)

    def four(self):
        self.from_hub(False, self.done)

    def five(self):
        for c in range(self.chunks):
            self.total[self.q, self.at(c)] = self.side_sum(c)
            self.share(c, self.q).start()

    def end(self):
        self.finish(self.held.at[self.mine])


def near_greet(ny, partner, rows, cols):
    my = lax.axis_index("scany")
    greet(
        [(True, partner)]
        + [(True, {"scany": lax.rem(my + d, ny)}) for d in range(1, ny)]
        + [(side.has, side.where) for side in rows]
        + [(jnp.logical_and(a.has, b.has), {**a.where, **b.where}) for a in rows for b in cols]
    )


def each(step):
    p = lax.axis_index("pos")
    for q in range(2):
        pl.when(p == q)(functools.partial(step, q))


class Placer:
    def __init__(self, offsets, bufs, m, positions):
        self.bufs, self.m = bufs, m
        self.tall, self.span = m + 8, m + 128
        self.top = (bufs.shape[2] - self.tall // 8) // 2
        self.spots = []
        for j in range(positions):
            row, col = offsets[j, 0], offsets[j, 1]
            self.spots.append((lax.rem(row, 8), lax.rem(col, 128), lax.div(row, 8), lax.div(col, 128)))

    def clear(self):
        n, k, rows = self.bufs.shape[:3]
        bottom = self.top + self.tall // 8
        for j in range(n):
            for c in range(k):
                self.bufs[j, c, 0 : self.top] = jnp.zeros((self.top, *self.bufs.shape[3:]), jnp.float32)
                self.bufs[j, c, bottom:rows] = jnp.zeros((rows - bottom, *self.bufs.shape[3:]), jnp.float32)

    def put(self, j, k, term):
        row_in, col_in, _, step = self.spots[j]
        m, wide = self.m, self.bufs.shape[4]
        blank_rows = jnp.zeros((self.tall - m, m), jnp.float32)
        blank_cols = jnp.zeros((self.tall, self.span - m), jnp.float32)
        moved = pltpu.roll(jnp.concatenate([term, blank_rows], 0), row_in, 0)
        moved = pltpu.roll(jnp.concatenate([moved, blank_cols], 1), col_in, 1)
        out = None
        for d in range((wide - self.span) // 128 + 1):
            parts = [jnp.zeros((self.tall, w), jnp.float32) for w in (128 * d, wide - self.span - 128 * d)]
            here = jnp.concatenate([x for x in (parts[0], moved, parts[1]) if x.shape[1]], 1)
            out = here if out is None else jnp.where(step == d, here, out)
        self.bufs[j, k, self.top : self.top + self.tall // 8] = out.reshape(self.tall // 8, 8, wide)

    def rows(self, k, r0, count):
        out = None
        for j, (_, _, row, _) in enumerate(self.spots):
            part = self.bufs[j, k, pl.ds(self.top - row + r0 // 8, count // 8)]
            out = part if out is None else out + part
        return out.reshape(count, self.bufs.shape[4])

    def window(self, j, pad, k):
        row_in, col_in, row, step = self.spots[j]
        wide = pad.shape[3]
        block = pad[k, pl.ds(row, self.tall // 8)].reshape(self.tall, wide)
        out = block[:, : self.span]
        for d in range(1, (wide - self.span) // 128 + 1):
            out = jnp.where(step == d, block[:, 128 * d : 128 * d + self.span], out)
        out = pltpu.roll(out, lax.rem(self.span - col_in, self.span), 1)[:, : self.m]
        return pltpu.roll(out, lax.rem(self.tall - row_in, self.tall), 0)[: self.m]


def forward(window, pr, pi, table_a, table_b):
    m = pr.shape[0]
    bf = jnp.bfloat16
    ar, ai = window
    er = pr * ar - pi * ai
    ei = pr * ai + pi * ar
    left = dot(table_a[...], jnp.concatenate([er.astype(bf), ei.astype(bf)], 0)).astype(bf)
    return er, ei, dot(jnp.concatenate([left[:m], left[m:]], 1), table_b[...])


def backward(er, ei, far, amplitude, table_a, table_b):
    m = er.shape[0]
    bf = jnp.bfloat16
    fr, fi = far[:, :m], far[:, m:]
    ratio = amplitude.astype(jnp.float32) / jnp.maximum(jnp.sqrt(fr * fr + fi * fi), 0.2)
    projected = jnp.concatenate([(fr * ratio).astype(bf), (fi * ratio).astype(bf)], 0)
    back_half = dot(table_b[...], projected).astype(bf)
    back = dot(jnp.concatenate([back_half[:m], back_half[m:]], 1), table_a[...])
    return back[:, :m] - er, back[:, m:] - ei


def whole_kernel(nx, ny, step_size, *refs):
    offsets, spec, *given = refs[:6]
    new_spec, new_probe = refs[6:8]
    pad, probe, amplitudes, table_a, table_b, bufs, grad, prob, total, light_all = refs[8:18]
    pair, acc, xr1, xr2, zr1, zr2, ipair, iacc, ixr, izr, ppair, held, inner, hub, part = refs[18:33]
    hsend, hrecv, local, gsend, grecv, isend, irecv, psend, precv = refs[33:]
    tile, m = spec.shape[3], probe.shape[1]
    wide = pad.shape[3]
    half = (wide - tile) // 2
    h = grad.shape[3]
    positions, chunks = amplitudes.shape[0], psend.shape[1]
    p = lax.axis_index("pos")
    partner = {"pos": 1 - p}
    loads = [pltpu.make_async_copy(spec, pad.at[:, pl.ds(half // 8, tile // 8), :, pl.ds(half, tile)], local.at[0])]
    for i, (src, dst) in enumerate(zip(given, (probe, amplitudes, table_a, table_b)), 1):
        loads.append(pltpu.make_async_copy(src, dst, local.at[i]))
    for c in loads:
        c.start()
    roles = [Role(q, nx, ny) for q in range(2)]
    sides = roles[1].sides1 + roles[0].sides1
    near_greet(ny, partner, roles[1].sides1, roles[0].sides1)
    halos = [Halo(r, spec, pad, hsend, hrecv, partner) for r in roles]
    folds = [
        Fold(
            roles[q],
            roles[1 - q],
            grad.at[q],
            grad.at[1 - q],
            pair,
            acc,
            (zr1, xr1, zr2, xr2),
            None,
            gsend,
            grecv,
            partner,
        )
        for q in range(2)
    ]
    role = Role(p, nx, ny, 0)
    light = Fold(
        role,
        role,
        grad.at[2, :, pl.ds(p, 1)],
        grad.at[2, :, pl.ds(1 - p, 1)],
        ipair,
        iacc,
        (None, ixr, izr, None),
        light_all,
        isend,
        irecv,
        partner,
    )
    probes = [
        kind(q, nx, ny, prob, ppair, held, inner, hub, part, total, psend, precv, partner)
        for q, kind in enumerate((SideFirst, ChainFirst))
    ]
    placer = Placer(offsets, bufs, m, positions)

    def gather(k):
        for g in range(4):
            for b in range(2):
                grad[k, g, b] = placer.rows(k, (2 * g + b) * h, h)

    each(lambda q: halos[q].begin())
    for i, at in enumerate(
        (
            (slice(None), pl.ds(0, half // 8)),
            (slice(None), pl.ds((half + tile) // 8, half // 8)),
            (slice(None), slice(None), slice(None), pl.ds(0, half)),
            (slice(None), slice(None), slice(None), pl.ds(half + tile, half)),
        )
    ):

        @pl.when(jnp.logical_not(sides[i].has))
        def _(at=at):
            pad[at] = jnp.zeros(pad.at[at].shape, pad.dtype)

    placer.clear()
    loads[1].wait()
    power = probe[0] * probe[0] + probe[1] * probe[1]
    for j in range(positions):
        placer.put(j, 2, power)
    gather(2)
    light.begin()

    def strips(q):
        halos[q].relay()

    def corners(q):
        halos[q].relay_corners()
        halos[1 - q].arrive()

    each(strips)
    for i in range(3):
        light.add(i)
    light.send_rims(0)
    each(corners)
    for c in loads[:1] + loads[2:]:
        c.wait()
    pr, pi = probe[0], probe[1]
    windows = [[placer.window(j, pad, k) for k in range(2)] for j in range(positions)]
    fields = [forward(windows[j], pr, pi, table_a, table_b) for j in range(positions)]
    light.fold(0)
    light.send_rims(1)
    diffs = [backward(*fields[j], amplitudes[j], table_a, table_b) for j in range(positions)]
    sums = [None, None]
    for (ar, ai), (dr, di) in zip(windows, diffs):
        for k, t in enumerate((ar * dr + ai * di, ar * di - ai * dr)):
            sums[k] = t if sums[k] is None else sums[k] + t
    rows = m // chunks
    for c in range(chunks):
        at = pl.ds(c * rows, rows)
        for k in range(2):
            prob[k, at] = sums[k][c * rows : (c + 1) * rows]
        remote(prob.at[1 - p, at], ppair.at[at], psend.at[0, c], precv.at[0, c], partner).start()
    for j, (dr, di) in enumerate(diffs):
        placer.put(j, 0, pr * dr + pi * di)
        placer.put(j, 1, pr * di - pi * dr)
    gather(1 - p)
    each(lambda q: folds[q].begin())
    gather(p)

    def update(q):
        q4 = folds[q].q4
        for g in range(2):
            for b in range(2):
                r0 = (2 * g + b) * h
                old = pad[q, (half + r0) // 8 : (half + r0 + h) // 8, :, half : half + tile].reshape(h, tile)
                new_spec[q, r0 : r0 + h] = old + acc[1 + g, b, :, q4 : 3 * q4] / (light_all[b, g, 0] + 1.0)

    def share_copy(q):
        return remote(new_spec.at[q], new_spec.at[q], gsend.at[7], grecv.at[7], partner)

    def object_last(q):
        light.arrive()
        folds[q].fold(1)
        update(q)
        share_copy(q).start()

    def objects(q):
        probe_sum, fold = probes[q], folds[q]
        probe_sum.one()
        inward, outward, late, early = probe_sum.parts()
        fold.add(0)
        fold.add(1)
        if q == 0:
            fold.send_rims(0)
        else:
            fold.send_rims(0, early)
        fold.add(2)
        light.fold(1)
        light.share()
        probe_sum.two()
        if q == 0:
            fold.fold(0)
            fold.send_rims(1)
            probe_sum.three()
            object_last(q)
            probe_sum.four()
        else:
            fold.fold(0, inward)
            fold.send_rims(0, late)
            probe_sum.three()
            fold.fold(0, outward)
            fold.send_rims(1)
            probe_sum.four()
            object_last(q)
            probe_sum.five()

    each(objects)

    def closing(q):
        for c in range(chunks):
            probes[q].share(c, 1 - q).wait_recv()
        share_copy(1 - q).wait_recv()
        share_copy(q).wait_send()
        light.finish()
        folds[q].finish()
        probes[q].end()
        halos[q].finish()

    each(closing)
    for k in range(2):
        new_probe[k] = probe[k] + total[k] * step_size


def emit_kernel(spec, probe, new_spec, new_probe, sem):
    copies = [
        pltpu.make_async_copy(src.at[k], dst.at[k], sem.at[i, k])
        for i, (src, dst) in enumerate(((spec, new_spec), (probe, new_probe)))
        for k in range(2)
    ]
    for c in copies:
        c.start()
    for c in copies:
        c.wait()


def tables(length):
    index = np.arange(length)
    angle = ((index[:, None] * index[None, :]) % length).astype(np.float32) * np.float32(2.0 * math.pi / length)
    scale = np.float32(1.0 / math.sqrt(length))
    c = np.cos(angle) * scale
    s = np.sin(angle) * scale
    a = np.block([[c, s], [-s, c]]).astype(jnp.bfloat16)
    b = np.block([[c, -s], [s, c]]).astype(jnp.bfloat16)
    return a, b


def shards(nx, ny, consts, specimen, probe_wave, amplitudes, offsets):
    m = probe_wave.shape[1]
    tile = specimen.shape[1]
    wide = tile + m
    f32 = jnp.float32
    vm = pl.BlockSpec(memory_space=VMEM)
    sm = pl.BlockSpec(memory_space=pltpu.SMEM)
    hbm = pl.BlockSpec(memory_space=pltpu.HBM)
    dma = pltpu.SemaphoreType.DMA
    n = nx * ny
    h = wide // 8
    chunks = 8
    positions = offsets.shape[0]
    held = (probe_wave, amplitudes, consts[0], consts[1])

    step_size = 1.0 / math.sqrt(positions * n * 2)
    results = pl.pallas_call(
        functools.partial(whole_kernel, nx, ny, step_size),
        out_shape=[VMEM(specimen.shape, f32), VMEM(probe_wave.shape, f32)],
        in_specs=[sm] + [hbm] * 5,
        out_specs=[vm, vm],
        scratch_shapes=[
            VMEM((2, wide // 8, 8, wide), f32),
            *[VMEM(x.shape, x.dtype) for x in held],
            VMEM((positions, 3, (2 * (tile - 8) + m + 8) // 8, 8, wide), f32),
            VMEM((3, 4, 2, h, wide), f32),
            VMEM((2, m, m), f32),
            VMEM((2, m, m), f32),
            VMEM((2, 2, 1, h, wide // 2), f32),
            VMEM((4, 2, h, wide), f32),
            VMEM((4, 2, h, wide), f32),
            VMEM((2, 4, 2, h, wide // 4), f32),
            VMEM((2, 2, 2, h, wide // 4), f32),
            VMEM((2, 2, h, wide), f32),
            VMEM((2, 2, h, wide // 2), f32),
            VMEM((4, 1, h, wide), f32),
            VMEM((4, 1, h, wide), f32),
            VMEM((2, 4, 1, h, wide // 4), f32),
            VMEM((2, 1, h, wide // 2), f32),
            VMEM((m, m), f32),
            VMEM((ny, m, m), f32),
            VMEM((m, m), f32),
            VMEM((m, m), f32),
            VMEM((m, m), f32),
            dma((20,)),
            dma((20,)),
            dma((5,)),
            dma((8,)),
            dma((8,)),
            dma((8,)),
            dma((8,)),
            dma((3 + ny, chunks)),
            dma((3 + ny, chunks)),
        ],
        compiler_params=pltpu.CompilerParams(vmem_limit_bytes=56 * 2**20, collective_id=0, has_side_effects=True),
        name="whole",
    )(offsets, *[pltpu.with_memory_space_constraint(x, pltpu.HBM) for x in (specimen.reshape(2, tile // 8, 8, tile), *held)])
    return pl.pallas_call(
        emit_kernel,
        out_shape=[jax.ShapeDtypeStruct(specimen.shape, f32), jax.ShapeDtypeStruct(probe_wave.shape, f32)],
        in_specs=[vm] * 2,
        out_specs=[pl.BlockSpec(memory_space=pl.ANY)] * 2,
        scratch_shapes=[dma((2, 2))],
        compiler_params=pltpu.CompilerParams(vmem_limit_bytes=2 * 2**20),
        name="emit",
    )(*results)


def solution(mesh):
    nx, ny = mesh.shape["scanx"], mesh.shape["scany"]

    def run(specimen, probe_wave, amplitudes, offsets):
        consts = tables(probe_wave.shape[2])
        return jax.shard_map(
            lambda *args: shards(nx, ny, [jnp.asarray(t) for t in consts], *args),
            mesh=mesh,
            in_specs=(
                P(None, ("groups", "scanx"), "scany"),
                P(None, "groups", None),
                P(("groups", "scanx", "scany", "pos"), None, None),
                P(("groups", "scanx", "scany", "pos"), None),
            ),
            out_specs=(P(None, ("groups", "scanx"), "scany"), P(None, "groups", None)),
            check_vma=False,
        )(specimen, probe_wave, amplitudes, offsets)

    return run
```

```python
import functools
import math

import jax
import jax.numpy as jnp
import numpy as np
from jax import lax
from jax.experimental import pallas as pl
from jax.experimental.pallas import tpu as pltpu
from jax.sharding import PartitionSpec as P

MESH = pl.DeviceIdType.MESH
VMEM = pltpu.VMEM


def remote(src, dst, send, recv, where):
    return pltpu.make_async_remote_copy(
        src_ref=src, dst_ref=dst, send_sem=send, recv_sem=recv, device_id=where, device_id_type=MESH
    )


def greet(conditions_devices):
    barrier = pltpu.get_barrier_semaphore()
    for present, where in conditions_devices:
        if present is True:
            pl.semaphore_signal(barrier, inc=1, device_id=where, device_id_type=MESH)
        else:

            @pl.when(present)
            def _(where=where):
                pl.semaphore_signal(barrier, inc=1, device_id=where, device_id_type=MESH)

    fixed = sum(1 for present, _ in conditions_devices if present is True)
    peers = [present.astype(jnp.int32) for present, _ in conditions_devices if present is not True]
    pl.semaphore_wait(barrier, sum(peers, fixed))


class Side:
    def __init__(self, axis, count, step):
        me = lax.axis_index(axis)
        self.has = me > 0 if step < 0 else me < count - 1
        self.where = {axis: me + step}


class Role:
    def __init__(self, q, nx, ny, order=None):
        order = q if order is None else order
        along_x = ("scanx", nx, Side("scanx", nx, -1), Side("scanx", nx, 1))
        along_y = ("scany", ny, Side("scany", ny, -1), Side("scany", ny, 1))
        one, two = (along_y, along_x) if order == 0 else (along_x, along_y)
        self.q, self.o, self.rows_first = q, 1 - q, order == 1
        self.axis1, self.n1, self.sides1 = one[0], one[1], one[2:]
        self.axis2, self.n2, self.sides2 = two[0], two[1], two[2:]
        self.me1, self.me2 = lax.axis_index(self.axis1), lax.axis_index(self.axis2)


def when(*conditions):
    return pl.when(functools.reduce(jnp.logical_and, [c for c in conditions if c is not True]))


def dot(a, b):
    return jnp.dot(a, b, preferred_element_type=jnp.float32)


class Halo:
    def __init__(self, role, spec, pad, send, recv, partner):
        self.r, self.spec, self.pad, self.partner = role, spec, pad, partner
        self.send, self.recv = send, recv
        self.direct = not role.rows_first
        tile = spec.shape[3]
        half = (pad.shape[3] - tile) // 2
        self.own = (half, tile)
        self.margins = ((0, half), (half + tile, half))
        self.edges = ((0, half), (tile - half, half))
        self.pad_edges = ((half, half), (tile, half))
        self.whole = (0, tile)

    def at(self, one, two):
        rows, cols = (one, two) if self.r.rows_first else (two, one)
        return (self.r.q, pl.ds(rows[0] // 8, rows[1] // 8), slice(None), pl.ds(*cols))

    def copy(self, src, dst, i, where):
        return remote(src, dst, self.send.at[i], self.recv.at[i], where)

    def strip1(self, m, e):
        return self.copy(
            self.spec.at[self.at(self.edges[1 - m], self.edges[e])],
            self.pad.at[self.at(self.margins[m], self.pad_edges[e])],
            2 * m + e,
            self.r.sides1[1 - m].where,
        )

    def strip2(self, m):
        return self.copy(
            self.spec.at[self.at(self.whole, self.edges[1 - m])],
            self.pad.at[self.at(self.own, self.margins[m])],
            4 + m,
            self.r.sides2[1 - m].where,
        )

    def corner(self, m1, m2):
        if self.direct:
            return self.copy(
                self.spec.at[self.at(self.edges[1 - m1], self.edges[1 - m2])],
                self.pad.at[self.at(self.margins[m1], self.margins[m2])],
                6 + 2 * m1 + m2,
                {**self.r.sides1[1 - m1].where, **self.r.sides2[1 - m2].where},
            )
        return self.copy(
            self.pad.at[self.at(self.margins[m1], self.pad_edges[1 - m2])],
            self.pad.at[self.at(self.margins[m1], self.margins[m2])],
            6 + 2 * m1 + m2,
            self.r.sides2[1 - m2].where,
        )

    def share(self, i, one, two):
        ref = self.pad.at[self.at(one, two)]
        return self.copy(ref, ref, 10 + i, self.partner)

    def share1(self, m, e):
        return self.share(2 * m + e, self.margins[m], self.pad_edges[e])

    def share2(self, m):
        return self.share(4 + m, self.own, self.margins[m])

    def share_corner(self, m1, m2):
        return self.share(6 + 2 * m1 + m2, self.margins[m1], self.margins[m2])

    def begin(self):
        r = self.r
        if self.direct:
            for m1 in range(2):
                for m2 in range(2):
                    when(r.sides1[1 - m1].has, r.sides2[1 - m2].has)(self.corner(m1, m2).start)
        for m in range(2):
            for e in range(2):
                when(r.sides1[1 - m].has, r.sides2[e].has)(self.strip1(m, e).start)
        for m in range(2):
            when(r.sides2[1 - m].has)(self.strip2(m).start)
        for m in range(2):
            for e in range(2):
                when(r.sides1[1 - m].has, jnp.logical_not(r.sides2[e].has))(self.strip1(m, e).start)

    def relay(self):
        r = self.r
        for m1 in range(2):
            for e in range(2):

                @when(r.sides1[m1].has, r.sides2[e].has)
                def _():
                    self.strip1(m1, e).wait_recv()
                    if not self.direct:
                        self.corner(m1, 1 - e).start()
                    self.share1(m1, e).start()

        for m in range(2):

            @when(r.sides2[m].has)
            def _():
                self.strip2(m).wait_recv()
                self.share2(m).start()

        for m1 in range(2):
            for e in range(2):

                @when(r.sides1[m1].has, jnp.logical_not(r.sides2[e].has))
                def _():
                    self.strip1(m1, e).wait_recv()
                    self.share1(m1, e).start()

    def relay_corners(self):
        r = self.r
        for m1 in range(2):
            for m2 in range(2):

                @when(r.sides1[m1].has, r.sides2[m2].has)
                def _():
                    self.corner(m1, m2).wait_recv()
                    self.share_corner(m1, m2).start()

    def arrive(self):
        r = self.r
        for m in range(2):
            for e in range(2):
                when(r.sides1[m].has)(self.share1(m, e).wait_recv)
            when(r.sides2[m].has)(self.share2(m).wait_recv)
        for m1 in range(2):
            for m2 in range(2):
                when(r.sides1[m1].has, r.sides2[m2].has)(self.share_corner(m1, m2).wait_recv)

    def finish(self):
        r = self.r
        for m in range(2):
            for e in range(2):
                when(r.sides1[1 - m].has)(self.strip1(m, e).wait_send)
                when(r.sides1[m].has)(self.share1(m, e).wait_send)
            when(r.sides2[1 - m].has)(self.strip2(m).wait_send)
            when(r.sides2[m].has)(self.share2(m).wait_send)
        for m1 in range(2):
            for m2 in range(2):
                sent = r.sides1[1 - m1].has if self.direct else r.sides1[m1].has
                when(sent, r.sides2[1 - m2].has)(self.corner(m1, m2).wait_send)
                when(r.sides1[m1].has, r.sides2[m2].has)(self.share_corner(m1, m2).wait_send)


class Fold:
    def __init__(self, role, other, mine, theirs, pair, acc, rims, core, send, recv, partner):
        self.r, self.other, self.mine, self.theirs, self.pair, self.acc = role, other, mine, theirs, pair, acc
        self.rows1, self.cols1, self.rows2, self.cols2 = rims
        self.core, self.send, self.recv, self.partner = core, send, recv, partner
        w = acc.shape[-1]
        self.w, self.q4 = w, w // 4

    def piece(self, i, r):
        q4, cols = self.q4, (slice(None),) * 3
        if r.rows_first:
            return ((pl.ds(0, 1),), (pl.ds(3, 1),), (pl.ds(1, 2),))[i]
        return cols + ((pl.ds(0, q4),), (pl.ds(3 * q4, q4),), (pl.ds(q4, 2 * q4),))[i]

    def needed(self, i, r):
        return pl.when(r.sides1[i].has) if i < 2 else lambda f: f()

    def pair_copy(self, i, r):
        at = self.piece(i, r)
        return remote(self.theirs.at[at], self.pair.at[at], self.send.at[i], self.recv.at[i], self.partner)

    def begin(self):
        for i in range(3):
            self.needed(i, self.other)(self.pair_copy(i, self.other).start)

    def add(self, i):
        @self.needed(i, self.r)
        def _():
            self.pair_copy(i, self.r).wait_recv()
            at = self.piece(i, self.r)
            self.acc[at] = self.mine[at] + self.pair[at]

    def spot(self, stage, i, m):
        r, q4, w = self.r, self.q4, self.w
        if r.rows_first == (stage == 0):
            if stage == 1:
                return (i, slice(None), slice(None), pl.ds(q4, 2 * q4)), self.rows2.at[m]
            cols = pl.ds(0, w)
            if r.n2 == 2:
                cols = pl.ds(pl.multiple_of((1 - r.me2) * q4, q4), 3 * q4)
            return (i, slice(None), slice(None), cols), self.rows1.at[m, :, :, cols]
        groups = pl.ds(0, 4) if stage == 0 else pl.ds(1, 2)
        return (groups, slice(None), slice(None), pl.ds(i * q4, q4)), (self.cols1 if stage == 0 else self.cols2).at[m]

    def rim_copy(self, stage, m):
        sides = self.r.sides1 if stage == 0 else self.r.sides2
        at, rim = self.spot(stage, 3 * (1 - m), m)
        i = 3 + 2 * stage + m
        return remote(self.acc.at[at], rim, self.send.at[i], self.recv.at[i], sides[1 - m].where)

    def send_rims(self, stage, only=lambda k: True):
        sides = self.r.sides1 if stage == 0 else self.r.sides2
        for m in range(2):
            when(sides[1 - m].has, only(1 - m))(self.rim_copy(stage, m).start)

    def fold(self, stage, only=lambda k: True):
        sides = self.r.sides1 if stage == 0 else self.r.sides2
        for m in range(2):

            @when(sides[m].has, only(m))
            def _():
                self.rim_copy(stage, m).wait_recv()
                at, rim = self.spot(stage, 1 + m, m)
                self.acc[at] = self.acc[at] + rim[...]

    def share_copy(self, q):
        return remote(self.core.at[q], self.core.at[q], self.send.at[7], self.recv.at[7], self.partner)

    def share(self):
        q4 = self.q4
        self.core[self.r.q] = self.acc[1:3, :, :, q4 : 3 * q4]
        self.share_copy(self.r.q).start()

    def arrive(self):
        self.share_copy(self.r.o).wait_recv()

    def finish(self):
        r = self.r
        for i in range(3):
            self.needed(i, self.other)(self.pair_copy(i, self.other).wait_send)
        for m in range(2):
            when(r.sides1[1 - m].has)(self.rim_copy(0, m).wait_send)
            when(r.sides2[1 - m].has)(self.rim_copy(1, m).wait_send)
        if self.core is not None:
            self.share_copy(r.q).wait_send()


class ProbeSum:
    def __init__(self, q, nx, ny, turn, prob, ppair, held, inner, hub, part, total, send, recv, partner):
        self.q, self.ny = q, ny
        self.prob, self.ppair, self.held = prob, ppair, held
        self.inner, self.hub, self.part, self.total = inner, hub, part, total
        self.send, self.recv, self.partner = send, recv, partner
        chunks = send.shape[1]
        self.rows = prob.shape[1] // chunks
        self.list = range(turn * chunks // 2, (turn + 1) * chunks // 2)
        me, mid = lax.axis_index("scanx"), nx // 2
        self.lower, self.upper = me < mid, me >= mid
        step = 2 * self.lower.astype(jnp.int32) - 1
        self.to_inner, self.to_outer = {"scanx": me + step}, {"scanx": me - step}
        self.has_outer = jnp.logical_and(me > 0, me < nx - 1)
        self.no_outer = jnp.logical_not(self.has_outer)
        self.is_hub = jnp.logical_or(me == mid - 1, me == mid)
        self.not_hub = jnp.logical_not(self.is_hub)
        self.mine = lax.axis_index("scany")

    def parts(self):
        inner = (self.upper, self.lower)
        return (
            lambda k: inner[k],
            lambda k: inner[1 - k],
            lambda k: jnp.logical_and(inner[k], self.not_hub),
            lambda k: jnp.logical_or(inner[1 - k], self.is_hub),
        )

    def at(self, c):
        return pl.ds(c * self.rows, self.rows)

    def copy(self, src, dst, s, r, c, where):
        return remote(src.at[self.at(c)], dst.at[self.at(c)], self.send.at[s, c], self.recv.at[r, c], where)

    def pair(self, c):
        return self.copy(self.prob.at[1 - self.q], self.ppair, 0, 0, c, self.partner)

    def inward(self, c):
        return self.copy(self.part, self.inner, 1, 1, c, self.to_inner)

    def across(self, c):
        return self.copy(self.part, self.hub, 1, 2, c, self.to_inner)

    def outward(self, c, src):
        return self.copy(src, self.hub, 2, 2, c, self.to_outer)

    def share(self, c, q):
        return self.copy(self.total.at[q], self.total.at[q], 3, 3, c, self.partner)

    def sides(self, c):
        out = []
        for d in range(1, self.ny):
            slot = self.held.at[self.mine]
            out.append(self.copy(slot, slot, 3 + d, 3 + d, c, {"scany": lax.rem(self.mine + d, self.ny)}))
        return out

    def side_arrive(self, c):
        for d in range(1, self.ny):
            slot = self.held.at[lax.rem(self.mine - d + self.ny, self.ny)]
            self.copy(slot, slot, 3 + d, 3 + d, c, self.partner).wait_recv()

    def side_sum(self, c):
        self.side_arrive(c)
        out = self.held[0, self.at(c)]
        for i in range(1, self.ny):
            out = out + self.held[i, self.at(c)]
        return out

    def pair_sum(self, c):
        self.pair(c).wait_recv()
        return self.prob[self.q, self.at(c)] + self.ppair[self.at(c)]

    def send_sides(self, c, value):
        self.held[self.mine, self.at(c)] = value
        for copy in self.sides(c):
            copy.start()

    def send_inward(self, c):
        when(self.not_hub)(self.inward(c).start)
        when(self.is_hub)(self.across(c).start)

    def collect(self, i):
        c = self.list[i]

        @pl.when(self.has_outer)
        def _():
            self.inward(c).wait_recv()
            self.part[self.at(c)] = self.part[self.at(c)] + self.inner[self.at(c)]
            self.send_inward(c)

    def start_part(self, c, value):
        self.part[self.at(c)] = value
        when(self.no_outer)(functools.partial(self.send_inward, c))

    def from_hub(self, i):
        c = self.list[i]
        self.across(c).wait_recv()
        self.done(c, self.part[self.at(c)] + self.hub[self.at(c)])

    def from_inner(self, i):
        c = self.list[i]
        self.across(c).wait_recv()
        self.done(c, self.hub[self.at(c)])

    def finish(self, src):
        for c in self.list:
            self.pair(c).wait_send()
            self.inward(c).wait_send()
            when(self.has_outer)(self.outward(c, src).wait_send)
            self.share(c, self.q).wait_send()
            for copy in self.sides(c):
                copy.wait_send()


class SideFirst(ProbeSum):
    def one(self):
        for c in self.list:
            self.send_sides(c, self.pair_sum(c))

    def side(self, i):
        c = self.list[i]
        self.start_part(c, self.side_sum(c))

    def done(self, c, value):
        self.total[self.q, self.at(c)] = value
        when(self.has_outer)(self.outward(c, self.total.at[self.q]).start)
        self.share(c, self.q).start()

    def end(self):
        self.finish(self.total.at[self.q])


class ChainFirst(ProbeSum):
    def one(self):
        for c in self.list:
            self.start_part(c, self.pair_sum(c))

    def side(self, i):
        c = self.list[i]
        self.total[self.q, self.at(c)] = self.side_sum(c)
        self.share(c, self.q).start()

    def done(self, c, value):
        self.send_sides(c, value)
        when(self.has_outer)(self.outward(c, self.held.at[self.mine]).start)

    def end(self):
        self.finish(self.held.at[self.mine])


class Both:
    def __init__(self, q, *args):
        self.q = q
        self.a, self.b = SideFirst(q, *args[:2], 0, *args[2:]), ChainFirst(q, *args[:2], 1, *args[2:])
        self.count = range(len(self.a.list))
        self.is_hub, self.not_hub, self.parts = self.a.is_hub, self.a.not_hub, self.a.parts

    def one(self):
        self.b.one()
        self.a.one()

    def two(self):
        for i in self.count:
            self.b.collect(i)
            self.a.side(i)

    def three(self):
        for i in self.count:
            self.a.collect(i)

        @pl.when(self.is_hub)
        def _():
            for i in self.count:
                self.b.from_hub(i)

    def four(self):
        @pl.when(self.is_hub)
        def _():
            for i in self.count:
                self.a.from_hub(i)
                self.b.side(i)

        @pl.when(self.not_hub)
        def _():
            for i in self.count:
                self.b.from_inner(i)

    def five(self):
        @pl.when(self.not_hub)
        def _():
            for i in self.count:
                self.a.from_inner(i)
                self.b.side(i)

    def end(self):
        self.a.end()
        self.b.end()


def near_greet(ny, partner, rows, cols):
    my = lax.axis_index("scany")
    greet(
        [(True, partner)]
        + [(True, {"scany": lax.rem(my + d, ny)}) for d in range(1, ny)]
        + [(side.has, side.where) for side in rows]
        + [(jnp.logical_and(a.has, b.has), {**a.where, **b.where}) for a in rows for b in cols]
    )


def each(step):
    p = lax.axis_index("pos")
    for q in range(2):
        pl.when(p == q)(functools.partial(step, q))


class Placer:
    def __init__(self, offsets, bufs, m, positions):
        self.bufs, self.m = bufs, m
        self.tall, self.span = m + 8, m + 128
        self.top = (bufs.shape[2] - self.tall // 8) // 2
        self.spots = []
        for j in range(positions):
            row, col = offsets[j, 0], offsets[j, 1]
            self.spots.append((lax.rem(row, 8), lax.rem(col, 128), lax.div(row, 8), lax.div(col, 128)))

    def clear(self):
        n, k, rows = self.bufs.shape[:3]
        bottom = self.top + self.tall // 8
        for j in range(n):
            for c in range(k):
                self.bufs[j, c, 0 : self.top] = jnp.zeros((self.top, *self.bufs.shape[3:]), jnp.float32)
                self.bufs[j, c, bottom:rows] = jnp.zeros((rows - bottom, *self.bufs.shape[3:]), jnp.float32)

    def put(self, j, k, term):
        row_in, col_in, _, step = self.spots[j]
        m, wide = self.m, self.bufs.shape[4]
        blank_rows = jnp.zeros((self.tall - m, m), jnp.float32)
        blank_cols = jnp.zeros((self.tall, self.span - m), jnp.float32)
        moved = pltpu.roll(jnp.concatenate([term, blank_rows], 0), row_in, 0)
        moved = pltpu.roll(jnp.concatenate([moved, blank_cols], 1), col_in, 1)
        out = None
        for d in range((wide - self.span) // 128 + 1):
            parts = [jnp.zeros((self.tall, w), jnp.float32) for w in (128 * d, wide - self.span - 128 * d)]
            here = jnp.concatenate([x for x in (parts[0], moved, parts[1]) if x.shape[1]], 1)
            out = here if out is None else jnp.where(step == d, here, out)
        self.bufs[j, k, self.top : self.top + self.tall // 8] = out.reshape(self.tall // 8, 8, wide)

    def rows(self, k, r0, count):
        out = None
        for j, (_, _, row, _) in enumerate(self.spots):
            part = self.bufs[j, k, pl.ds(self.top - row + r0 // 8, count // 8)]
            out = part if out is None else out + part
        return out.reshape(count, self.bufs.shape[4])

    def window(self, j, pad, k):
        row_in, col_in, row, step = self.spots[j]
        wide = pad.shape[3]
        block = pad[k, pl.ds(row, self.tall // 8)].reshape(self.tall, wide)
        out = block[:, : self.span]
        for d in range(1, (wide - self.span) // 128 + 1):
            out = jnp.where(step == d, block[:, 128 * d : 128 * d + self.span], out)
        out = pltpu.roll(out, lax.rem(self.span - col_in, self.span), 1)[:, : self.m]
        return pltpu.roll(out, lax.rem(self.tall - row_in, self.tall), 0)[: self.m]


def forward(window, pr, pi, table_a, table_b):
    m = pr.shape[0]
    bf = jnp.bfloat16
    ar, ai = window
    er = pr * ar - pi * ai
    ei = pr * ai + pi * ar
    left = dot(table_a[...], jnp.concatenate([er.astype(bf), ei.astype(bf)], 0)).astype(bf)
    return er, ei, dot(jnp.concatenate([left[:m], left[m:]], 1), table_b[...])


def backward(er, ei, far, amplitude, table_a, table_b):
    m = er.shape[0]
    bf = jnp.bfloat16
    fr, fi = far[:, :m], far[:, m:]
    ratio = amplitude.astype(jnp.float32) / jnp.maximum(jnp.sqrt(fr * fr + fi * fi), 0.2)
    projected = jnp.concatenate([(fr * ratio).astype(bf), (fi * ratio).astype(bf)], 0)
    back_half = dot(table_b[...], projected).astype(bf)
    back = dot(jnp.concatenate([back_half[:m], back_half[m:]], 1), table_a[...])
    return back[:, :m] - er, back[:, m:] - ei


def whole_kernel(nx, ny, step_size, *refs):
    offsets, spec, *given = refs[:6]
    new_spec, new_probe = refs[6:8]
    pad, probe, amplitudes, table_a, table_b, bufs, grad, prob, total, light_all = refs[8:18]
    pair, acc, xr1, xr2, zr1, zr2, ipair, iacc, ixr, izr, ppair, held, inner, hub, part = refs[18:33]
    hsend, hrecv, local, gsend, grecv, isend, irecv, psend, precv = refs[33:]
    tile, m = spec.shape[3], probe.shape[1]
    wide = pad.shape[3]
    half = (wide - tile) // 2
    h = grad.shape[3]
    positions, chunks = amplitudes.shape[0], psend.shape[1]
    p = lax.axis_index("pos")
    partner = {"pos": 1 - p}
    loads = [pltpu.make_async_copy(spec, pad.at[:, pl.ds(half // 8, tile // 8), :, pl.ds(half, tile)], local.at[0])]
    for i, (src, dst) in enumerate(zip(given, (probe, amplitudes, table_a, table_b)), 1):
        loads.append(pltpu.make_async_copy(src, dst, local.at[i]))
    for c in loads:
        c.start()
    roles = [Role(q, nx, ny) for q in range(2)]
    sides = roles[1].sides1 + roles[0].sides1
    near_greet(ny, partner, roles[1].sides1, roles[0].sides1)
    halos = [Halo(r, spec, pad, hsend, hrecv, partner) for r in roles]
    folds = [
        Fold(
            roles[q],
            roles[1 - q],
            grad.at[q],
            grad.at[1 - q],
            pair,
            acc,
            (zr1, xr1, zr2, xr2),
            None,
            gsend,
            grecv,
            partner,
        )
        for q in range(2)
    ]
    role = Role(p, nx, ny, 0)
    light = Fold(
        role,
        role,
        grad.at[2, :, pl.ds(p, 1)],
        grad.at[2, :, pl.ds(1 - p, 1)],
        ipair,
        iacc,
        (None, ixr, izr, None),
        light_all,
        isend,
        irecv,
        partner,
    )
    probes = [Both(q, nx, ny, prob, ppair, held, inner, hub, part, total, psend, precv, partner) for q in range(2)]
    placer = Placer(offsets, bufs, m, positions)

    def gather(k):
        for g in range(4):
            for b in range(2):
                grad[k, g, b] = placer.rows(k, (2 * g + b) * h, h)

    each(lambda q: halos[q].begin())
    for i, at in enumerate(
        (
            (slice(None), pl.ds(0, half // 8)),
            (slice(None), pl.ds((half + tile) // 8, half // 8)),
            (slice(None), slice(None), slice(None), pl.ds(0, half)),
            (slice(None), slice(None), slice(None), pl.ds(half + tile, half)),
        )
    ):

        @pl.when(jnp.logical_not(sides[i].has))
        def _(at=at):
            pad[at] = jnp.zeros(pad.at[at].shape, pad.dtype)

    placer.clear()
    loads[1].wait()
    power = probe[0] * probe[0] + probe[1] * probe[1]
    for j in range(positions):
        placer.put(j, 2, power)
    gather(2)
    light.begin()

    def strips(q):
        halos[q].relay()

    def corners(q):
        halos[q].relay_corners()
        halos[1 - q].arrive()

    each(strips)
    for i in range(3):
        light.add(i)
    light.send_rims(0)
    each(corners)
    for c in loads[:1] + loads[2:]:
        c.wait()
    pr, pi = probe[0], probe[1]
    windows = [[placer.window(j, pad, k) for k in range(2)] for j in range(positions)]
    fields = [forward(windows[j], pr, pi, table_a, table_b) for j in range(positions)]
    diffs = [backward(*fields[j], amplitudes[j], table_a, table_b) for j in range(positions)]
    sums = [None, None]
    for (ar, ai), (dr, di) in zip(windows, diffs):
        for k, t in enumerate((ar * dr + ai * di, ar * di - ai * dr)):
            sums[k] = t if sums[k] is None else sums[k] + t
    rows = m // chunks
    for c in range(chunks):
        at = pl.ds(c * rows, rows)
        for k in range(2):
            prob[k, at] = sums[k][c * rows : (c + 1) * rows]
        remote(prob.at[1 - p, at], ppair.at[at], psend.at[0, c], precv.at[0, c], partner).start()
    for j, (dr, di) in enumerate(diffs):
        placer.put(j, 0, pr * dr + pi * di)
        placer.put(j, 1, pr * di - pi * dr)
    gather(1 - p)
    each(lambda q: folds[q].begin())
    gather(p)

    def update(q):
        q4 = folds[q].q4
        for g in range(2):
            for b in range(2):
                r0 = (2 * g + b) * h
                old = pad[q, (half + r0) // 8 : (half + r0 + h) // 8, :, half : half + tile].reshape(h, tile)
                new_spec[q, r0 : r0 + h] = old + acc[1 + g, b, :, q4 : 3 * q4] / (light_all[b, g, 0] + 1.0)

    def share_copy(q):
        return remote(new_spec.at[q], new_spec.at[q], gsend.at[7], grecv.at[7], partner)

    def object_last(q):
        light.arrive()
        folds[q].fold(1)
        update(q)
        share_copy(q).start()

    def objects(q):
        probe_sum, fold = probes[q], folds[q]
        inward, outward, late, early = probe_sum.parts()
        probe_sum.one()
        fold.add(0)
        fold.add(1)
        if q == 0:
            fold.send_rims(0)
        else:
            fold.send_rims(0, early)
        fold.add(2)
        light.fold(0)
        light.send_rims(1)
        probe_sum.two()
        if q == 1:
            fold.send_rims(0, late)
        probe_sum.three()
        fold.fold(0)
        fold.send_rims(1)
        light.fold(1)
        light.share()
        probe_sum.four()
        object_last(q)
        probe_sum.five()

    each(objects)

    def closing(q):
        for c in range(chunks):
            probes[q].a.share(c, 1 - q).wait_recv()
        share_copy(1 - q).wait_recv()
        share_copy(q).wait_send()
        light.finish()
        folds[q].finish()
        probes[q].end()
        halos[q].finish()

    each(closing)
    for k in range(2):
        new_probe[k] = probe[k] + total[k] * step_size


def emit_kernel(spec, probe, new_spec, new_probe, sem):
    copies = [
        pltpu.make_async_copy(src.at[k], dst.at[k], sem.at[i, k])
        for i, (src, dst) in enumerate(((spec, new_spec), (probe, new_probe)))
        for k in range(2)
    ]
    for c in copies:
        c.start()
    for c in copies:
        c.wait()


def tables(length):
    index = np.arange(length)
    angle = ((index[:, None] * index[None, :]) % length).astype(np.float32) * np.float32(2.0 * math.pi / length)
    scale = np.float32(1.0 / math.sqrt(length))
    c = np.cos(angle) * scale
    s = np.sin(angle) * scale
    a = np.block([[c, s], [-s, c]]).astype(jnp.bfloat16)
    b = np.block([[c, -s], [s, c]]).astype(jnp.bfloat16)
    return a, b


def shards(nx, ny, consts, specimen, probe_wave, amplitudes, offsets):
    m = probe_wave.shape[1]
    tile = specimen.shape[1]
    wide = tile + m
    f32 = jnp.float32
    vm = pl.BlockSpec(memory_space=VMEM)
    sm = pl.BlockSpec(memory_space=pltpu.SMEM)
    hbm = pl.BlockSpec(memory_space=pltpu.HBM)
    dma = pltpu.SemaphoreType.DMA
    n = nx * ny
    h = wide // 8
    chunks = 8
    positions = offsets.shape[0]
    held = (probe_wave, amplitudes, consts[0], consts[1])

    step_size = 1.0 / math.sqrt(positions * n * 2)
    results = pl.pallas_call(
        functools.partial(whole_kernel, nx, ny, step_size),
        out_shape=[VMEM(specimen.shape, f32), VMEM(probe_wave.shape, f32)],
        in_specs=[sm] + [hbm] * 5,
        out_specs=[vm, vm],
        scratch_shapes=[
            VMEM((2, wide // 8, 8, wide), f32),
            *[VMEM(x.shape, x.dtype) for x in held],
            VMEM((positions, 3, (2 * (tile - 8) + m + 8) // 8, 8, wide), f32),
            VMEM((3, 4, 2, h, wide), f32),
            VMEM((2, m, m), f32),
            VMEM((2, m, m), f32),
            VMEM((2, 2, 1, h, wide // 2), f32),
            VMEM((4, 2, h, wide), f32),
            VMEM((4, 2, h, wide), f32),
            VMEM((2, 4, 2, h, wide // 4), f32),
            VMEM((2, 2, 2, h, wide // 4), f32),
            VMEM((2, 2, h, wide), f32),
            VMEM((2, 2, h, wide // 2), f32),
            VMEM((4, 1, h, wide), f32),
            VMEM((4, 1, h, wide), f32),
            VMEM((2, 4, 1, h, wide // 4), f32),
            VMEM((2, 1, h, wide // 2), f32),
            VMEM((m, m), f32),
            VMEM((ny, m, m), f32),
            VMEM((m, m), f32),
            VMEM((m, m), f32),
            VMEM((m, m), f32),
            dma((20,)),
            dma((20,)),
            dma((5,)),
            dma((8,)),
            dma((8,)),
            dma((8,)),
            dma((8,)),
            dma((3 + ny, chunks)),
            dma((3 + ny, chunks)),
        ],
        compiler_params=pltpu.CompilerParams(vmem_limit_bytes=56 * 2**20, collective_id=0, has_side_effects=True),
        name="whole",
    )(offsets, *[pltpu.with_memory_space_constraint(x, pltpu.HBM) for x in (specimen.reshape(2, tile // 8, 8, tile), *held)])
    return pl.pallas_call(
        emit_kernel,
        out_shape=[jax.ShapeDtypeStruct(specimen.shape, f32), jax.ShapeDtypeStruct(probe_wave.shape, f32)],
        in_specs=[vm] * 2,
        out_specs=[pl.BlockSpec(memory_space=pl.ANY)] * 2,
        scratch_shapes=[dma((2, 2))],
        compiler_params=pltpu.CompilerParams(vmem_limit_bytes=2 * 2**20),
        name="emit",
    )(*results)


def solution(mesh):
    nx, ny = mesh.shape["scanx"], mesh.shape["scany"]

    def run(specimen, probe_wave, amplitudes, offsets):
        consts = tables(probe_wave.shape[2])
        return jax.shard_map(
            lambda *args: shards(nx, ny, [jnp.asarray(t) for t in consts], *args),
            mesh=mesh,
            in_specs=(
                P(None, ("groups", "scanx"), "scany"),
                P(None, "groups", None),
                P(("groups", "scanx", "scany", "pos"), None, None),
                P(("groups", "scanx", "scany", "pos"), None),
            ),
            out_specs=(P(None, ("groups", "scanx"), "scany"), P(None, "groups", None)),
            check_vma=False,
        )(specimen, probe_wave, amplitudes, offsets)

    return run
```

```python
import functools
import math

import jax
import jax.numpy as jnp
import numpy as np
from jax import lax
from jax.experimental import pallas as pl
from jax.experimental.pallas import tpu as pltpu
from jax.sharding import PartitionSpec as P

MESH = pl.DeviceIdType.MESH
VMEM = pltpu.VMEM


def remote(src, dst, send, recv, where):
    return pltpu.make_async_remote_copy(
        src_ref=src, dst_ref=dst, send_sem=send, recv_sem=recv, device_id=where, device_id_type=MESH
    )


def greet(conditions_devices):
    barrier = pltpu.get_barrier_semaphore()
    for present, where in conditions_devices:
        if present is True:
            pl.semaphore_signal(barrier, inc=1, device_id=where, device_id_type=MESH)
        else:

            @pl.when(present)
            def _(where=where):
                pl.semaphore_signal(barrier, inc=1, device_id=where, device_id_type=MESH)

    fixed = sum(1 for present, _ in conditions_devices if present is True)
    peers = [present.astype(jnp.int32) for present, _ in conditions_devices if present is not True]
    pl.semaphore_wait(barrier, sum(peers, fixed))


class Side:
    def __init__(self, axis, count, step):
        me = lax.axis_index(axis)
        self.has = me > 0 if step < 0 else me < count - 1
        self.where = {axis: me + step}


class Role:
    def __init__(self, q, nx, ny, order=None):
        order = q if order is None else order
        along_x = ("scanx", nx, Side("scanx", nx, -1), Side("scanx", nx, 1))
        along_y = ("scany", ny, Side("scany", ny, -1), Side("scany", ny, 1))
        one, two = (along_y, along_x) if order == 0 else (along_x, along_y)
        self.q, self.o, self.rows_first = q, 1 - q, order == 1
        self.axis1, self.n1, self.sides1 = one[0], one[1], one[2:]
        self.axis2, self.n2, self.sides2 = two[0], two[1], two[2:]
        self.me1, self.me2 = lax.axis_index(self.axis1), lax.axis_index(self.axis2)


def when(*conditions):
    return pl.when(functools.reduce(jnp.logical_and, [c for c in conditions if c is not True]))


def dot(a, b):
    return jnp.dot(a, b, preferred_element_type=jnp.float32)


class Halo:
    def __init__(self, role, spec, pad, send, recv, partner):
        self.r, self.spec, self.pad, self.partner = role, spec, pad, partner
        self.send, self.recv = send, recv
        self.direct = not role.rows_first
        tile = spec.shape[3]
        half = (pad.shape[3] - tile) // 2
        self.own = (half, tile)
        self.margins = ((0, half), (half + tile, half))
        self.edges = ((0, half), (tile - half, half))
        self.pad_edges = ((half, half), (tile, half))
        self.whole = (0, tile)

    def at(self, one, two):
        rows, cols = (one, two) if self.r.rows_first else (two, one)
        return (self.r.q, pl.ds(rows[0] // 8, rows[1] // 8), slice(None), pl.ds(*cols))

    def copy(self, src, dst, i, where):
        return remote(src, dst, self.send.at[i], self.recv.at[i], where)

    def strip1(self, m, e):
        return self.copy(
            self.spec.at[self.at(self.edges[1 - m], self.edges[e])],
            self.pad.at[self.at(self.margins[m], self.pad_edges[e])],
            2 * m + e,
            self.r.sides1[1 - m].where,
        )

    def strip2(self, m):
        return self.copy(
            self.spec.at[self.at(self.whole, self.edges[1 - m])],
            self.pad.at[self.at(self.own, self.margins[m])],
            4 + m,
            self.r.sides2[1 - m].where,
        )

    def corner(self, m1, m2):
        if self.direct:
            return self.copy(
                self.spec.at[self.at(self.edges[1 - m1], self.edges[1 - m2])],
                self.pad.at[self.at(self.margins[m1], self.margins[m2])],
                6 + 2 * m1 + m2,
                {**self.r.sides1[1 - m1].where, **self.r.sides2[1 - m2].where},
            )
        return self.copy(
            self.pad.at[self.at(self.margins[m1], self.pad_edges[1 - m2])],
            self.pad.at[self.at(self.margins[m1], self.margins[m2])],
            6 + 2 * m1 + m2,
            self.r.sides2[1 - m2].where,
        )

    def share(self, i, one, two):
        ref = self.pad.at[self.at(one, two)]
        return self.copy(ref, ref, 10 + i, self.partner)

    def share1(self, m, e):
        return self.share(2 * m + e, self.margins[m], self.pad_edges[e])

    def share2(self, m):
        return self.share(4 + m, self.own, self.margins[m])

    def share_corner(self, m1, m2):
        return self.share(6 + 2 * m1 + m2, self.margins[m1], self.margins[m2])

    def begin(self):
        r = self.r
        if self.direct:
            for m1 in range(2):
                for m2 in range(2):
                    when(r.sides1[1 - m1].has, r.sides2[1 - m2].has)(self.corner(m1, m2).start)
        for m in range(2):
            for e in range(2):
                when(r.sides1[1 - m].has, r.sides2[e].has)(self.strip1(m, e).start)
        for m in range(2):
            when(r.sides2[1 - m].has)(self.strip2(m).start)
        for m in range(2):
            for e in range(2):
                when(r.sides1[1 - m].has, jnp.logical_not(r.sides2[e].has))(self.strip1(m, e).start)

    def relay(self):
        r = self.r
        for m1 in range(2):
            for e in range(2):

                @when(r.sides1[m1].has, r.sides2[e].has)
                def _():
                    self.strip1(m1, e).wait_recv()
                    if not self.direct:
                        self.corner(m1, 1 - e).start()
                    self.share1(m1, e).start()

        for m in range(2):

            @when(r.sides2[m].has)
            def _():
                self.strip2(m).wait_recv()
                self.share2(m).start()

        for m1 in range(2):
            for e in range(2):

                @when(r.sides1[m1].has, jnp.logical_not(r.sides2[e].has))
                def _():
                    self.strip1(m1, e).wait_recv()
                    self.share1(m1, e).start()

    def relay_corners(self):
        r = self.r
        for m1 in range(2):
            for m2 in range(2):

                @when(r.sides1[m1].has, r.sides2[m2].has)
                def _():
                    self.corner(m1, m2).wait_recv()
                    self.share_corner(m1, m2).start()

    def arrive(self):
        r = self.r
        for m in range(2):
            for e in range(2):
                when(r.sides1[m].has)(self.share1(m, e).wait_recv)
            when(r.sides2[m].has)(self.share2(m).wait_recv)
        for m1 in range(2):
            for m2 in range(2):
                when(r.sides1[m1].has, r.sides2[m2].has)(self.share_corner(m1, m2).wait_recv)

    def finish(self):
        r = self.r
        for m in range(2):
            for e in range(2):
                when(r.sides1[1 - m].has)(self.strip1(m, e).wait_send)
                when(r.sides1[m].has)(self.share1(m, e).wait_send)
            when(r.sides2[1 - m].has)(self.strip2(m).wait_send)
            when(r.sides2[m].has)(self.share2(m).wait_send)
        for m1 in range(2):
            for m2 in range(2):
                sent = r.sides1[1 - m1].has if self.direct else r.sides1[m1].has
                when(sent, r.sides2[1 - m2].has)(self.corner(m1, m2).wait_send)
                when(r.sides1[m1].has, r.sides2[m2].has)(self.share_corner(m1, m2).wait_send)


class Fold:
    def __init__(self, role, other, mine, theirs, pair, acc, rims, core, send, recv, partner):
        self.r, self.other, self.mine, self.theirs, self.pair, self.acc = role, other, mine, theirs, pair, acc
        self.rows1, self.cols1, self.rows2, self.cols2 = rims
        self.core, self.send, self.recv, self.partner = core, send, recv, partner
        w = acc.shape[-1]
        self.w, self.q4 = w, w // 4

    def piece(self, i, r):
        q4, cols = self.q4, (slice(None),) * 3
        if r.rows_first:
            return ((pl.ds(0, 1),), (pl.ds(3, 1),), (pl.ds(1, 2),))[i]
        return cols + ((pl.ds(0, q4),), (pl.ds(3 * q4, q4),), (pl.ds(q4, 2 * q4),))[i]

    def needed(self, i, r):
        return pl.when(r.sides1[i].has) if i < 2 else lambda f: f()

    def pair_copy(self, i, r):
        at = self.piece(i, r)
        return remote(self.theirs.at[at], self.pair.at[at], self.send.at[i], self.recv.at[i], self.partner)

    def begin(self):
        for i in range(3):
            self.needed(i, self.other)(self.pair_copy(i, self.other).start)

    def add(self, i):
        @self.needed(i, self.r)
        def _():
            self.pair_copy(i, self.r).wait_recv()
            at = self.piece(i, self.r)
            self.acc[at] = self.mine[at] + self.pair[at]

    def spot(self, stage, i, m):
        r, q4, w = self.r, self.q4, self.w
        if r.rows_first == (stage == 0):
            if stage == 1:
                return (i, slice(None), slice(None), pl.ds(q4, 2 * q4)), self.rows2.at[m]
            cols = pl.ds(0, w)
            if r.n2 == 2:
                cols = pl.ds(pl.multiple_of((1 - r.me2) * q4, q4), 3 * q4)
            return (i, slice(None), slice(None), cols), self.rows1.at[m, :, :, cols]
        groups = pl.ds(0, 4) if stage == 0 else pl.ds(1, 2)
        return (groups, slice(None), slice(None), pl.ds(i * q4, q4)), (self.cols1 if stage == 0 else self.cols2).at[m]

    def rim_copy(self, stage, m):
        sides = self.r.sides1 if stage == 0 else self.r.sides2
        at, rim = self.spot(stage, 3 * (1 - m), m)
        i = 3 + 2 * stage + m
        return remote(self.acc.at[at], rim, self.send.at[i], self.recv.at[i], sides[1 - m].where)

    def send_rims(self, stage, only=lambda k: True):
        sides = self.r.sides1 if stage == 0 else self.r.sides2
        for m in range(2):
            when(sides[1 - m].has, only(1 - m))(self.rim_copy(stage, m).start)

    def fold(self, stage, only=lambda k: True):
        sides = self.r.sides1 if stage == 0 else self.r.sides2
        for m in range(2):

            @when(sides[m].has, only(m))
            def _():
                self.rim_copy(stage, m).wait_recv()
                at, rim = self.spot(stage, 1 + m, m)
                self.acc[at] = self.acc[at] + rim[...]

    def share_copy(self, q):
        return remote(self.core.at[q], self.core.at[q], self.send.at[7], self.recv.at[7], self.partner)

    def share(self):
        q4 = self.q4
        self.core[self.r.q] = self.acc[1:3, :, :, q4 : 3 * q4]
        self.share_copy(self.r.q).start()

    def arrive(self):
        self.share_copy(self.r.o).wait_recv()

    def finish(self):
        r = self.r
        for i in range(3):
            self.needed(i, self.other)(self.pair_copy(i, self.other).wait_send)
        for m in range(2):
            when(r.sides1[1 - m].has)(self.rim_copy(0, m).wait_send)
            when(r.sides2[1 - m].has)(self.rim_copy(1, m).wait_send)
        if self.core is not None:
            self.share_copy(r.q).wait_send()


class ProbeSum:
    def __init__(self, q, nx, ny, prob, ppair, held, inner, hub, part, total, send, recv, partner):
        self.q, self.ny = q, ny
        self.prob, self.ppair, self.held = prob, ppair, held
        self.inner, self.hub, self.part, self.total = inner, hub, part, total
        self.send, self.recv, self.partner = send, recv, partner
        self.chunks = send.shape[1]
        self.rows = prob.shape[1] // self.chunks
        me, mid = lax.axis_index("scanx"), nx // 2
        self.lower, self.upper = me < mid, me >= mid
        step = 2 * self.lower.astype(jnp.int32) - 1
        self.to_inner, self.to_outer = {"scanx": me + step}, {"scanx": me - step}
        self.has_outer = jnp.logical_and(me > 0, me < nx - 1)
        self.no_outer = jnp.logical_not(self.has_outer)
        self.is_hub = jnp.logical_or(me == mid - 1, me == mid)
        self.not_hub = jnp.logical_not(self.is_hub)
        self.mine = lax.axis_index("scany")

    def parts(self):
        inner = (self.upper, self.lower)
        return (
            lambda k: inner[k],
            lambda k: inner[1 - k],
            lambda k: jnp.logical_and(inner[k], self.not_hub),
            lambda k: jnp.logical_or(inner[1 - k], self.is_hub),
        )

    def at(self, c):
        return pl.ds(c * self.rows, self.rows)

    def copy(self, src, dst, s, r, c, where):
        return remote(src.at[self.at(c)], dst.at[self.at(c)], self.send.at[s, c], self.recv.at[r, c], where)

    def pair(self, c):
        return self.copy(self.prob.at[1 - self.q], self.ppair, 0, 0, c, self.partner)

    def inward(self, c):
        return self.copy(self.part, self.inner, 1, 1, c, self.to_inner)

    def across(self, c):
        return self.copy(self.part, self.hub, 1, 2, c, self.to_inner)

    def outward(self, c, src):
        return self.copy(src, self.hub, 2, 2, c, self.to_outer)

    def share(self, c, q):
        return self.copy(self.total.at[q], self.total.at[q], 3, 3, c, self.partner)

    def sides(self, c):
        out = []
        for d in range(1, self.ny):
            slot = self.held.at[self.mine]
            out.append(self.copy(slot, slot, 3 + d, 3 + d, c, {"scany": lax.rem(self.mine + d, self.ny)}))
        return out

    def side_arrive(self, c):
        for d in range(1, self.ny):
            slot = self.held.at[lax.rem(self.mine - d + self.ny, self.ny)]
            self.copy(slot, slot, 3 + d, 3 + d, c, self.partner).wait_recv()

    def side_sum(self, c):
        self.side_arrive(c)
        out = self.held[0, self.at(c)]
        for i in range(1, self.ny):
            out = out + self.held[i, self.at(c)]
        return out

    def pair_sum(self, c):
        self.pair(c).wait_recv()
        return self.prob[self.q, self.at(c)] + self.ppair[self.at(c)]

    def send_sides(self, c, value):
        self.held[self.mine, self.at(c)] = value
        for copy in self.sides(c):
            copy.start()

    def send_inward(self, c):
        when(self.not_hub)(self.inward(c).start)
        when(self.is_hub)(self.across(c).start)

    def collect(self):
        @pl.when(self.has_outer)
        def _():
            for c in range(self.chunks):
                self.inward(c).wait_recv()
                self.part[self.at(c)] = self.part[self.at(c)] + self.inner[self.at(c)]
                self.send_inward(c)

    def start_part(self, c, value):
        self.part[self.at(c)] = value
        when(self.no_outer)(functools.partial(self.send_inward, c))

    def from_hub(self, hubs, after, chunks=None):
        @pl.when(self.is_hub if hubs else self.not_hub)
        def _():
            for c in chunks or range(self.chunks):
                self.across(c).wait_recv()
                value = self.hub[self.at(c)]
                after(c, self.part[self.at(c)] + value if hubs else value)

    def finish(self, src):
        for c in range(self.chunks):
            self.pair(c).wait_send()
            self.inward(c).wait_send()
            when(self.has_outer)(self.outward(c, src).wait_send)
            self.share(c, self.q).wait_send()
            for copy in self.sides(c):
                copy.wait_send()


class SideFirst(ProbeSum):
    def one(self):
        for c in range(self.chunks):
            self.send_sides(c, self.pair_sum(c))

    def two(self):
        for c in range(self.chunks):
            self.start_part(c, self.side_sum(c))
        self.collect()

    def done(self, c, value):
        self.total[self.q, self.at(c)] = value
        when(self.has_outer)(self.outward(c, self.total.at[self.q]).start)
        self.share(c, self.q).start()

    def three(self, chunks=None):
        self.from_hub(True, self.done, chunks)

    def four(self):
        self.from_hub(False, self.done)

    def five(self):
        pass

    def end(self):
        self.finish(self.total.at[self.q])


class ChainFirst(ProbeSum):
    def one(self):
        for c in range(self.chunks):
            self.start_part(c, self.pair_sum(c))

    def two(self):
        self.collect()

    def done(self, c, value):
        self.send_sides(c, value)
        when(self.has_outer)(self.outward(c, self.held.at[self.mine]).start)

    def three(self, chunks=None):
        self.from_hub(True, self.done, chunks)

    def four(self):
        self.from_hub(False, self.done)

    def five(self):
        for c in range(self.chunks):
            self.total[self.q, self.at(c)] = self.side_sum(c)
            self.share(c, self.q).start()

    def end(self):
        self.finish(self.held.at[self.mine])


def near_greet(ny, partner, rows, cols):
    my = lax.axis_index("scany")
    greet(
        [(True, partner)]
        + [(True, {"scany": lax.rem(my + d, ny)}) for d in range(1, ny)]
        + [(side.has, side.where) for side in rows]
        + [(jnp.logical_and(a.has, b.has), {**a.where, **b.where}) for a in rows for b in cols]
    )


def each(step):
    p = lax.axis_index("pos")
    for q in range(2):
        pl.when(p == q)(functools.partial(step, q))


class Placer:
    def __init__(self, offsets, bufs, m, positions):
        self.bufs, self.m = bufs, m
        self.tall, self.span = m + 8, m + 128
        self.top = (bufs.shape[2] - self.tall // 8) // 2
        self.spots = []
        for j in range(positions):
            row, col = offsets[j, 0], offsets[j, 1]
            self.spots.append((lax.rem(row, 8), lax.rem(col, 128), lax.div(row, 8), lax.div(col, 128)))

    def clear(self):
        n, k, rows = self.bufs.shape[:3]
        bottom = self.top + self.tall // 8
        for j in range(n):
            for c in range(k):
                self.bufs[j, c, 0 : self.top] = jnp.zeros((self.top, *self.bufs.shape[3:]), jnp.float32)
                self.bufs[j, c, bottom:rows] = jnp.zeros((rows - bottom, *self.bufs.shape[3:]), jnp.float32)

    def put(self, j, k, term):
        row_in, col_in, _, step = self.spots[j]
        m, wide = self.m, self.bufs.shape[4]
        blank_rows = jnp.zeros((self.tall - m, m), jnp.float32)
        blank_cols = jnp.zeros((self.tall, self.span - m), jnp.float32)
        moved = pltpu.roll(jnp.concatenate([term, blank_rows], 0), row_in, 0)
        moved = pltpu.roll(jnp.concatenate([moved, blank_cols], 1), col_in, 1)
        out = None
        for d in range((wide - self.span) // 128 + 1):
            parts = [jnp.zeros((self.tall, w), jnp.float32) for w in (128 * d, wide - self.span - 128 * d)]
            here = jnp.concatenate([x for x in (parts[0], moved, parts[1]) if x.shape[1]], 1)
            out = here if out is None else jnp.where(step == d, here, out)
        self.bufs[j, k, self.top : self.top + self.tall // 8] = out.reshape(self.tall // 8, 8, wide)

    def rows(self, k, r0, count):
        out = None
        for j, (_, _, row, _) in enumerate(self.spots):
            part = self.bufs[j, k, pl.ds(self.top - row + r0 // 8, count // 8)]
            out = part if out is None else out + part
        return out.reshape(count, self.bufs.shape[4])

    def window(self, j, pad, k):
        row_in, col_in, row, step = self.spots[j]
        wide = pad.shape[3]
        block = pad[k, pl.ds(row, self.tall // 8)].reshape(self.tall, wide)
        out = block[:, : self.span]
        for d in range(1, (wide - self.span) // 128 + 1):
            out = jnp.where(step == d, block[:, 128 * d : 128 * d + self.span], out)
        out = pltpu.roll(out, lax.rem(self.span - col_in, self.span), 1)[:, : self.m]
        return pltpu.roll(out, lax.rem(self.tall - row_in, self.tall), 0)[: self.m]


def forward(window, pr, pi, table_a, table_b):
    m = pr.shape[0]
    bf = jnp.bfloat16
    ar, ai = window
    er = pr * ar - pi * ai
    ei = pr * ai + pi * ar
    left = dot(table_a[...], jnp.concatenate([er.astype(bf), ei.astype(bf)], 0)).astype(bf)
    return er, ei, dot(jnp.concatenate([left[:m], left[m:]], 1), table_b[...])


def backward(er, ei, far, amplitude, table_a, table_b):
    m = er.shape[0]
    bf = jnp.bfloat16
    fr, fi = far[:, :m], far[:, m:]
    ratio = amplitude.astype(jnp.float32) / jnp.maximum(jnp.sqrt(fr * fr + fi * fi), 0.2)
    projected = jnp.concatenate([(fr * ratio).astype(bf), (fi * ratio).astype(bf)], 0)
    back_half = dot(table_b[...], projected).astype(bf)
    back = dot(jnp.concatenate([back_half[:m], back_half[m:]], 1), table_a[...])
    return back[:, :m] - er, back[:, m:] - ei


def whole_kernel(nx, ny, step_size, *refs):
    offsets, spec, *given = refs[:6]
    new_spec, new_probe = refs[6:8]
    pad, probe, amplitudes, table_a, table_b, bufs, grad, prob, total, light_all = refs[8:18]
    pair, acc, xr1, xr2, zr1, zr2, ipair, iacc, ixr, izr, ppair, held, inner, hub, part = refs[18:33]
    hsend, hrecv, local, gsend, grecv, isend, irecv, psend, precv = refs[33:]
    tile, m = spec.shape[3], probe.shape[1]
    wide = pad.shape[3]
    half = (wide - tile) // 2
    h = grad.shape[3]
    positions, chunks = amplitudes.shape[0], psend.shape[1]
    p = lax.axis_index("pos")
    partner = {"pos": 1 - p}
    loads = [pltpu.make_async_copy(spec, pad.at[:, pl.ds(half // 8, tile // 8), :, pl.ds(half, tile)], local.at[0])]
    for i, (src, dst) in enumerate(zip(given, (probe, amplitudes, table_a, table_b)), 1):
        loads.append(pltpu.make_async_copy(src, dst, local.at[i]))
    for c in loads:
        c.start()
    roles = [Role(q, nx, ny) for q in range(2)]
    sides = roles[1].sides1 + roles[0].sides1
    near_greet(ny, partner, roles[1].sides1, roles[0].sides1)
    halos = [Halo(r, spec, pad, hsend, hrecv, partner) for r in roles]
    folds = [
        Fold(
            roles[q],
            roles[1 - q],
            grad.at[q],
            grad.at[1 - q],
            pair,
            acc,
            (zr1, xr1, zr2, xr2),
            None,
            gsend,
            grecv,
            partner,
        )
        for q in range(2)
    ]
    role = Role(p, nx, ny, 0)
    light = Fold(
        role,
        role,
        grad.at[2, :, pl.ds(p, 1)],
        grad.at[2, :, pl.ds(1 - p, 1)],
        ipair,
        iacc,
        (None, ixr, izr, None),
        light_all,
        isend,
        irecv,
        partner,
    )
    probes = [
        kind(q, nx, ny, prob, ppair, held, inner, hub, part, total, psend, precv, partner)
        for q, kind in enumerate((SideFirst, ChainFirst))
    ]
    placer = Placer(offsets, bufs, m, positions)

    def gather(k):
        for g in range(4):
            for b in range(2):
                grad[k, g, b] = placer.rows(k, (2 * g + b) * h, h)

    each(lambda q: halos[q].begin())
    for i, at in enumerate(
        (
            (slice(None), pl.ds(0, half // 8)),
            (slice(None), pl.ds((half + tile) // 8, half // 8)),
            (slice(None), slice(None), slice(None), pl.ds(0, half)),
            (slice(None), slice(None), slice(None), pl.ds(half + tile, half)),
        )
    ):

        @pl.when(jnp.logical_not(sides[i].has))
        def _(at=at):
            pad[at] = jnp.zeros(pad.at[at].shape, pad.dtype)

    placer.clear()
    loads[1].wait()
    power = probe[0] * probe[0] + probe[1] * probe[1]
    for j in range(positions):
        placer.put(j, 2, power)
    gather(2)
    light.begin()

    def strips(q):
        halos[q].relay()

    def corners(q):
        halos[q].relay_corners()
        halos[1 - q].arrive()

    each(strips)
    for i in range(3):
        light.add(i)
    light.send_rims(0)
    each(corners)
    for c in loads[:1] + loads[2:]:
        c.wait()
    pr, pi = probe[0], probe[1]
    windows = [[placer.window(j, pad, k) for k in range(2)] for j in range(positions)]
    fields = [forward(windows[j], pr, pi, table_a, table_b) for j in range(positions)]
    diffs = [backward(*fields[j], amplitudes[j], table_a, table_b) for j in range(positions)]
    sums = [None, None]
    for (ar, ai), (dr, di) in zip(windows, diffs):
        for k, t in enumerate((ar * dr + ai * di, ar * di - ai * dr)):
            sums[k] = t if sums[k] is None else sums[k] + t
    rows = m // chunks
    for c in range(chunks):
        at = pl.ds(c * rows, rows)
        for k in range(2):
            prob[k, at] = sums[k][c * rows : (c + 1) * rows]
        remote(prob.at[1 - p, at], ppair.at[at], psend.at[0, c], precv.at[0, c], partner).start()
    for j, (dr, di) in enumerate(diffs):
        placer.put(j, 0, pr * dr + pi * di)
        placer.put(j, 1, pr * di - pi * dr)
    gather(1 - p)
    each(lambda q: folds[q].begin())
    gather(p)

    def update(q):
        q4 = folds[q].q4
        for g in range(2):
            for b in range(2):
                r0 = (2 * g + b) * h
                old = pad[q, (half + r0) // 8 : (half + r0 + h) // 8, :, half : half + tile].reshape(h, tile)
                new_spec[q, r0 : r0 + h] = old + acc[1 + g, b, :, q4 : 3 * q4] / (light_all[b, g, 0] + 1.0)

    def share_copy(q):
        return remote(new_spec.at[q], new_spec.at[q], gsend.at[7], grecv.at[7], partner)

    def object_last(q):
        light.arrive()
        folds[q].fold(1)
        update(q)
        share_copy(q).start()

    def objects(q):
        probe_sum, fold = probes[q], folds[q]
        inward, outward, late, early = probe_sum.parts()
        probe_sum.one()
        fold.add(0)
        fold.add(1)
        if q == 0:
            fold.send_rims(0)
        else:
            fold.send_rims(0, early)
        light.fold(0)
        light.send_rims(1)
        fold.add(2)
        probe_sum.two()
        if q == 0:
            fold.fold(0)
            fold.send_rims(1)
            light.fold(1)
            light.share()
            probe_sum.three()
            object_last(q)
            probe_sum.four()
        else:
            probe_sum.three()
            fold.fold(0, inward)
            fold.send_rims(0, late)
            fold.fold(0, outward)
            fold.send_rims(1)
            light.fold(1)
            light.share()
            probe_sum.four()
            object_last(q)
            probe_sum.five()

    each(objects)

    def closing(q):
        for c in range(chunks):
            probes[q].share(c, 1 - q).wait_recv()
        share_copy(1 - q).wait_recv()
        share_copy(q).wait_send()
        light.finish()
        folds[q].finish()
        probes[q].end()
        halos[q].finish()

    each(closing)
    for k in range(2):
        new_probe[k] = probe[k] + total[k] * step_size


def emit_kernel(spec, probe, new_spec, new_probe, sem):
    copies = [
        pltpu.make_async_copy(src.at[k], dst.at[k], sem.at[i, k])
        for i, (src, dst) in enumerate(((spec, new_spec), (probe, new_probe)))
        for k in range(2)
    ]
    for c in copies:
        c.start()
    for c in copies:
        c.wait()


def tables(length):
    index = np.arange(length)
    angle = ((index[:, None] * index[None, :]) % length).astype(np.float32) * np.float32(2.0 * math.pi / length)
    scale = np.float32(1.0 / math.sqrt(length))
    c = np.cos(angle) * scale
    s = np.sin(angle) * scale
    a = np.block([[c, s], [-s, c]]).astype(jnp.bfloat16)
    b = np.block([[c, -s], [s, c]]).astype(jnp.bfloat16)
    return a, b


def shards(nx, ny, consts, specimen, probe_wave, amplitudes, offsets):
    m = probe_wave.shape[1]
    tile = specimen.shape[1]
    wide = tile + m
    f32 = jnp.float32
    vm = pl.BlockSpec(memory_space=VMEM)
    sm = pl.BlockSpec(memory_space=pltpu.SMEM)
    hbm = pl.BlockSpec(memory_space=pltpu.HBM)
    dma = pltpu.SemaphoreType.DMA
    n = nx * ny
    h = wide // 8
    chunks = 8
    positions = offsets.shape[0]
    held = (probe_wave, amplitudes, consts[0], consts[1])

    step_size = 1.0 / math.sqrt(positions * n * 2)
    results = pl.pallas_call(
        functools.partial(whole_kernel, nx, ny, step_size),
        out_shape=[VMEM(specimen.shape, f32), VMEM(probe_wave.shape, f32)],
        in_specs=[sm] + [hbm] * 5,
        out_specs=[vm, vm],
        scratch_shapes=[
            VMEM((2, wide // 8, 8, wide), f32),
            *[VMEM(x.shape, x.dtype) for x in held],
            VMEM((positions, 3, (2 * (tile - 8) + m + 8) // 8, 8, wide), f32),
            VMEM((3, 4, 2, h, wide), f32),
            VMEM((2, m, m), f32),
            VMEM((2, m, m), f32),
            VMEM((2, 2, 1, h, wide // 2), f32),
            VMEM((4, 2, h, wide), f32),
            VMEM((4, 2, h, wide), f32),
            VMEM((2, 4, 2, h, wide // 4), f32),
            VMEM((2, 2, 2, h, wide // 4), f32),
            VMEM((2, 2, h, wide), f32),
            VMEM((2, 2, h, wide // 2), f32),
            VMEM((4, 1, h, wide), f32),
            VMEM((4, 1, h, wide), f32),
            VMEM((2, 4, 1, h, wide // 4), f32),
            VMEM((2, 1, h, wide // 2), f32),
            VMEM((m, m), f32),
            VMEM((ny, m, m), f32),
            VMEM((m, m), f32),
            VMEM((m, m), f32),
            VMEM((m, m), f32),
            dma((20,)),
            dma((20,)),
            dma((5,)),
            dma((8,)),
            dma((8,)),
            dma((8,)),
            dma((8,)),
            dma((3 + ny, chunks)),
            dma((3 + ny, chunks)),
        ],
        compiler_params=pltpu.CompilerParams(vmem_limit_bytes=56 * 2**20, collective_id=0, has_side_effects=True),
        name="whole",
    )(offsets, *[pltpu.with_memory_space_constraint(x, pltpu.HBM) for x in (specimen.reshape(2, tile // 8, 8, tile), *held)])
    return pl.pallas_call(
        emit_kernel,
        out_shape=[jax.ShapeDtypeStruct(specimen.shape, f32), jax.ShapeDtypeStruct(probe_wave.shape, f32)],
        in_specs=[vm] * 2,
        out_specs=[pl.BlockSpec(memory_space=pl.ANY)] * 2,
        scratch_shapes=[dma((2, 2))],
        compiler_params=pltpu.CompilerParams(vmem_limit_bytes=2 * 2**20),
        name="emit",
    )(*results)


def solution(mesh):
    nx, ny = mesh.shape["scanx"], mesh.shape["scany"]

    def run(specimen, probe_wave, amplitudes, offsets):
        consts = tables(probe_wave.shape[2])
        return jax.shard_map(
            lambda *args: shards(nx, ny, [jnp.asarray(t) for t in consts], *args),
            mesh=mesh,
            in_specs=(
                P(None, ("groups", "scanx"), "scany"),
                P(None, "groups", None),
                P(("groups", "scanx", "scany", "pos"), None, None),
                P(("groups", "scanx", "scany", "pos"), None),
            ),
            out_specs=(P(None, ("groups", "scanx"), "scany"), P(None, "groups", None)),
            check_vma=False,
        )(specimen, probe_wave, amplitudes, offsets)

    return run
```

```python
import functools
import math

import jax
import jax.numpy as jnp
import numpy as np
from jax import lax
from jax.experimental import pallas as pl
from jax.experimental.pallas import tpu as pltpu
from jax.sharding import PartitionSpec as P

MESH = pl.DeviceIdType.MESH
VMEM = pltpu.VMEM


def remote(src, dst, send, recv, where):
    return pltpu.make_async_remote_copy(
        src_ref=src, dst_ref=dst, send_sem=send, recv_sem=recv, device_id=where, device_id_type=MESH
    )


def greet(conditions_devices):
    barrier = pltpu.get_barrier_semaphore()
    for present, where in conditions_devices:
        if present is True:
            pl.semaphore_signal(barrier, inc=1, device_id=where, device_id_type=MESH)
        else:

            @pl.when(present)
            def _(where=where):
                pl.semaphore_signal(barrier, inc=1, device_id=where, device_id_type=MESH)

    fixed = sum(1 for present, _ in conditions_devices if present is True)
    peers = [present.astype(jnp.int32) for present, _ in conditions_devices if present is not True]
    pl.semaphore_wait(barrier, sum(peers, fixed))


class Side:
    def __init__(self, axis, count, step):
        me = lax.axis_index(axis)
        self.has = me > 0 if step < 0 else me < count - 1
        self.where = {axis: me + step}


class Role:
    def __init__(self, q, nx, ny, order=None):
        order = q if order is None else order
        along_x = ("scanx", nx, Side("scanx", nx, -1), Side("scanx", nx, 1))
        along_y = ("scany", ny, Side("scany", ny, -1), Side("scany", ny, 1))
        one, two = (along_y, along_x) if order == 0 else (along_x, along_y)
        self.q, self.o, self.rows_first = q, 1 - q, order == 1
        self.axis1, self.n1, self.sides1 = one[0], one[1], one[2:]
        self.axis2, self.n2, self.sides2 = two[0], two[1], two[2:]
        self.me1, self.me2 = lax.axis_index(self.axis1), lax.axis_index(self.axis2)


def when(*conditions):
    return pl.when(functools.reduce(jnp.logical_and, [c for c in conditions if c is not True]))


def dot(a, b):
    return jnp.dot(a, b, preferred_element_type=jnp.float32)


class Halo:
    def __init__(self, role, spec, pad, send, recv, partner):
        self.r, self.spec, self.pad, self.partner = role, spec, pad, partner
        self.send, self.recv = send, recv
        self.direct = not role.rows_first
        tile = spec.shape[3]
        half = (pad.shape[3] - tile) // 2
        self.own = (half, tile)
        self.margins = ((0, half), (half + tile, half))
        self.edges = ((0, half), (tile - half, half))
        self.pad_edges = ((half, half), (tile, half))
        self.whole = (0, tile)

    def at(self, one, two):
        rows, cols = (one, two) if self.r.rows_first else (two, one)
        return (self.r.q, pl.ds(rows[0] // 8, rows[1] // 8), slice(None), pl.ds(*cols))

    def copy(self, src, dst, i, where):
        return remote(src, dst, self.send.at[i], self.recv.at[i], where)

    def strip1(self, m, e):
        return self.copy(
            self.spec.at[self.at(self.edges[1 - m], self.edges[e])],
            self.pad.at[self.at(self.margins[m], self.pad_edges[e])],
            2 * m + e,
            self.r.sides1[1 - m].where,
        )

    def strip2(self, m):
        return self.copy(
            self.spec.at[self.at(self.whole, self.edges[1 - m])],
            self.pad.at[self.at(self.own, self.margins[m])],
            4 + m,
            self.r.sides2[1 - m].where,
        )

    def corner(self, m1, m2):
        if self.direct:
            return self.copy(
                self.spec.at[self.at(self.edges[1 - m1], self.edges[1 - m2])],
                self.pad.at[self.at(self.margins[m1], self.margins[m2])],
                6 + 2 * m1 + m2,
                {**self.r.sides1[1 - m1].where, **self.r.sides2[1 - m2].where},
            )
        return self.copy(
            self.pad.at[self.at(self.margins[m1], self.pad_edges[1 - m2])],
            self.pad.at[self.at(self.margins[m1], self.margins[m2])],
            6 + 2 * m1 + m2,
            self.r.sides2[1 - m2].where,
        )

    def share(self, i, one, two):
        ref = self.pad.at[self.at(one, two)]
        return self.copy(ref, ref, 10 + i, self.partner)

    def share1(self, m, e):
        return self.share(2 * m + e, self.margins[m], self.pad_edges[e])

    def share2(self, m):
        return self.share(4 + m, self.own, self.margins[m])

    def share_corner(self, m1, m2):
        return self.share(6 + 2 * m1 + m2, self.margins[m1], self.margins[m2])

    def begin(self):
        r = self.r
        if self.direct:
            for m1 in range(2):
                for m2 in range(2):
                    when(r.sides1[1 - m1].has, r.sides2[1 - m2].has)(self.corner(m1, m2).start)
        for m in range(2):
            for e in range(2):
                when(r.sides1[1 - m].has, r.sides2[e].has)(self.strip1(m, e).start)
        for m in range(2):
            when(r.sides2[1 - m].has)(self.strip2(m).start)
        for m in range(2):
            for e in range(2):
                when(r.sides1[1 - m].has, jnp.logical_not(r.sides2[e].has))(self.strip1(m, e).start)

    def relay(self):
        r = self.r
        for m1 in range(2):
            for e in range(2):

                @when(r.sides1[m1].has, r.sides2[e].has)
                def _():
                    self.strip1(m1, e).wait_recv()
                    if not self.direct:
                        self.corner(m1, 1 - e).start()
                    self.share1(m1, e).start()

        for m in range(2):

            @when(r.sides2[m].has)
            def _():
                self.strip2(m).wait_recv()
                self.share2(m).start()

        for m1 in range(2):
            for e in range(2):

                @when(r.sides1[m1].has, jnp.logical_not(r.sides2[e].has))
                def _():
                    self.strip1(m1, e).wait_recv()
                    self.share1(m1, e).start()

    def relay_corners(self):
        r = self.r
        for m1 in range(2):
            for m2 in range(2):

                @when(r.sides1[m1].has, r.sides2[m2].has)
                def _():
                    self.corner(m1, m2).wait_recv()
                    self.share_corner(m1, m2).start()

    def arrive(self):
        r = self.r
        for m in range(2):
            for e in range(2):
                when(r.sides1[m].has)(self.share1(m, e).wait_recv)
            when(r.sides2[m].has)(self.share2(m).wait_recv)
        for m1 in range(2):
            for m2 in range(2):
                when(r.sides1[m1].has, r.sides2[m2].has)(self.share_corner(m1, m2).wait_recv)

    def finish(self):
        r = self.r
        for m in range(2):
            for e in range(2):
                when(r.sides1[1 - m].has)(self.strip1(m, e).wait_send)
                when(r.sides1[m].has)(self.share1(m, e).wait_send)
            when(r.sides2[1 - m].has)(self.strip2(m).wait_send)
            when(r.sides2[m].has)(self.share2(m).wait_send)
        for m1 in range(2):
            for m2 in range(2):
                sent = r.sides1[1 - m1].has if self.direct else r.sides1[m1].has
                when(sent, r.sides2[1 - m2].has)(self.corner(m1, m2).wait_send)
                when(r.sides1[m1].has, r.sides2[m2].has)(self.share_corner(m1, m2).wait_send)


class Fold:
    def __init__(self, role, other, mine, theirs, pair, acc, rims, core, send, recv, partner):
        self.r, self.other, self.mine, self.theirs, self.pair, self.acc = role, other, mine, theirs, pair, acc
        self.rows1, self.cols1, self.rows2, self.cols2 = rims
        self.core, self.send, self.recv, self.partner = core, send, recv, partner
        w = acc.shape[-1]
        self.w, self.q4 = w, w // 4

    def piece(self, i, r):
        q4, cols = self.q4, (slice(None),) * 3
        if r.rows_first:
            return ((pl.ds(0, 1),), (pl.ds(3, 1),), (pl.ds(1, 2),))[i]
        return cols + ((pl.ds(0, q4),), (pl.ds(3 * q4, q4),), (pl.ds(q4, 2 * q4),))[i]

    def needed(self, i, r):
        return pl.when(r.sides1[i].has) if i < 2 else lambda f: f()

    def pair_copy(self, i, r):
        at = self.piece(i, r)
        return remote(self.theirs.at[at], self.pair.at[at], self.send.at[i], self.recv.at[i], self.partner)

    def begin(self):
        for i in range(3):
            self.needed(i, self.other)(self.pair_copy(i, self.other).start)

    def add(self, i):
        @self.needed(i, self.r)
        def _():
            self.pair_copy(i, self.r).wait_recv()
            at = self.piece(i, self.r)
            self.acc[at] = self.mine[at] + self.pair[at]

    def spot(self, stage, i, m):
        r, q4, w = self.r, self.q4, self.w
        if r.rows_first == (stage == 0):
            if stage == 1:
                return (i, slice(None), slice(None), pl.ds(q4, 2 * q4)), self.rows2.at[m]
            cols = pl.ds(0, w)
            if r.n2 == 2:
                cols = pl.ds(pl.multiple_of((1 - r.me2) * q4, q4), 3 * q4)
            return (i, slice(None), slice(None), cols), self.rows1.at[m, :, :, cols]
        groups = pl.ds(0, 4) if stage == 0 else pl.ds(1, 2)
        return (groups, slice(None), slice(None), pl.ds(i * q4, q4)), (self.cols1 if stage == 0 else self.cols2).at[m]

    def rim_copy(self, stage, m):
        sides = self.r.sides1 if stage == 0 else self.r.sides2
        at, rim = self.spot(stage, 3 * (1 - m), m)
        i = 3 + 2 * stage + m
        return remote(self.acc.at[at], rim, self.send.at[i], self.recv.at[i], sides[1 - m].where)

    def send_rims(self, stage, only=lambda k: True):
        sides = self.r.sides1 if stage == 0 else self.r.sides2
        for m in range(2):
            when(sides[1 - m].has, only(1 - m))(self.rim_copy(stage, m).start)

    def fold(self, stage, only=lambda k: True):
        sides = self.r.sides1 if stage == 0 else self.r.sides2
        for m in range(2):

            @when(sides[m].has, only(m))
            def _():
                self.rim_copy(stage, m).wait_recv()
                at, rim = self.spot(stage, 1 + m, m)
                self.acc[at] = self.acc[at] + rim[...]

    def share_copy(self, q):
        return remote(self.core.at[q], self.core.at[q], self.send.at[7], self.recv.at[7], self.partner)

    def share(self):
        q4 = self.q4
        self.core[self.r.q] = self.acc[1:3, :, :, q4 : 3 * q4]
        self.share_copy(self.r.q).start()

    def arrive(self):
        self.share_copy(self.r.o).wait_recv()

    def finish(self):
        r = self.r
        for i in range(3):
            self.needed(i, self.other)(self.pair_copy(i, self.other).wait_send)
        for m in range(2):
            when(r.sides1[1 - m].has)(self.rim_copy(0, m).wait_send)
            when(r.sides2[1 - m].has)(self.rim_copy(1, m).wait_send)
        if self.core is not None:
            self.share_copy(r.q).wait_send()


class ProbeSum:
    def __init__(self, q, nx, ny, prob, ppair, held, inner, hub, part, total, send, recv, partner):
        self.q, self.ny = q, ny
        self.prob, self.ppair, self.held = prob, ppair, held
        self.inner, self.hub, self.part, self.total = inner, hub, part, total
        self.send, self.recv, self.partner = send, recv, partner
        self.chunks = recv.shape[1]
        self.rows = prob.shape[1] // self.chunks
        me, mid = lax.axis_index("scanx"), nx // 2
        self.lower, self.upper = me < mid, me >= mid
        step = 2 * self.lower.astype(jnp.int32) - 1
        self.to_inner, self.to_outer = {"scanx": me + step}, {"scanx": me - step}
        self.has_outer = jnp.logical_and(me > 0, me < nx - 1)
        self.no_outer = jnp.logical_not(self.has_outer)
        self.is_hub = jnp.logical_or(me == mid - 1, me == mid)
        self.not_hub = jnp.logical_not(self.is_hub)
        self.mine = lax.axis_index("scany")

    def parts(self):
        inner = (self.upper, self.lower)
        return (
            lambda k: inner[k],
            lambda k: inner[1 - k],
            lambda k: jnp.logical_and(inner[k], self.not_hub),
            lambda k: jnp.logical_and(inner[k], self.is_hub),
        )

    def at(self, c):
        return pl.ds(c * self.rows, self.rows)

    def copy(self, src, dst, s, r, c, where):
        return remote(src.at[self.at(c)], dst.at[self.at(c)], self.send.at[s], self.recv.at[r, c], where)

    def pair(self, c):
        return self.copy(self.prob.at[1 - self.q], self.ppair, 0, 0, c, self.partner)

    def inward(self, c):
        return self.copy(self.part, self.inner, 1, 1, c, self.to_inner)

    def across(self, c):
        return self.copy(self.part, self.hub, 1, 2, c, self.to_inner)

    def outward(self, c, src):
        return self.copy(src, self.hub, 2, 2, c, self.to_outer)

    def share(self, c, q):
        return self.copy(self.total.at[q], self.total.at[q], 3, 3, c, self.partner)

    def sides(self, c):
        out = []
        for d in range(1, self.ny):
            slot = self.held.at[self.mine]
            out.append(self.copy(slot, slot, 3 + d, 3 + d, c, {"scany": lax.rem(self.mine + d, self.ny)}))
        return out

    def side_arrive(self, c):
        for d in range(1, self.ny):
            slot = self.held.at[lax.rem(self.mine - d + self.ny, self.ny)]
            self.copy(slot, slot, 3 + d, 3 + d, c, self.partner).wait_recv()

    def side_sum(self, c):
        self.side_arrive(c)
        out = self.held[0, self.at(c)]
        for i in range(1, self.ny):
            out = out + self.held[i, self.at(c)]
        return out

    def pair_sum(self, c):
        self.pair(c).wait_recv()
        return self.prob[self.q, self.at(c)] + self.ppair[self.at(c)]

    def send_sides(self, c, value):
        self.held[self.mine, self.at(c)] = value
        for copy in self.sides(c):
            copy.start()

    def send_inward(self, c):
        when(self.not_hub)(self.inward(c).start)
        when(self.is_hub)(self.across(c).start)

    def collect(self):
        @pl.when(self.has_outer)
        def _():
            for c in range(self.chunks):
                self.inward(c).wait_recv()
                self.part[self.at(c)] = self.part[self.at(c)] + self.inner[self.at(c)]
                self.send_inward(c)

    def start_part(self, c, value):
        self.part[self.at(c)] = value
        when(self.no_outer)(functools.partial(self.send_inward, c))

    def from_hub(self, hubs, after, chunks=None):
        @pl.when(self.is_hub if hubs else self.not_hub)
        def _():
            for c in chunks or range(self.chunks):
                self.across(c).wait_recv()
                value = self.hub[self.at(c)]
                after(c, self.part[self.at(c)] + value if hubs else value)

    def finish(self):
        def sent(stage):
            remote(self.part, self.hub, self.send.at[stage], self.recv.at[2, 0], self.partner).wait_send()

        sent(0)
        sent(1)
        pl.when(self.has_outer)(functools.partial(sent, 2))
        for stage in range(3, 3 + self.ny):
            sent(stage)


class SideFirst(ProbeSum):
    def one(self):
        for c in range(self.chunks):
            self.send_sides(c, self.pair_sum(c))

    def two(self):
        for c in range(self.chunks):
            self.start_part(c, self.side_sum(c))
        self.collect()

    def done(self, c, value):
        self.total[self.q, self.at(c)] = value
        when(self.has_outer)(self.outward(c, self.total.at[self.q]).start)
        self.share(c, self.q).start()

    def three(self, chunks=None):
        self.from_hub(True, self.done, chunks)

    def four(self):
        self.from_hub(False, self.done)

    def five(self):
        pass

    def end(self):
        self.finish()


class ChainFirst(ProbeSum):
    def one(self):
        for c in range(self.chunks):
            self.start_part(c, self.pair_sum(c))

    def two(self):
        self.collect()

    def done(self, c, value):
        self.send_sides(c, value)
        when(self.has_outer)(self.outward(c, self.held.at[self.mine]).start)

    def three(self, chunks=None):
        self.from_hub(True, self.done, chunks)

    def four(self):
        self.from_hub(False, self.done)

    def five(self):
        for c in range(self.chunks):
            self.total[self.q, self.at(c)] = self.side_sum(c)
            self.share(c, self.q).start()

    def end(self):
        self.finish()


def near_greet(ny, partner, rows, cols):
    my = lax.axis_index("scany")
    greet(
        [(True, partner)]
        + [(True, {"scany": lax.rem(my + d, ny)}) for d in range(1, ny)]
        + [(side.has, side.where) for side in rows]
        + [(jnp.logical_and(a.has, b.has), {**a.where, **b.where}) for a in rows for b in cols]
    )


def each(step):
    p = lax.axis_index("pos")
    for q in range(2):
        pl.when(p == q)(functools.partial(step, q))


class Placer:
    def __init__(self, offsets, bufs, m, positions):
        self.bufs, self.m = bufs, m
        self.tall, self.span = m + 8, m + 128
        self.top = (bufs.shape[2] - self.tall // 8) // 2
        self.spots = []
        for j in range(positions):
            row, col = offsets[j, 0], offsets[j, 1]
            self.spots.append((lax.rem(row, 8), lax.rem(col, 128), lax.div(row, 8), lax.div(col, 128)))

    def clear(self):
        n, k, rows = self.bufs.shape[:3]
        bottom = self.top + self.tall // 8
        for j in range(n):
            for c in range(k):
                self.bufs[j, c, 0 : self.top] = jnp.zeros((self.top, *self.bufs.shape[3:]), jnp.float32)
                self.bufs[j, c, bottom:rows] = jnp.zeros((rows - bottom, *self.bufs.shape[3:]), jnp.float32)

    def put(self, j, k, term):
        row_in, col_in, _, step = self.spots[j]
        m, wide = self.m, self.bufs.shape[4]
        blank_rows = jnp.zeros((self.tall - m, m), jnp.float32)
        blank_cols = jnp.zeros((self.tall, self.span - m), jnp.float32)
        moved = pltpu.roll(jnp.concatenate([term, blank_rows], 0), row_in, 0)
        moved = pltpu.roll(jnp.concatenate([moved, blank_cols], 1), col_in, 1)
        out = None
        for d in range((wide - self.span) // 128 + 1):
            parts = [jnp.zeros((self.tall, w), jnp.float32) for w in (128 * d, wide - self.span - 128 * d)]
            here = jnp.concatenate([x for x in (parts[0], moved, parts[1]) if x.shape[1]], 1)
            out = here if out is None else jnp.where(step == d, here, out)
        self.bufs[j, k, self.top : self.top + self.tall // 8] = out.reshape(self.tall // 8, 8, wide)

    def rows(self, k, r0, count):
        out = None
        for j, (_, _, row, _) in enumerate(self.spots):
            part = self.bufs[j, k, pl.ds(self.top - row + r0 // 8, count // 8)]
            out = part if out is None else out + part
        return out.reshape(count, self.bufs.shape[4])

    def window(self, j, pad, k):
        row_in, col_in, row, step = self.spots[j]
        wide = pad.shape[3]
        block = pad[k, pl.ds(row, self.tall // 8)].reshape(self.tall, wide)
        out = block[:, : self.span]
        for d in range(1, (wide - self.span) // 128 + 1):
            out = jnp.where(step == d, block[:, 128 * d : 128 * d + self.span], out)
        out = pltpu.roll(out, lax.rem(self.span - col_in, self.span), 1)[:, : self.m]
        return pltpu.roll(out, lax.rem(self.tall - row_in, self.tall), 0)[: self.m]


def forward(window, pr, pi, table_a, table_b):
    m = pr.shape[0]
    bf = jnp.bfloat16
    ar, ai = window
    er = pr * ar - pi * ai
    ei = pr * ai + pi * ar
    left = dot(table_a[...], jnp.concatenate([er.astype(bf), ei.astype(bf)], 0)).astype(bf)
    return er, ei, dot(jnp.concatenate([left[:m], left[m:]], 1), table_b[...])


def backward(er, ei, far, amplitude, table_a, table_b):
    m = er.shape[0]
    bf = jnp.bfloat16
    fr, fi = far[:, :m], far[:, m:]
    ratio = amplitude.astype(jnp.float32) / jnp.maximum(jnp.sqrt(fr * fr + fi * fi), 0.2)
    projected = jnp.concatenate([(fr * ratio).astype(bf), (fi * ratio).astype(bf)], 0)
    back_half = dot(table_b[...], projected).astype(bf)
    back = dot(jnp.concatenate([back_half[:m], back_half[m:]], 1), table_a[...])
    return back[:, :m] - er, back[:, m:] - ei


def whole_kernel(nx, ny, step_size, *refs):
    offsets, spec, *given = refs[:6]
    new_spec, new_probe = refs[6:8]
    pad, probe, amplitudes, table_a, table_b, bufs, grad, prob, total, light_all = refs[8:18]
    pair, acc, xr1, xr2, zr1, zr2, ipair, iacc, ixr, izr, ppair, held, inner, hub, part = refs[18:33]
    hsend, hrecv, local, gsend, grecv, isend, irecv, psend, precv = refs[33:]
    tile, m = spec.shape[3], probe.shape[1]
    wide = pad.shape[3]
    half = (wide - tile) // 2
    h = grad.shape[3]
    positions, chunks = amplitudes.shape[0], precv.shape[1]
    p = lax.axis_index("pos")
    partner = {"pos": 1 - p}
    loads = [pltpu.make_async_copy(spec, pad.at[:, pl.ds(half // 8, tile // 8), :, pl.ds(half, tile)], local.at[0])]
    for i, (src, dst) in enumerate(zip(given, (probe, amplitudes, table_a, table_b)), 1):
        loads.append(pltpu.make_async_copy(src, dst, local.at[i]))
    for c in loads:
        c.start()
    roles = [Role(q, nx, ny) for q in range(2)]
    sides = roles[1].sides1 + roles[0].sides1
    near_greet(ny, partner, roles[1].sides1, roles[0].sides1)
    halos = [Halo(r, spec, pad, hsend, hrecv, partner) for r in roles]
    folds = [
        Fold(
            roles[q],
            roles[1 - q],
            grad.at[q],
            grad.at[1 - q],
            pair,
            acc,
            (zr1, xr1, zr2, xr2),
            None,
            gsend,
            grecv,
            partner,
        )
        for q in range(2)
    ]
    role = Role(p, nx, ny, 1)
    light = Fold(
        role,
        role,
        grad.at[2, :, pl.ds(p, 1)],
        grad.at[2, :, pl.ds(1 - p, 1)],
        ipair,
        iacc,
        (izr, None, None, ixr),
        light_all,
        isend,
        irecv,
        partner,
    )
    probes = [
        kind(q, nx, ny, prob, ppair, held, inner, hub, part, total, psend, precv, partner)
        for q, kind in enumerate((SideFirst, ChainFirst))
    ]
    placer = Placer(offsets, bufs, m, positions)

    def gather(k):
        for g in range(4):
            for b in range(2):
                grad[k, g, b] = placer.rows(k, (2 * g + b) * h, h)

    each(lambda q: halos[q].begin())
    for i, at in enumerate(
        (
            (slice(None), pl.ds(0, half // 8)),
            (slice(None), pl.ds((half + tile) // 8, half // 8)),
            (slice(None), slice(None), slice(None), pl.ds(0, half)),
            (slice(None), slice(None), slice(None), pl.ds(half + tile, half)),
        )
    ):

        @pl.when(jnp.logical_not(sides[i].has))
        def _(at=at):
            pad[at] = jnp.zeros(pad.at[at].shape, pad.dtype)

    placer.clear()
    loads[1].wait()
    power = probe[0] * probe[0] + probe[1] * probe[1]
    for j in range(positions):
        placer.put(j, 2, power)
    gather(2)
    light.begin()

    def strips(q):
        halos[q].relay()

    def corners(q):
        halos[q].relay_corners()
        halos[1 - q].arrive()

    for i in range(3):
        light.add(i)
    light.send_rims(0)
    each(strips)
    each(corners)
    for c in loads[:1] + loads[2:]:
        c.wait()
    pr, pi = probe[0], probe[1]
    windows = [[placer.window(j, pad, k) for k in range(2)] for j in range(positions)]
    fields = [forward(windows[j], pr, pi, table_a, table_b) for j in range(positions)]
    light.fold(0)
    light.send_rims(1)
    diffs = [backward(*fields[j], amplitudes[j], table_a, table_b) for j in range(positions)]
    sums = [None, None]
    for (ar, ai), (dr, di) in zip(windows, diffs):
        for k, t in enumerate((ar * dr + ai * di, ar * di - ai * dr)):
            sums[k] = t if sums[k] is None else sums[k] + t
    rows = m // chunks
    for c in range(chunks):
        at = pl.ds(c * rows, rows)
        for k in range(2):
            prob[k, at] = sums[k][c * rows : (c + 1) * rows]
        remote(prob.at[1 - p, at], ppair.at[at], psend.at[0], precv.at[0, c], partner).start()
    for j, (dr, di) in enumerate(diffs):
        placer.put(j, 0, pr * dr + pi * di)
        placer.put(j, 1, pr * di - pi * dr)
    gather(1 - p)
    each(lambda q: folds[q].begin())
    gather(p)

    def update(q):
        q4 = folds[q].q4
        for g in range(2):
            for b in range(2):
                r0 = (2 * g + b) * h
                old = pad[q, (half + r0) // 8 : (half + r0 + h) // 8, :, half : half + tile].reshape(h, tile)
                new_spec[q, r0 : r0 + h] = old + acc[1 + g, b, :, q4 : 3 * q4] / (light_all[b, g, 0] + 1.0)

    def share_copy(q):
        return remote(new_spec.at[q], new_spec.at[q], gsend.at[7], grecv.at[7], partner)

    def object_last(q):
        light.arrive()
        folds[q].fold(1)
        update(q)
        share_copy(q).start()

    def objects(q):
        probe_sum, fold = probes[q], folds[q]
        inward, outward, late, middle = probe_sum.parts()
        probe_sum.one()
        fold.add(0)
        fold.add(1)
        if q == 0:
            fold.send_rims(0)
        else:
            fold.send_rims(0, outward)
        fold.add(2)
        light.fold(1)
        light.share()
        probe_sum.two()
        if q == 0:
            fold.fold(0)
            fold.send_rims(1)
            probe_sum.three()
            object_last(q)
            probe_sum.four()
        else:
            fold.send_rims(0, middle)
            probe_sum.three()
            fold.fold(0, inward)
            fold.send_rims(0, late)
            fold.fold(0, outward)
            fold.send_rims(1)
            probe_sum.four()
            object_last(q)
            probe_sum.five()

    each(objects)

    def closing(q):
        for c in range(chunks):
            probes[q].share(c, 1 - q).wait_recv()
        share_copy(1 - q).wait_recv()
        share_copy(q).wait_send()
        light.finish()
        folds[q].finish()
        probes[q].end()
        halos[q].finish()

    each(closing)
    for k in range(2):
        new_probe[k] = probe[k] + total[k] * step_size


def emit_kernel(spec, probe, new_spec, new_probe, sem):
    copies = [
        pltpu.make_async_copy(src.at[k, at], dst.at[k, at], sem.at[i, k, j])
        for i, (src, dst) in enumerate(((spec, new_spec), (probe, new_probe)))
        for k in range(2)
        for j, at in enumerate((pl.ds(0, src.shape[1] // 2), pl.ds(src.shape[1] // 2, src.shape[1] // 2)))
    ]
    for c in copies:
        c.start()
    for c in copies:
        c.wait()


def tables(length):
    index = np.arange(length)
    angle = ((index[:, None] * index[None, :]) % length).astype(np.float32) * np.float32(2.0 * math.pi / length)
    scale = np.float32(1.0 / math.sqrt(length))
    c = np.cos(angle) * scale
    s = np.sin(angle) * scale
    a = np.block([[c, s], [-s, c]]).astype(jnp.bfloat16)
    b = np.block([[c, -s], [s, c]]).astype(jnp.bfloat16)
    return a, b


def shards(nx, ny, consts, specimen, probe_wave, amplitudes, offsets):
    m = probe_wave.shape[1]
    tile = specimen.shape[1]
    wide = tile + m
    f32 = jnp.float32
    vm = pl.BlockSpec(memory_space=VMEM)
    sm = pl.BlockSpec(memory_space=pltpu.SMEM)
    hbm = pl.BlockSpec(memory_space=pltpu.HBM)
    dma = pltpu.SemaphoreType.DMA
    n = nx * ny
    h = wide // 8
    chunks = 8
    positions = offsets.shape[0]
    held = (probe_wave, amplitudes, consts[0], consts[1])

    step_size = 1.0 / math.sqrt(positions * n * 2)
    results = pl.pallas_call(
        functools.partial(whole_kernel, nx, ny, step_size),
        out_shape=[VMEM(specimen.shape, f32), VMEM(probe_wave.shape, f32)],
        in_specs=[sm] + [hbm] * 5,
        out_specs=[vm, vm],
        scratch_shapes=[
            VMEM((2, wide // 8, 8, wide), f32),
            *[VMEM(x.shape, x.dtype) for x in held],
            VMEM((positions, 3, (2 * (tile - 8) + m + 8) // 8, 8, wide), f32),
            VMEM((3, 4, 2, h, wide), f32),
            VMEM((2, m, m), f32),
            VMEM((2, m, m), f32),
            VMEM((2, 2, 1, h, wide // 2), f32),
            VMEM((4, 2, h, wide), f32),
            VMEM((4, 2, h, wide), f32),
            VMEM((2, 4, 2, h, wide // 4), f32),
            VMEM((2, 2, 2, h, wide // 4), f32),
            VMEM((2, 2, h, wide), f32),
            VMEM((2, 2, h, wide // 2), f32),
            VMEM((4, 1, h, wide), f32),
            VMEM((4, 1, h, wide), f32),
            VMEM((2, 2, 1, h, wide // 4), f32),
            VMEM((2, 1, h, wide), f32),
            VMEM((m, m), f32),
            VMEM((ny, m, m), f32),
            VMEM((m, m), f32),
            VMEM((m, m), f32),
            VMEM((m, m), f32),
            dma((20,)),
            dma((20,)),
            dma((5,)),
            dma((8,)),
            dma((8,)),
            dma((8,)),
            dma((8,)),
            dma((3 + ny,)),
            dma((3 + ny, chunks)),
        ],
        compiler_params=pltpu.CompilerParams(vmem_limit_bytes=56 * 2**20, collective_id=0, has_side_effects=True),
        name="whole",
    )(offsets, *[pltpu.with_memory_space_constraint(x, pltpu.HBM) for x in (specimen.reshape(2, tile // 8, 8, tile), *held)])
    return pl.pallas_call(
        emit_kernel,
        out_shape=[jax.ShapeDtypeStruct(specimen.shape, f32), jax.ShapeDtypeStruct(probe_wave.shape, f32)],
        in_specs=[vm] * 2,
        out_specs=[pl.BlockSpec(memory_space=pl.ANY)] * 2,
        scratch_shapes=[dma((2, 2, 2))],
        compiler_params=pltpu.CompilerParams(vmem_limit_bytes=2 * 2**20),
        name="emit",
    )(*results)


def solution(mesh):
    nx, ny = mesh.shape["scanx"], mesh.shape["scany"]

    def run(specimen, probe_wave, amplitudes, offsets):
        consts = tables(probe_wave.shape[2])
        return jax.shard_map(
            lambda *args: shards(nx, ny, [jnp.asarray(t) for t in consts], *args),
            mesh=mesh,
            in_specs=(
                P(None, ("groups", "scanx"), "scany"),
                P(None, "groups", None),
                P(("groups", "scanx", "scany", "pos"), None, None),
                P(("groups", "scanx", "scany", "pos"), None),
            ),
            out_specs=(P(None, ("groups", "scanx"), "scany"), P(None, "groups", None)),
            check_vma=False,
        )(specimen, probe_wave, amplitudes, offsets)

    return run
```

```python
import functools
import math

import jax
import jax.numpy as jnp
import numpy as np
from jax import lax
from jax.experimental import pallas as pl
from jax.experimental.pallas import tpu as pltpu
from jax.sharding import PartitionSpec as P

MESH = pl.DeviceIdType.MESH
VMEM = pltpu.VMEM


def remote(src, dst, send, recv, where):
    return pltpu.make_async_remote_copy(
        src_ref=src, dst_ref=dst, send_sem=send, recv_sem=recv, device_id=where, device_id_type=MESH
    )


def greet(conditions_devices):
    barrier = pltpu.get_barrier_semaphore()
    for present, where in conditions_devices:
        if present is True:
            pl.semaphore_signal(barrier, inc=1, device_id=where, device_id_type=MESH)
        else:

            @pl.when(present)
            def _(where=where):
                pl.semaphore_signal(barrier, inc=1, device_id=where, device_id_type=MESH)

    fixed = sum(1 for present, _ in conditions_devices if present is True)
    peers = [present.astype(jnp.int32) for present, _ in conditions_devices if present is not True]
    pl.semaphore_wait(barrier, sum(peers, fixed))


class Side:
    def __init__(self, axis, count, step):
        me = lax.axis_index(axis)
        self.has = me > 0 if step < 0 else me < count - 1
        self.where = {axis: me + step}


class Role:
    def __init__(self, q, nx, ny, order=None):
        order = q if order is None else order
        along_x = ("scanx", nx, Side("scanx", nx, -1), Side("scanx", nx, 1))
        along_y = ("scany", ny, Side("scany", ny, -1), Side("scany", ny, 1))
        one, two = (along_y, along_x) if order == 0 else (along_x, along_y)
        self.q, self.o, self.rows_first = q, 1 - q, order == 1
        self.axis1, self.n1, self.sides1 = one[0], one[1], one[2:]
        self.axis2, self.n2, self.sides2 = two[0], two[1], two[2:]
        self.me1, self.me2 = lax.axis_index(self.axis1), lax.axis_index(self.axis2)


def when(*conditions):
    return pl.when(functools.reduce(jnp.logical_and, [c for c in conditions if c is not True]))


def dot(a, b):
    return jnp.dot(a, b, preferred_element_type=jnp.float32)


class Halo:
    def __init__(self, role, spec, pad, send, recv, partner):
        self.r, self.spec, self.pad, self.partner = role, spec, pad, partner
        self.send, self.recv = send, recv
        self.direct = not role.rows_first
        tile = spec.shape[3]
        half = (pad.shape[3] - tile) // 2
        self.own = (half, tile)
        self.margins = ((0, half), (half + tile, half))
        self.edges = ((0, half), (tile - half, half))
        self.pad_edges = ((half, half), (tile, half))
        self.whole = (0, tile)

    def at(self, one, two):
        rows, cols = (one, two) if self.r.rows_first else (two, one)
        return (self.r.q, pl.ds(rows[0] // 8, rows[1] // 8), slice(None), pl.ds(*cols))

    def copy(self, src, dst, i, where):
        return remote(src, dst, self.send.at[i], self.recv.at[i], where)

    def strip1(self, m, e):
        return self.copy(
            self.spec.at[self.at(self.edges[1 - m], self.edges[e])],
            self.pad.at[self.at(self.margins[m], self.pad_edges[e])],
            2 * m + e,
            self.r.sides1[1 - m].where,
        )

    def strip2(self, m):
        return self.copy(
            self.spec.at[self.at(self.whole, self.edges[1 - m])],
            self.pad.at[self.at(self.own, self.margins[m])],
            4 + m,
            self.r.sides2[1 - m].where,
        )

    def corner(self, m1, m2):
        if self.direct:
            return self.copy(
                self.spec.at[self.at(self.edges[1 - m1], self.edges[1 - m2])],
                self.pad.at[self.at(self.margins[m1], self.margins[m2])],
                6 + 2 * m1 + m2,
                {**self.r.sides1[1 - m1].where, **self.r.sides2[1 - m2].where},
            )
        return self.copy(
            self.pad.at[self.at(self.margins[m1], self.pad_edges[1 - m2])],
            self.pad.at[self.at(self.margins[m1], self.margins[m2])],
            6 + 2 * m1 + m2,
            self.r.sides2[1 - m2].where,
        )

    def share(self, i, one, two):
        ref = self.pad.at[self.at(one, two)]
        return self.copy(ref, ref, 10 + i, self.partner)

    def share1(self, m, e):
        return self.share(2 * m + e, self.margins[m], self.pad_edges[e])

    def share2(self, m):
        return self.share(4 + m, self.own, self.margins[m])

    def share_corner(self, m1, m2):
        return self.share(6 + 2 * m1 + m2, self.margins[m1], self.margins[m2])

    def begin(self):
        r = self.r
        for m in range(2):
            for e in range(2):
                when(r.sides1[1 - m].has, r.sides2[e].has)(self.strip1(m, e).start)
        for m in range(2):
            when(r.sides2[1 - m].has)(self.strip2(m).start)
        for m in range(2):
            for e in range(2):
                when(r.sides1[1 - m].has, jnp.logical_not(r.sides2[e].has))(self.strip1(m, e).start)

    def begin_corners(self):
        r = self.r
        for m1 in range(2):
            for m2 in range(2):
                when(r.sides1[1 - m1].has, r.sides2[1 - m2].has)(self.corner(m1, m2).start)

    def relay(self):
        r = self.r
        for m1 in range(2):
            for e in range(2):

                @when(r.sides1[m1].has, r.sides2[e].has)
                def _():
                    self.strip1(m1, e).wait_recv()
                    if not self.direct:
                        self.corner(m1, 1 - e).start()
                    self.share1(m1, e).start()

        for m1 in range(2):
            for e in range(2):

                @when(r.sides1[m1].has, jnp.logical_not(r.sides2[e].has))
                def _():
                    self.strip1(m1, e).wait_recv()
                    self.share1(m1, e).start()

    def relay_second(self):
        r = self.r
        for m in range(2):

            @when(r.sides2[m].has)
            def _():
                self.strip2(m).wait_recv()
                self.share2(m).start()

    def relay_corners(self):
        r = self.r
        for m1 in range(2):
            for m2 in range(2):

                @when(r.sides1[m1].has, r.sides2[m2].has)
                def _():
                    self.corner(m1, m2).wait_recv()
                    self.share_corner(m1, m2).start()

    def arrive(self):
        r = self.r
        for m in range(2):
            for e in range(2):
                when(r.sides1[m].has)(self.share1(m, e).wait_recv)
            when(r.sides2[m].has)(self.share2(m).wait_recv)
        for m1 in range(2):
            for m2 in range(2):
                when(r.sides1[m1].has, r.sides2[m2].has)(self.share_corner(m1, m2).wait_recv)

    def finish(self):
        r = self.r
        for m in range(2):
            for e in range(2):
                when(r.sides1[1 - m].has)(self.strip1(m, e).wait_send)
                when(r.sides1[m].has)(self.share1(m, e).wait_send)
            when(r.sides2[1 - m].has)(self.strip2(m).wait_send)
            when(r.sides2[m].has)(self.share2(m).wait_send)
        for m1 in range(2):
            for m2 in range(2):
                sent = r.sides1[1 - m1].has if self.direct else r.sides1[m1].has
                when(sent, r.sides2[1 - m2].has)(self.corner(m1, m2).wait_send)
                when(r.sides1[m1].has, r.sides2[m2].has)(self.share_corner(m1, m2).wait_send)


class Fold:
    def __init__(self, role, other, mine, theirs, pair, acc, rims, core, send, recv, partner):
        self.r, self.other, self.mine, self.theirs, self.pair, self.acc = role, other, mine, theirs, pair, acc
        self.rows1, self.cols1, self.rows2, self.cols2 = rims
        self.core, self.send, self.recv, self.partner = core, send, recv, partner
        w = acc.shape[-1]
        self.w, self.q4 = w, w // 4

    def piece(self, i, r):
        q4, cols = self.q4, (slice(None),) * 3
        if r.rows_first:
            return ((pl.ds(0, 1), pl.ds(3, 1), pl.ds(1, 2))[i], slice(None), slice(None), self.columns())
        return cols + ((pl.ds(0, q4),), (pl.ds(3 * q4, q4),), (pl.ds(q4, 2 * q4),))[i]

    def columns(self):
        q4 = self.q4
        if self.r.n2 == 2 and self.r.rows_first:
            return pl.ds(pl.multiple_of((1 - self.r.me2) * q4, q4), 3 * q4)
        return pl.ds(0, self.w)

    def needed(self, i, r):
        return pl.when(r.sides1[i].has) if i < 2 else lambda f: f()

    def pair_copy(self, i, r):
        at = self.piece(i, r)
        return remote(self.theirs.at[at], self.pair.at[at], self.send.at[i], self.recv.at[i], self.partner)

    def begin(self):
        for i in range(3):
            self.needed(i, self.other)(self.pair_copy(i, self.other).start)

    def add(self, i):
        @self.needed(i, self.r)
        def _():
            self.pair_copy(i, self.r).wait_recv()
            at = self.piece(i, self.r)
            self.acc[at] = self.mine[at] + self.pair[at]

    def spot(self, stage, i, m):
        r, q4, w = self.r, self.q4, self.w
        if r.rows_first == (stage == 0):
            if stage == 1:
                return (i, slice(None), slice(None), pl.ds(q4, 2 * q4)), self.rows2.at[m]
            cols = self.columns()
            return (i, slice(None), slice(None), cols), self.rows1.at[m, :, :, cols]
        groups = pl.ds(0, 4) if stage == 0 else pl.ds(1, 2)
        return (groups, slice(None), slice(None), pl.ds(i * q4, q4)), (self.cols1 if stage == 0 else self.cols2).at[m]

    def rim_copy(self, stage, m):
        sides = self.r.sides1 if stage == 0 else self.r.sides2
        at, rim = self.spot(stage, 3 * (1 - m), m)
        i = 3 + 2 * stage + m
        return remote(self.acc.at[at], rim, self.send.at[i], self.recv.at[i], sides[1 - m].where)

    def send_rims(self, stage, only=lambda k: True):
        sides = self.r.sides1 if stage == 0 else self.r.sides2
        for m in range(2):
            when(sides[1 - m].has, only(1 - m))(self.rim_copy(stage, m).start)

    def fold(self, stage, only=lambda k: True):
        sides = self.r.sides1 if stage == 0 else self.r.sides2
        for m in range(2):

            @when(sides[m].has, only(m))
            def _():
                self.rim_copy(stage, m).wait_recv()
                at, rim = self.spot(stage, 1 + m, m)
                self.acc[at] = self.acc[at] + rim[...]

    def share_copy(self, q):
        return remote(self.core.at[q], self.core.at[q], self.send.at[7], self.recv.at[7], self.partner)

    def share(self):
        q4 = self.q4
        self.core[self.r.q] = self.acc[1:3, :, :, q4 : 3 * q4]
        self.share_copy(self.r.q).start()

    def arrive(self):
        self.share_copy(self.r.o).wait_recv()

    def finish(self):
        r = self.r
        for i in range(3):
            self.needed(i, self.other)(self.pair_copy(i, self.other).wait_send)
        for m in range(2):
            when(r.sides1[1 - m].has)(self.rim_copy(0, m).wait_send)
            when(r.sides2[1 - m].has)(self.rim_copy(1, m).wait_send)
        if self.core is not None:
            self.share_copy(r.q).wait_send()


class ProbeSum:
    PAIR, INNER, OUTER, ROW = range(4)

    def __init__(self, q, nx, ny, prob, ppair, row_in, out_in, part, hub, total, send, recv, shared, partner):
        self.q, self.ny, self.chunks = q, ny, range(recv.shape[1])
        self.shared_sems = shared
        self.prob, self.ppair, self.row_in, self.out_in = prob, ppair, row_in, out_in
        self.part, self.hub, self.total = part, hub, total
        self.send, self.recv, self.partner = send, recv, partner
        self.size = prob.shape[1] // ny
        self.rows = self.size // len(self.chunks)
        me, mid = lax.axis_index("scanx"), nx // 2
        self.lower, self.upper = me < mid, me >= mid
        step = 2 * self.lower.astype(jnp.int32) - 1
        self.inner, self.outer = {"scanx": me + step}, {"scanx": me - step}
        self.has_outer = jnp.logical_and(me > 0, me < nx - 1)
        self.is_hub = jnp.logical_or(me == mid - 1, me == mid)
        self.not_hub = jnp.logical_not(self.is_hub)
        self.mine = lax.axis_index("scany")

    def column(self, d):
        return lax.rem(self.mine + d, self.ny)

    def origin(self, d):
        return lax.rem(self.mine - d + self.ny, self.ny)

    def at(self, h, c):
        if isinstance(h, int):
            return pl.ds(h * self.size + c * self.rows, self.rows)
        return pl.ds(pl.multiple_of(h * self.size + c * self.rows, 8), self.rows)

    def copy(self, src, dst, s, r, c, where):
        return remote(src, dst, self.send.at[s], self.recv.at[r, c], where)

    def pair(self, h, c):
        at = self.at(h, c)
        return self.copy(self.prob.at[1 - self.q, at], self.ppair.at[at], self.PAIR, self.PAIR, c, self.partner)

    def to_owner(self, d, c):
        to = self.column(d)
        src, dst = self.ppair.at[self.at(to, c)], self.row_in.at[self.mine, self.at(0, c)]
        return self.copy(src, dst, self.ROW + d - 1, self.ROW + d - 1, c, {"scany": to})

    def pass_in(self, c):
        at = self.at(0, c)
        return self.copy(self.part.at[at], self.out_in.at[at], self.INNER, self.INNER, c, self.inner)

    def between_hubs(self, c):
        at = self.at(0, c)
        return self.copy(self.part.at[at], self.hub.at[at], self.INNER, self.OUTER, c, self.inner)

    def pass_out(self, c):
        src, dst = self.total.at[self.q, self.at(self.mine, c)], self.hub.at[self.at(0, c)]
        return self.copy(src, dst, self.OUTER, self.OUTER, c, self.outer)

    def to_row(self, d, c):
        ref = self.total.at[self.q, self.at(self.mine, c)]
        return self.copy(ref, ref, self.ROW + self.ny + d - 2, self.ROW + self.ny + d - 2, c, {"scany": self.column(d)})

    def share(self, d, c, q):
        ref = self.total.at[q, self.at(self.origin(d), c)]
        return remote(ref, ref, self.shared_sems.at[0], self.shared_sems.at[1], self.partner)

    def wait(self, ref, r, c):
        self.copy(ref, ref, self.PAIR, r, c, self.partner).wait_recv()

    def one(self):
        for c in self.chunks:
            self.wait(self.ppair.at[pl.ds(0, self.ny * self.rows)], self.PAIR, c)
            for h in range(self.ny):
                at = self.at(h, c)
                self.ppair[at] = self.prob[self.q, at] + self.ppair[at]
            for d in range(1, self.ny):
                self.to_owner(d, c).start()

    def two(self):
        for c in self.chunks:
            at = self.at(0, c)
            value = self.ppair[self.at(self.mine, c)]
            for d in range(1, self.ny):
                slot = self.row_in.at[self.origin(d), at]
                self.wait(slot, self.ROW + d - 1, c)
                value = value + slot[...]
            self.part[at] = value

            @pl.when(self.has_outer)
            def _():
                slot = self.out_in.at[at]
                self.wait(slot, self.INNER, c)
                self.part[at] = self.part[at] + slot[...]

            pl.when(self.is_hub)(self.between_hubs(c).start)
            pl.when(self.not_hub)(self.pass_in(c).start)

    def inward(self, k):
        return self.upper if k == 0 else self.lower

    def late(self, k):
        return jnp.logical_and(self.inward(k), self.not_hub)

    def early(self, k):
        return jnp.logical_not(self.late(k))

    def three(self, chunks):
        for c in chunks:
            at, mine = self.at(0, c), self.at(self.mine, c)
            self.wait(self.hub.at[at], self.OUTER, c)

            @pl.when(self.is_hub)
            def _():
                self.total[self.q, mine] = self.part[at] + self.hub[at]

            @pl.when(self.not_hub)
            def _():
                self.total[self.q, mine] = self.hub[at]

            pl.when(self.has_outer)(self.pass_out(c).start)
            for d in range(1, self.ny):
                self.to_row(d, c).start()
            self.share(0, c, self.q).start()

    def four(self):
        for c in self.chunks:
            for d in range(1, self.ny):
                self.wait(self.total.at[self.q, self.at(self.origin(d), c)], self.ROW + self.ny + d - 2, c)
                self.share(d, c, self.q).start()

    def shared(self):
        ref = self.total.at[1 - self.q]
        remote(ref, ref, self.shared_sems.at[0], self.shared_sems.at[1], self.partner).wait_recv()

    def end(self):
        def sent(ref, stage):
            remote(ref, ref, self.send.at[stage], self.recv.at[0, 0], self.partner).wait_send()

        sent(self.ppair, self.PAIR)
        ref = self.total.at[self.q]
        remote(ref, ref, self.shared_sems.at[0], self.shared_sems.at[1], self.partner).wait_send()
        sent(self.part, self.INNER)
        pl.when(self.has_outer)(functools.partial(sent, self.part, self.OUTER))
        for d in range(1, self.ny):
            sent(self.part, self.ROW + d - 1)
            sent(self.part, self.ROW + self.ny + d - 2)


def near_greet(ny, partner, rows):
    my = lax.axis_index("scany")
    greet(
        [(True, partner)]
        + [(True, {"scany": lax.rem(my + d, ny)}) for d in range(1, ny)]
        + [(side.has, side.where) for side in rows]
    )


def row_ready(sem, rows):
    for i, side in enumerate(rows):

        @pl.when(side.has)
        def _(i=i, side=side):
            pl.semaphore_signal(sem.at[1 - i], inc=1, device_id=side.where, device_id_type=MESH)


def row_wait(sem, rows):
    for i, side in enumerate(rows):
        pl.when(side.has)(functools.partial(pl.semaphore_wait, sem.at[i], 1))


def each(step):
    p = lax.axis_index("pos")
    for q in range(2):
        pl.when(p == q)(functools.partial(step, q))


class Placer:
    def __init__(self, offsets, bufs, m, positions):
        self.bufs, self.m = bufs, m
        self.tall, self.span = m + 8, m + 128
        self.top = (bufs.shape[2] - self.tall // 8) // 2
        self.spots = []
        for j in range(positions):
            row, col = offsets[j, 0], offsets[j, 1]
            self.spots.append((lax.rem(row, 8), lax.rem(col, 128), lax.div(row, 8), lax.div(col, 128)))

    def clear(self):
        n, k, rows = self.bufs.shape[:3]
        bottom = self.top + self.tall // 8
        for j in range(n):
            for c in range(k):
                self.bufs[j, c, 0 : self.top] = jnp.zeros((self.top, *self.bufs.shape[3:]), jnp.float32)
                self.bufs[j, c, bottom:rows] = jnp.zeros((rows - bottom, *self.bufs.shape[3:]), jnp.float32)

    def put(self, j, k, term):
        row_in, col_in, _, step = self.spots[j]
        m, wide = self.m, self.bufs.shape[4]
        blank_rows = jnp.zeros((self.tall - m, m), jnp.float32)
        blank_cols = jnp.zeros((self.tall, self.span - m), jnp.float32)
        moved = pltpu.roll(jnp.concatenate([term, blank_rows], 0), row_in, 0)
        moved = pltpu.roll(jnp.concatenate([moved, blank_cols], 1), col_in, 1)
        out = None
        for d in range((wide - self.span) // 128 + 1):
            parts = [jnp.zeros((self.tall, w), jnp.float32) for w in (128 * d, wide - self.span - 128 * d)]
            here = jnp.concatenate([x for x in (parts[0], moved, parts[1]) if x.shape[1]], 1)
            out = here if out is None else jnp.where(step == d, here, out)
        self.bufs[j, k, self.top : self.top + self.tall // 8] = out.reshape(self.tall // 8, 8, wide)

    def rows(self, k, r0, count):
        out = None
        for j, (_, _, row, _) in enumerate(self.spots):
            part = self.bufs[j, k, pl.ds(self.top - row + r0 // 8, count // 8)]
            out = part if out is None else out + part
        return out.reshape(count, self.bufs.shape[4])

    def window(self, j, pad, k):
        row_in, col_in, row, step = self.spots[j]
        wide = pad.shape[3]
        block = pad[k, pl.ds(row, self.tall // 8)].reshape(self.tall, wide)
        out = block[:, : self.span]
        for d in range(1, (wide - self.span) // 128 + 1):
            out = jnp.where(step == d, block[:, 128 * d : 128 * d + self.span], out)
        out = pltpu.roll(out, lax.rem(self.span - col_in, self.span), 1)[:, : self.m]
        return pltpu.roll(out, lax.rem(self.tall - row_in, self.tall), 0)[: self.m]


def forward(window, pr, pi, table_a, table_b):
    m = pr.shape[0]
    bf = jnp.bfloat16
    ar, ai = window
    er = pr * ar - pi * ai
    ei = pr * ai + pi * ar
    left = dot(table_a[...], jnp.concatenate([er.astype(bf), ei.astype(bf)], 0)).astype(bf)
    return er, ei, dot(jnp.concatenate([left[:m], left[m:]], 1), table_b[...])


def backward(er, ei, far, amplitude, table_a, table_b):
    m = er.shape[0]
    bf = jnp.bfloat16
    fr, fi = far[:, :m], far[:, m:]
    ratio = amplitude.astype(jnp.float32) / jnp.maximum(jnp.sqrt(fr * fr + fi * fi), 0.2)
    projected = jnp.concatenate([(fr * ratio).astype(bf), (fi * ratio).astype(bf)], 0)
    back_half = dot(table_b[...], projected).astype(bf)
    back = dot(jnp.concatenate([back_half[:m], back_half[m:]], 1), table_a[...])
    return back[:, :m] - er, back[:, m:] - ei


def whole_kernel(nx, ny, step_size, *refs):
    offsets, spec, *given = refs[:6]
    new_spec, new_probe = refs[6:8]
    pad, probe, amplitudes, table_a, table_b, bufs, grad, prob, total, light_all = refs[8:18]
    pair, acc, xr2, zr1, ipair, iacc, ixr, izr, ppair, row_in, out_in, part, hub = refs[18:31]
    hsend, hrecv, local, gsend, grecv, isend, irecv, psend, precv, ssems, ready = refs[31:]
    tile, m = spec.shape[3], probe.shape[1]
    wide = pad.shape[3]
    half = (wide - tile) // 2
    h = grad.shape[3]
    positions, chunks = amplitudes.shape[0], precv.shape[1]
    p = lax.axis_index("pos")
    partner = {"pos": 1 - p}
    loads = [pltpu.make_async_copy(spec, pad.at[:, pl.ds(half // 8, tile // 8), :, pl.ds(half, tile)], local.at[0])]
    for i, (src, dst) in enumerate(zip(given, (probe, amplitudes, table_a, table_b)), 1):
        loads.append(pltpu.make_async_copy(src, dst, local.at[i]))
    for c in loads:
        c.start()
    roles = [Role(q, nx, ny) for q in range(2)]
    sides = roles[1].sides1 + roles[0].sides1
    near_greet(ny, partner, roles[1].sides1)
    halos = [Halo(r, spec, pad, hsend, hrecv, partner) for r in roles]
    role = Role(p, nx, ny, 1)
    fold = Fold(role, role, grad.at[p], grad.at[1 - p], pair, acc, (zr1, None, None, xr2), None, gsend, grecv, partner)
    light = Fold(
        role,
        role,
        grad.at[2, :, pl.ds(p, 1)],
        grad.at[2, :, pl.ds(1 - p, 1)],
        ipair,
        iacc,
        (izr, None, None, ixr),
        light_all,
        isend,
        irecv,
        partner,
    )
    probe_sum = ProbeSum(p, nx, ny, prob, ppair, row_in, out_in, part, hub, total, psend, precv, ssems, partner)
    placer = Placer(offsets, bufs, m, positions)

    def gather(k):
        for g in range(4):
            for b in range(2):
                grad[k, g, b] = placer.rows(k, (2 * g + b) * h, h)

    rows = roles[1].sides1
    pl.when(p == 0)(functools.partial(row_ready, ready, rows))
    each(lambda q: halos[q].begin())
    for i, at in enumerate(
        (
            (slice(None), pl.ds(0, half // 8)),
            (slice(None), pl.ds((half + tile) // 8, half // 8)),
            (slice(None), slice(None), slice(None), pl.ds(0, half)),
            (slice(None), slice(None), slice(None), pl.ds(half + tile, half)),
        )
    ):

        @pl.when(jnp.logical_not(sides[i].has))
        def _(at=at):
            pad[at] = jnp.zeros(pad.at[at].shape, pad.dtype)

    placer.clear()

    @pl.when(p == 0)
    def _():
        row_wait(ready, rows)
        halos[0].begin_corners()

    loads[1].wait()
    power = probe[0] * probe[0] + probe[1] * probe[1]
    for j in range(positions):
        placer.put(j, 2, power)
    gather(2)
    light.begin()

    def strips(q):
        halos[q].relay()

    def corners(q):
        halos[q].relay_second()
        halos[q].relay_corners()
        halos[1 - q].arrive()

    for i in range(3):
        light.add(i)
    light.send_rims(0)
    each(strips)
    each(corners)
    for c in loads[:1] + loads[2:]:
        c.wait()
    pr, pi = probe[0], probe[1]
    windows = [[placer.window(j, pad, k) for k in range(2)] for j in range(positions)]
    fields = [forward(windows[j], pr, pi, table_a, table_b) for j in range(positions)]
    light.fold(0)
    light.send_rims(1)
    diffs = [backward(*fields[j], amplitudes[j], table_a, table_b) for j in range(positions)]
    sums = [None, None]
    for (ar, ai), (dr, di) in zip(windows, diffs):
        for k, t in enumerate((ar * dr + ai * di, ar * di - ai * dr)):
            sums[k] = t if sums[k] is None else sums[k] + t
    for c in range(chunks):
        for part_of in range(ny):
            at = probe_sum.at(part_of, c)
            for k in range(2):
                prob[k, at] = sums[k][at.start : at.start + at.size]
            probe_sum.pair(part_of, c).start()
    for j, (dr, di) in enumerate(diffs):
        placer.put(j, 0, pr * dr + pi * di)
        placer.put(j, 1, pr * di - pi * dr)
    gather(1 - p)
    fold.begin()
    gather(p)

    def share_copy(q):
        return remote(new_spec.at[q], new_spec.at[q], gsend.at[7], grecv.at[7], partner)

    probe_sum.one()
    fold.add(0)
    fold.add(1)
    fold.send_rims(0, probe_sum.early)
    fold.add(2)
    light.fold(1)
    light.share()
    probe_sum.two()
    fold.send_rims(0, probe_sum.late)

    def strips_in():
        fold.fold(0)
        fold.send_rims(1)

    pl.when(jnp.logical_not(probe_sum.has_outer))(strips_in)
    probe_sum.three(range(chunks))
    pl.when(probe_sum.has_outer)(strips_in)
    light.arrive()
    fold.fold(1)
    q4 = fold.q4
    for g in range(2):
        for b in range(2):
            r0 = (2 * g + b) * h
            old = pad[p, (half + r0) // 8 : (half + r0 + h) // 8, :, half : half + tile].reshape(h, tile)
            new_spec[p, r0 : r0 + h] = old + acc[1 + g, b, :, q4 : 3 * q4] / (light_all[b, g, 0] + 1.0)
    share_copy(p).start()
    probe_sum.four()
    probe_sum.shared()
    share_copy(1 - p).wait_recv()
    share_copy(p).wait_send()
    light.finish()
    fold.finish()
    probe_sum.end()
    each(lambda q: halos[q].finish())
    for k in range(2):
        new_probe[k] = probe[k] + total[k] * step_size


def emit_kernel(spec, probe, new_spec, new_probe, sem):
    copies = [
        pltpu.make_async_copy(src.at[k, at], dst.at[k, at], sem.at[i, k, j])
        for i, (src, dst) in enumerate(((spec, new_spec), (probe, new_probe)))
        for k in range(2)
        for j, at in enumerate((pl.ds(0, src.shape[1] // 2), pl.ds(src.shape[1] // 2, src.shape[1] // 2)))
    ]
    for c in copies:
        c.start()
    for c in copies:
        c.wait()


def tables(length):
    index = np.arange(length)
    angle = ((index[:, None] * index[None, :]) % length).astype(np.float32) * np.float32(2.0 * math.pi / length)
    scale = np.float32(1.0 / math.sqrt(length))
    c = np.cos(angle) * scale
    s = np.sin(angle) * scale
    a = np.block([[c, s], [-s, c]]).astype(jnp.bfloat16)
    b = np.block([[c, -s], [s, c]]).astype(jnp.bfloat16)
    return a, b


def shards(nx, ny, consts, specimen, probe_wave, amplitudes, offsets):
    m = probe_wave.shape[1]
    tile = specimen.shape[1]
    wide = tile + m
    f32 = jnp.float32
    vm = pl.BlockSpec(memory_space=VMEM)
    sm = pl.BlockSpec(memory_space=pltpu.SMEM)
    hbm = pl.BlockSpec(memory_space=pltpu.HBM)
    dma = pltpu.SemaphoreType.DMA
    n = nx * ny
    h = wide // 8
    chunks = 8
    positions = offsets.shape[0]
    held = (probe_wave, amplitudes, consts[0], consts[1])

    step_size = 1.0 / math.sqrt(positions * n * 2)
    results = pl.pallas_call(
        functools.partial(whole_kernel, nx, ny, step_size),
        out_shape=[VMEM(specimen.shape, f32), VMEM(probe_wave.shape, f32)],
        in_specs=[sm] + [hbm] * 5,
        out_specs=[vm, vm],
        scratch_shapes=[
            VMEM((2, wide // 8, 8, wide), f32),
            *[VMEM(x.shape, x.dtype) for x in held],
            VMEM((positions, 3, (2 * (tile - 8) + m + 8) // 8, 8, wide), f32),
            VMEM((3, 4, 2, h, wide), f32),
            VMEM((2, m, m), f32),
            VMEM((2, m, m), f32),
            VMEM((2, 2, 1, h, wide // 2), f32),
            VMEM((4, 2, h, wide), f32),
            VMEM((4, 2, h, wide), f32),
            VMEM((2, 2, 2, h, wide // 4), f32),
            VMEM((2, 2, h, wide), f32),
            VMEM((4, 1, h, wide), f32),
            VMEM((4, 1, h, wide), f32),
            VMEM((2, 2, 1, h, wide // 4), f32),
            VMEM((2, 1, h, wide), f32),
            VMEM((m, m), f32),
            VMEM((ny, m // ny, m), f32),
            VMEM((m // ny, m), f32),
            VMEM((m // ny, m), f32),
            VMEM((m // ny, m), f32),
            dma((20,)),
            dma((20,)),
            dma((5,)),
            dma((8,)),
            dma((8,)),
            dma((8,)),
            dma((8,)),
            dma((1 + 2 * ny,)),
            dma((1 + 2 * ny, chunks)),
            dma((2,)),
            pltpu.SemaphoreType.REGULAR((2,)),
        ],
        compiler_params=pltpu.CompilerParams(vmem_limit_bytes=56 * 2**20, collective_id=0, has_side_effects=True),
        name="whole",
    )(offsets, *[pltpu.with_memory_space_constraint(x, pltpu.HBM) for x in (specimen.reshape(2, tile // 8, 8, tile), *held)])
    return pl.pallas_call(
        emit_kernel,
        out_shape=[jax.ShapeDtypeStruct(specimen.shape, f32), jax.ShapeDtypeStruct(probe_wave.shape, f32)],
        in_specs=[vm] * 2,
        out_specs=[pl.BlockSpec(memory_space=pl.ANY)] * 2,
        scratch_shapes=[dma((2, 2, 2))],
        compiler_params=pltpu.CompilerParams(vmem_limit_bytes=2 * 2**20),
        name="emit",
    )(*results)


def solution(mesh):
    nx, ny = mesh.shape["scanx"], mesh.shape["scany"]

    def run(specimen, probe_wave, amplitudes, offsets):
        consts = tables(probe_wave.shape[2])
        return jax.shard_map(
            lambda *args: shards(nx, ny, [jnp.asarray(t) for t in consts], *args),
            mesh=mesh,
            in_specs=(
                P(None, ("groups", "scanx"), "scany"),
                P(None, "groups", None),
                P(("groups", "scanx", "scany", "pos"), None, None),
                P(("groups", "scanx", "scany", "pos"), None),
            ),
            out_specs=(P(None, ("groups", "scanx"), "scany"), P(None, "groups", None)),
            check_vma=False,
        )(specimen, probe_wave, amplitudes, offsets)

    return run
```

```python
import functools
import math

import jax
import jax.numpy as jnp
import numpy as np
from jax import lax
from jax.experimental import pallas as pl
from jax.experimental.pallas import tpu as pltpu
from jax.sharding import PartitionSpec as P

MESH = pl.DeviceIdType.MESH
VMEM = pltpu.VMEM


def remote(src, dst, send, recv, where):
    return pltpu.make_async_remote_copy(
        src_ref=src, dst_ref=dst, send_sem=send, recv_sem=recv, device_id=where, device_id_type=MESH
    )


def greet(conditions_devices):
    barrier = pltpu.get_barrier_semaphore()
    for present, where in conditions_devices:
        if present is True:
            pl.semaphore_signal(barrier, inc=1, device_id=where, device_id_type=MESH)
        else:

            @pl.when(present)
            def _(where=where):
                pl.semaphore_signal(barrier, inc=1, device_id=where, device_id_type=MESH)

    fixed = sum(1 for present, _ in conditions_devices if present is True)
    peers = [present.astype(jnp.int32) for present, _ in conditions_devices if present is not True]
    pl.semaphore_wait(barrier, sum(peers, fixed))


class Side:
    def __init__(self, axis, count, step):
        me = lax.axis_index(axis)
        self.has = me > 0 if step < 0 else me < count - 1
        self.where = {axis: me + step}


class Role:
    def __init__(self, q, nx, ny, order=None):
        order = q if order is None else order
        along_x = ("scanx", nx, Side("scanx", nx, -1), Side("scanx", nx, 1))
        along_y = ("scany", ny, Side("scany", ny, -1), Side("scany", ny, 1))
        one, two = (along_y, along_x) if order == 0 else (along_x, along_y)
        self.q, self.o, self.rows_first = q, 1 - q, order == 1
        self.axis1, self.n1, self.sides1 = one[0], one[1], one[2:]
        self.axis2, self.n2, self.sides2 = two[0], two[1], two[2:]
        self.me1, self.me2 = lax.axis_index(self.axis1), lax.axis_index(self.axis2)


def when(*conditions):
    return pl.when(functools.reduce(jnp.logical_and, [c for c in conditions if c is not True]))


def dot(a, b):
    return jnp.dot(a, b, preferred_element_type=jnp.float32)


class Halo:
    def __init__(self, role, spec, pad, send, recv, partner):
        self.r, self.spec, self.pad, self.partner = role, spec, pad, partner
        self.send, self.recv = send, recv
        self.direct = not role.rows_first
        tile = spec.shape[3]
        half = (pad.shape[3] - tile) // 2
        self.own = (half, tile)
        self.margins = ((0, half), (half + tile, half))
        self.edges = ((0, half), (tile - half, half))
        self.pad_edges = ((half, half), (tile, half))
        self.whole = (0, tile)

    def at(self, one, two):
        rows, cols = (one, two) if self.r.rows_first else (two, one)
        return (self.r.q, pl.ds(rows[0] // 8, rows[1] // 8), slice(None), pl.ds(*cols))

    def copy(self, src, dst, i, where):
        return remote(src, dst, self.send.at[i], self.recv.at[i], where)

    def strip1(self, m, e):
        return self.copy(
            self.spec.at[self.at(self.edges[1 - m], self.edges[e])],
            self.pad.at[self.at(self.margins[m], self.pad_edges[e])],
            2 * m + e,
            self.r.sides1[1 - m].where,
        )

    def strip2(self, m):
        return self.copy(
            self.spec.at[self.at(self.whole, self.edges[1 - m])],
            self.pad.at[self.at(self.own, self.margins[m])],
            4 + m,
            self.r.sides2[1 - m].where,
        )

    def corner(self, m1, m2):
        if self.direct:
            return self.copy(
                self.spec.at[self.at(self.edges[1 - m1], self.edges[1 - m2])],
                self.pad.at[self.at(self.margins[m1], self.margins[m2])],
                6 + 2 * m1 + m2,
                {**self.r.sides1[1 - m1].where, **self.r.sides2[1 - m2].where},
            )
        return self.copy(
            self.pad.at[self.at(self.margins[m1], self.pad_edges[1 - m2])],
            self.pad.at[self.at(self.margins[m1], self.margins[m2])],
            6 + 2 * m1 + m2,
            self.r.sides2[1 - m2].where,
        )

    def share(self, i, one, two):
        ref = self.pad.at[self.at(one, two)]
        return self.copy(ref, ref, 10 + i, self.partner)

    def share1(self, m, e):
        return self.share(2 * m + e, self.margins[m], self.pad_edges[e])

    def share2(self, m):
        return self.share(4 + m, self.own, self.margins[m])

    def share_corner(self, m1, m2):
        return self.share(6 + 2 * m1 + m2, self.margins[m1], self.margins[m2])

    def begin(self):
        r = self.r
        for m in range(2):
            for e in range(2):
                when(r.sides1[1 - m].has, r.sides2[e].has)(self.strip1(m, e).start)
        for m in range(2):
            when(r.sides2[1 - m].has)(self.strip2(m).start)
        for m in range(2):
            for e in range(2):
                when(r.sides1[1 - m].has, jnp.logical_not(r.sides2[e].has))(self.strip1(m, e).start)

    def begin_corners(self):
        r = self.r
        for m1 in range(2):
            for m2 in range(2):
                when(r.sides1[1 - m1].has, r.sides2[1 - m2].has)(self.corner(m1, m2).start)

    def relay(self):
        r = self.r
        for m1 in range(2):
            for e in range(2):

                @when(r.sides1[m1].has, r.sides2[e].has)
                def _():
                    self.strip1(m1, e).wait_recv()
                    if not self.direct:
                        self.corner(m1, 1 - e).start()
                    self.share1(m1, e).start()

        for m1 in range(2):
            for e in range(2):

                @when(r.sides1[m1].has, jnp.logical_not(r.sides2[e].has))
                def _():
                    self.strip1(m1, e).wait_recv()
                    self.share1(m1, e).start()

    def relay_second(self):
        r = self.r
        for m in range(2):

            @when(r.sides2[m].has)
            def _():
                self.strip2(m).wait_recv()
                self.share2(m).start()

    def relay_corners(self):
        r = self.r
        for m1 in range(2):
            for m2 in range(2):

                @when(r.sides1[m1].has, r.sides2[m2].has)
                def _():
                    self.corner(m1, m2).wait_recv()
                    self.share_corner(m1, m2).start()

    def arrive(self):
        r = self.r
        for m in range(2):
            for e in range(2):
                when(r.sides1[m].has)(self.share1(m, e).wait_recv)
            when(r.sides2[m].has)(self.share2(m).wait_recv)
        for m1 in range(2):
            for m2 in range(2):
                when(r.sides1[m1].has, r.sides2[m2].has)(self.share_corner(m1, m2).wait_recv)

    def finish(self):
        r = self.r
        for m in range(2):
            for e in range(2):
                when(r.sides1[1 - m].has)(self.strip1(m, e).wait_send)
                when(r.sides1[m].has)(self.share1(m, e).wait_send)
            when(r.sides2[1 - m].has)(self.strip2(m).wait_send)
            when(r.sides2[m].has)(self.share2(m).wait_send)
        for m1 in range(2):
            for m2 in range(2):
                sent = r.sides1[1 - m1].has if self.direct else r.sides1[m1].has
                when(sent, r.sides2[1 - m2].has)(self.corner(m1, m2).wait_send)
                when(r.sides1[m1].has, r.sides2[m2].has)(self.share_corner(m1, m2).wait_send)


class Fold:
    def __init__(self, role, other, mine, theirs, pair, acc, rims, core, send, recv, partner):
        self.r, self.other, self.mine, self.theirs, self.pair, self.acc = role, other, mine, theirs, pair, acc
        self.rows1, self.cols1, self.rows2, self.cols2 = rims
        self.core, self.send, self.recv, self.partner = core, send, recv, partner
        w = acc.shape[-1]
        self.w, self.q4 = w, w // 4

    def piece(self, i, r):
        q4, cols = self.q4, (slice(None),) * 3
        if r.rows_first:
            return ((pl.ds(0, 1), pl.ds(3, 1), pl.ds(1, 2))[i], slice(None), slice(None), self.columns())
        return cols + ((pl.ds(0, q4),), (pl.ds(3 * q4, q4),), (pl.ds(q4, 2 * q4),))[i]

    def columns(self):
        q4 = self.q4
        if self.r.n2 == 2 and self.r.rows_first:
            return pl.ds(pl.multiple_of((1 - self.r.me2) * q4, q4), 3 * q4)
        return pl.ds(0, self.w)

    def needed(self, i, r):
        return pl.when(r.sides1[i].has) if i < 2 else lambda f: f()

    def pair_copy(self, i, r):
        at = self.piece(i, r)
        return remote(self.theirs.at[at], self.pair.at[at], self.send.at[i], self.recv.at[i], self.partner)

    def begin(self):
        for i in range(3):
            self.needed(i, self.other)(self.pair_copy(i, self.other).start)

    def add(self, i):
        @self.needed(i, self.r)
        def _():
            self.pair_copy(i, self.r).wait_recv()
            at = self.piece(i, self.r)
            self.acc[at] = self.mine[at] + self.pair[at]

    def spot(self, stage, i, m):
        r, q4, w = self.r, self.q4, self.w
        if r.rows_first == (stage == 0):
            if stage == 1:
                return (i, slice(None), slice(None), pl.ds(q4, 2 * q4)), self.rows2.at[m]
            cols = self.columns()
            return (i, slice(None), slice(None), cols), self.rows1.at[m, :, :, cols]
        groups = pl.ds(0, 4) if stage == 0 else pl.ds(1, 2)
        return (groups, slice(None), slice(None), pl.ds(i * q4, q4)), (self.cols1 if stage == 0 else self.cols2).at[m]

    def rim_copy(self, stage, m):
        sides = self.r.sides1 if stage == 0 else self.r.sides2
        at, rim = self.spot(stage, 3 * (1 - m), m)
        i = 3 + 2 * stage + m
        return remote(self.acc.at[at], rim, self.send.at[i], self.recv.at[i], sides[1 - m].where)

    def send_rims(self, stage, only=lambda k: True):
        sides = self.r.sides1 if stage == 0 else self.r.sides2
        for m in range(2):
            when(sides[1 - m].has, only(1 - m))(self.rim_copy(stage, m).start)

    def fold(self, stage, only=lambda k: True):
        sides = self.r.sides1 if stage == 0 else self.r.sides2
        for m in range(2):

            @when(sides[m].has, only(m))
            def _():
                self.rim_copy(stage, m).wait_recv()
                at, rim = self.spot(stage, 1 + m, m)
                self.acc[at] = self.acc[at] + rim[...]

    def share_copy(self, q):
        return remote(self.core.at[q], self.core.at[q], self.send.at[7], self.recv.at[7], self.partner)

    def share(self):
        q4 = self.q4
        self.core[self.r.q] = self.acc[1:3, :, :, q4 : 3 * q4]
        self.share_copy(self.r.q).start()

    def arrive(self):
        self.share_copy(self.r.o).wait_recv()

    def finish(self):
        r = self.r
        for i in range(3):
            self.needed(i, self.other)(self.pair_copy(i, self.other).wait_send)
        for m in range(2):
            when(r.sides1[1 - m].has)(self.rim_copy(0, m).wait_send)
            when(r.sides2[1 - m].has)(self.rim_copy(1, m).wait_send)
        if self.core is not None:
            self.share_copy(r.q).wait_send()


class ProbeSum:
    PAIR, INNER, OUTER, ROW = range(4)

    def __init__(self, q, nx, ny, prob, ppair, row_in, out_in, part, hub, total, send, recv, shared, partner):
        self.q, self.ny, self.chunks = q, ny, range(recv.shape[1])
        self.shared_sems = shared
        self.prob, self.ppair, self.row_in, self.out_in = prob, ppair, row_in, out_in
        self.part, self.hub, self.total = part, hub, total
        self.send, self.recv, self.partner = send, recv, partner
        self.size = prob.shape[1] // ny
        self.rows = self.size // len(self.chunks)
        me, mid = lax.axis_index("scanx"), nx // 2
        self.lower, self.upper = me < mid, me >= mid
        step = 2 * self.lower.astype(jnp.int32) - 1
        self.inner, self.outer = {"scanx": me + step}, {"scanx": me - step}
        self.has_outer = jnp.logical_and(me > 0, me < nx - 1)
        self.is_hub = jnp.logical_or(me == mid - 1, me == mid)
        self.not_hub = jnp.logical_not(self.is_hub)
        self.is_last = jnp.logical_and(self.not_hub, jnp.logical_not(self.has_outer))
        self.not_last = jnp.logical_not(self.is_last)
        near_end = jnp.logical_or(me == 1, me == nx - 2)
        self.outer_last = jnp.logical_and(self.has_outer, near_end)
        self.first_direct = len(self.chunks) - len(self.chunks) * 4 // 8
        self.mine = lax.axis_index("scany")

    def column(self, d):
        return lax.rem(self.mine + d, self.ny)

    def origin(self, d):
        return lax.rem(self.mine - d + self.ny, self.ny)

    def at(self, h, c):
        if isinstance(h, int):
            return pl.ds(h * self.size + c * self.rows, self.rows)
        return pl.ds(pl.multiple_of(h * self.size + c * self.rows, 8), self.rows)

    def copy(self, src, dst, s, r, c, where):
        return remote(src, dst, self.send.at[s], self.recv.at[r, c], where)

    def pair(self, h, c):
        at = self.at(h, c)
        return self.copy(self.prob.at[1 - self.q, at], self.ppair.at[at], self.PAIR, self.PAIR, c, self.partner)

    def to_owner(self, d, c):
        to = self.column(d)
        src, dst = self.ppair.at[self.at(to, c)], self.row_in.at[self.mine, self.at(0, c)]
        return self.copy(src, dst, self.ROW + d - 1, self.ROW + d - 1, c, {"scany": to})

    def pass_in(self, c):
        at = self.at(0, c)
        return self.copy(self.part.at[at], self.out_in.at[at], self.INNER, self.INNER, c, self.inner)

    def between_hubs(self, c):
        at = self.at(0, c)
        return self.copy(self.part.at[at], self.hub.at[at], self.INNER, self.OUTER, c, self.inner)

    def pass_out(self, c):
        src, dst = self.total.at[self.q, self.at(self.mine, c)], self.hub.at[self.at(0, c)]
        return self.copy(src, dst, self.OUTER, self.OUTER, c, self.outer)

    def to_row(self, d, c):
        ref = self.total.at[self.q, self.at(self.mine, c)]
        return self.copy(ref, ref, self.ROW + self.ny + d - 2, self.ROW + self.ny + d - 2, c, {"scany": self.column(d)})

    def to_end(self, d, c):
        ref = self.total.at[self.q, self.at(self.mine, c)]
        where = {"scanx": self.outer["scanx"], "scany": self.column(d)}
        return remote(ref, ref, self.shared_sems.at[1 + d], self.recv.at[self.ROW + self.ny + d - 2, c], where)

    def share(self, d, c, q):
        ref = self.total.at[q, self.at(self.origin(d), c)]
        return remote(ref, ref, self.shared_sems.at[0], self.shared_sems.at[1], self.partner)

    def wait(self, ref, r, c):
        self.copy(ref, ref, self.PAIR, r, c, self.partner).wait_recv()

    def one(self):
        for c in self.chunks:
            self.wait(self.ppair.at[pl.ds(0, self.ny * self.rows)], self.PAIR, c)
            for h in range(self.ny):
                at = self.at(h, c)
                self.ppair[at] = self.prob[self.q, at] + self.ppair[at]
            for d in range(1, self.ny):
                self.to_owner(d, c).start()

    def two(self):
        for c in self.chunks:
            at = self.at(0, c)
            value = self.ppair[self.at(self.mine, c)]
            for d in range(1, self.ny):
                slot = self.row_in.at[self.origin(d), at]
                self.wait(slot, self.ROW + d - 1, c)
                value = value + slot[...]
            self.part[at] = value

            @pl.when(self.has_outer)
            def _():
                slot = self.out_in.at[at]
                self.wait(slot, self.INNER, c)
                self.part[at] = self.part[at] + slot[...]

            pl.when(self.is_hub)(self.between_hubs(c).start)
            pl.when(self.not_hub)(self.pass_in(c).start)

    def inward(self, k):
        return self.upper if k == 0 else self.lower

    def late(self, k):
        return jnp.logical_and(self.inward(k), self.not_hub)

    def early(self, k):
        return jnp.logical_not(self.late(k))

    def three(self, chunks):
        for c in chunks:
            at, mine = self.at(0, c), self.at(self.mine, c)
            self.wait(self.hub.at[at], self.OUTER, c)

            @pl.when(self.is_hub)
            def _():
                self.total[self.q, mine] = self.part[at] + self.hub[at]

            @pl.when(self.not_hub)
            def _():
                self.total[self.q, mine] = self.hub[at]

            pl.when(self.has_outer)(self.pass_out(c).start)
            for d in range(1, self.ny):
                if c < self.first_direct:
                    self.to_row(d, c).start()
                else:
                    pl.when(self.outer_last)(self.to_end(d, c).start)
                    pl.when(self.not_last)(self.to_row(d, c).start)
            self.share(0, c, self.q).start()

    def four(self):
        for c in self.chunks:
            for d in range(1, self.ny):
                self.wait(self.total.at[self.q, self.at(self.origin(d), c)], self.ROW + self.ny + d - 2, c)
                self.share(d, c, self.q).start()

    def shared(self):
        ref = self.total.at[1 - self.q]
        remote(ref, ref, self.shared_sems.at[0], self.shared_sems.at[1], self.partner).wait_recv()

    def end(self):
        def sent(ref, stage):
            remote(ref, ref, self.send.at[stage], self.recv.at[0, 0], self.partner).wait_send()

        sent(self.ppair, self.PAIR)
        ref = self.total.at[self.q]
        remote(ref, ref, self.shared_sems.at[0], self.shared_sems.at[1], self.partner).wait_send()
        sent(self.part, self.INNER)
        pl.when(self.has_outer)(functools.partial(sent, self.part, self.OUTER))
        for d in range(1, self.ny):
            sent(self.part, self.ROW + d - 1)
            first = self.first_direct * self.rows
            stage = self.ROW + self.ny + d - 2
            pl.when(self.not_last)(functools.partial(sent, self.part, stage))
            pl.when(self.is_last)(functools.partial(sent, self.part.at[pl.ds(0, first)], stage))

            @pl.when(self.outer_last)
            def _():
                ref = self.part.at[pl.ds(0, self.size - first)]
                remote(ref, ref, self.shared_sems.at[1 + d], self.recv.at[0, 0], self.partner).wait_send()


def near_greet(ny, partner, rows):
    my = lax.axis_index("scany")
    greet(
        [(True, partner)]
        + [(True, {"scany": lax.rem(my + d, ny)}) for d in range(1, ny)]
        + [(side.has, side.where) for side in rows]
    )


def row_ready(sem, rows):
    for i, side in enumerate(rows):

        @pl.when(side.has)
        def _(i=i, side=side):
            pl.semaphore_signal(sem.at[1 - i], inc=1, device_id=side.where, device_id_type=MESH)


def row_wait(sem, rows):
    for i, side in enumerate(rows):
        pl.when(side.has)(functools.partial(pl.semaphore_wait, sem.at[i], 1))


def each(step):
    p = lax.axis_index("pos")
    for q in range(2):
        pl.when(p == q)(functools.partial(step, q))


class Placer:
    def __init__(self, offsets, bufs, m, positions):
        self.bufs, self.m = bufs, m
        self.tall, self.span = m + 8, m + 128
        self.top = (bufs.shape[2] - self.tall // 8) // 2
        self.spots = []
        for j in range(positions):
            row, col = offsets[j, 0], offsets[j, 1]
            self.spots.append((lax.rem(row, 8), lax.rem(col, 128), lax.div(row, 8), lax.div(col, 128)))

    def clear(self):
        n, k, rows = self.bufs.shape[:3]
        bottom = self.top + self.tall // 8
        for j in range(n):
            for c in range(k):
                self.bufs[j, c, 0 : self.top] = jnp.zeros((self.top, *self.bufs.shape[3:]), jnp.float32)
                self.bufs[j, c, bottom:rows] = jnp.zeros((rows - bottom, *self.bufs.shape[3:]), jnp.float32)

    def put(self, j, k, term):
        row_in, col_in, _, step = self.spots[j]
        m, wide = self.m, self.bufs.shape[4]
        blank_rows = jnp.zeros((self.tall - m, m), jnp.float32)
        blank_cols = jnp.zeros((self.tall, self.span - m), jnp.float32)
        moved = pltpu.roll(jnp.concatenate([term, blank_rows], 0), row_in, 0)
        moved = pltpu.roll(jnp.concatenate([moved, blank_cols], 1), col_in, 1)
        out = None
        for d in range((wide - self.span) // 128 + 1):
            parts = [jnp.zeros((self.tall, w), jnp.float32) for w in (128 * d, wide - self.span - 128 * d)]
            here = jnp.concatenate([x for x in (parts[0], moved, parts[1]) if x.shape[1]], 1)
            out = here if out is None else jnp.where(step == d, here, out)
        self.bufs[j, k, self.top : self.top + self.tall // 8] = out.reshape(self.tall // 8, 8, wide)

    def rows(self, k, r0, count):
        out = None
        for j, (_, _, row, _) in enumerate(self.spots):
            part = self.bufs[j, k, pl.ds(self.top - row + r0 // 8, count // 8)]
            out = part if out is None else out + part
        return out.reshape(count, self.bufs.shape[4])

    def window(self, j, pad, k):
        row_in, col_in, row, step = self.spots[j]
        wide = pad.shape[3]
        block = pad[k, pl.ds(row, self.tall // 8)].reshape(self.tall, wide)
        out = block[:, : self.span]
        for d in range(1, (wide - self.span) // 128 + 1):
            out = jnp.where(step == d, block[:, 128 * d : 128 * d + self.span], out)
        out = pltpu.roll(out, lax.rem(self.span - col_in, self.span), 1)[:, : self.m]
        return pltpu.roll(out, lax.rem(self.tall - row_in, self.tall), 0)[: self.m]


def forward(window, pr, pi, table_a, table_b):
    m = pr.shape[0]
    bf = jnp.bfloat16
    ar, ai = window
    er = pr * ar - pi * ai
    ei = pr * ai + pi * ar
    left = dot(table_a[...], jnp.concatenate([er.astype(bf), ei.astype(bf)], 0)).astype(bf)
    return er, ei, dot(jnp.concatenate([left[:m], left[m:]], 1), table_b[...])


def backward(er, ei, far, amplitude, table_a, table_b):
    m = er.shape[0]
    bf = jnp.bfloat16
    fr, fi = far[:, :m], far[:, m:]
    ratio = amplitude.astype(jnp.float32) / jnp.maximum(jnp.sqrt(fr * fr + fi * fi), 0.2)
    projected = jnp.concatenate([(fr * ratio).astype(bf), (fi * ratio).astype(bf)], 0)
    back_half = dot(table_b[...], projected).astype(bf)
    back = dot(jnp.concatenate([back_half[:m], back_half[m:]], 1), table_a[...])
    return back[:, :m] - er, back[:, m:] - ei


def whole_kernel(nx, ny, step_size, *refs):
    offsets, spec, *given = refs[:6]
    new_spec, new_probe = refs[6:8]
    pad, probe, amplitudes, table_a, table_b, bufs, grad, prob, total, light_all = refs[8:18]
    pair, acc, xr2, zr1, ipair, iacc, ixr, izr, ppair, row_in, out_in, part, hub = refs[18:31]
    hsend, hrecv, local, gsend, grecv, isend, irecv, psend, precv, ssems, ready = refs[31:]
    tile, m = spec.shape[3], probe.shape[1]
    wide = pad.shape[3]
    half = (wide - tile) // 2
    h = grad.shape[3]
    positions, chunks = amplitudes.shape[0], precv.shape[1]
    p = lax.axis_index("pos")
    partner = {"pos": 1 - p}
    loads = [pltpu.make_async_copy(spec, pad.at[:, pl.ds(half // 8, tile // 8), :, pl.ds(half, tile)], local.at[0])]
    for i, (src, dst) in enumerate(zip(given, (probe, amplitudes, table_a, table_b)), 1):
        loads.append(pltpu.make_async_copy(src, dst, local.at[i]))
    for c in loads:
        c.start()
    roles = [Role(q, nx, ny) for q in range(2)]
    sides = roles[1].sides1 + roles[0].sides1
    near_greet(ny, partner, roles[1].sides1)
    halos = [Halo(r, spec, pad, hsend, hrecv, partner) for r in roles]
    role = Role(p, nx, ny, 1)
    fold = Fold(role, role, grad.at[p], grad.at[1 - p], pair, acc, (zr1, None, None, xr2), None, gsend, grecv, partner)
    light = Fold(
        role,
        role,
        grad.at[2, :, pl.ds(p, 1)],
        grad.at[2, :, pl.ds(1 - p, 1)],
        ipair,
        iacc,
        (izr, None, None, ixr),
        light_all,
        isend,
        irecv,
        partner,
    )
    probe_sum = ProbeSum(p, nx, ny, prob, ppair, row_in, out_in, part, hub, total, psend, precv, ssems, partner)
    placer = Placer(offsets, bufs, m, positions)

    def gather(k):
        for g in range(4):
            for b in range(2):
                grad[k, g, b] = placer.rows(k, (2 * g + b) * h, h)

    rows = roles[1].sides1
    pl.when(p == 0)(functools.partial(row_ready, ready, rows))
    each(lambda q: halos[q].begin())
    for i, at in enumerate(
        (
            (slice(None), pl.ds(0, half // 8)),
            (slice(None), pl.ds((half + tile) // 8, half // 8)),
            (slice(None), slice(None), slice(None), pl.ds(0, half)),
            (slice(None), slice(None), slice(None), pl.ds(half + tile, half)),
        )
    ):

        @pl.when(jnp.logical_not(sides[i].has))
        def _(at=at):
            pad[at] = jnp.zeros(pad.at[at].shape, pad.dtype)

    placer.clear()

    @pl.when(p == 0)
    def _():
        row_wait(ready, rows)
        halos[0].begin_corners()

    loads[1].wait()
    power = probe[0] * probe[0] + probe[1] * probe[1]
    for j in range(positions):
        placer.put(j, 2, power)
    gather(2)
    light.begin()

    def strips(q):
        halos[q].relay()

    def corners(q):
        halos[q].relay_second()
        halos[q].relay_corners()
        halos[1 - q].arrive()

    for i in range(3):
        light.add(i)
    light.send_rims(0)
    each(strips)
    each(corners)
    for c in loads[:1] + loads[2:]:
        c.wait()
    pr, pi = probe[0], probe[1]
    windows = [[placer.window(j, pad, k) for k in range(2)] for j in range(positions)]
    fields = [forward(windows[j], pr, pi, table_a, table_b) for j in range(positions)]
    light.fold(0)
    light.send_rims(1)
    diffs = [backward(*fields[j], amplitudes[j], table_a, table_b) for j in range(positions)]
    sums = [None, None]
    for (ar, ai), (dr, di) in zip(windows, diffs):
        for k, t in enumerate((ar * dr + ai * di, ar * di - ai * dr)):
            sums[k] = t if sums[k] is None else sums[k] + t
    for c in range(chunks):
        for part_of in range(ny):
            at = probe_sum.at(part_of, c)
            for k in range(2):
                prob[k, at] = sums[k][at.start : at.start + at.size]
            probe_sum.pair(part_of, c).start()
    for j, (dr, di) in enumerate(diffs):
        placer.put(j, 0, pr * dr + pi * di)
        placer.put(j, 1, pr * di - pi * dr)
    gather(1 - p)
    fold.begin()
    gather(p)

    def share_copy(q):
        return remote(new_spec.at[q], new_spec.at[q], gsend.at[7], grecv.at[7], partner)

    probe_sum.one()
    fold.add(0)
    fold.add(1)
    fold.send_rims(0, probe_sum.early)
    fold.add(2)
    light.fold(1)
    light.share()
    probe_sum.two()
    fold.send_rims(0, probe_sum.late)

    def strips_in():
        fold.fold(0)
        fold.send_rims(1)

    pl.when(jnp.logical_not(probe_sum.has_outer))(strips_in)
    probe_sum.three(range(chunks))
    pl.when(probe_sum.has_outer)(strips_in)
    light.arrive()
    fold.fold(1)
    q4 = fold.q4
    for g in range(2):
        for b in range(2):
            r0 = (2 * g + b) * h
            old = pad[p, (half + r0) // 8 : (half + r0 + h) // 8, :, half : half + tile].reshape(h, tile)
            new_spec[p, r0 : r0 + h] = old + acc[1 + g, b, :, q4 : 3 * q4] / (light_all[b, g, 0] + 1.0)
    share_copy(p).start()
    probe_sum.four()
    probe_sum.shared()
    share_copy(1 - p).wait_recv()
    share_copy(p).wait_send()
    light.finish()
    fold.finish()
    probe_sum.end()
    each(lambda q: halos[q].finish())
    for k in range(2):
        new_probe[k] = probe[k] + total[k] * step_size


def emit_kernel(spec, probe, new_spec, new_probe, sem):
    copies = [
        pltpu.make_async_copy(src.at[k, at], dst.at[k, at], sem.at[i, k, j])
        for i, (src, dst) in enumerate(((spec, new_spec), (probe, new_probe)))
        for k in range(2)
        for j, at in enumerate((pl.ds(0, src.shape[1] // 2), pl.ds(src.shape[1] // 2, src.shape[1] // 2)))
    ]
    for c in copies:
        c.start()
    for c in copies:
        c.wait()


def tables(length):
    index = np.arange(length)
    angle = ((index[:, None] * index[None, :]) % length).astype(np.float32) * np.float32(2.0 * math.pi / length)
    scale = np.float32(1.0 / math.sqrt(length))
    c = np.cos(angle) * scale
    s = np.sin(angle) * scale
    a = np.block([[c, s], [-s, c]]).astype(jnp.bfloat16)
    b = np.block([[c, -s], [s, c]]).astype(jnp.bfloat16)
    return a, b


def shards(nx, ny, consts, specimen, probe_wave, amplitudes, offsets):
    m = probe_wave.shape[1]
    tile = specimen.shape[1]
    wide = tile + m
    f32 = jnp.float32
    vm = pl.BlockSpec(memory_space=VMEM)
    sm = pl.BlockSpec(memory_space=pltpu.SMEM)
    hbm = pl.BlockSpec(memory_space=pltpu.HBM)
    dma = pltpu.SemaphoreType.DMA
    n = nx * ny
    h = wide // 8
    chunks = 8
    positions = offsets.shape[0]
    held = (probe_wave, amplitudes, consts[0], consts[1])

    step_size = 1.0 / math.sqrt(positions * n * 2)
    results = pl.pallas_call(
        functools.partial(whole_kernel, nx, ny, step_size),
        out_shape=[VMEM(specimen.shape, f32), VMEM(probe_wave.shape, f32)],
        in_specs=[sm] + [hbm] * 5,
        out_specs=[vm, vm],
        scratch_shapes=[
            VMEM((2, wide // 8, 8, wide), f32),
            *[VMEM(x.shape, x.dtype) for x in held],
            VMEM((positions, 3, (2 * (tile - 8) + m + 8) // 8, 8, wide), f32),
            VMEM((3, 4, 2, h, wide), f32),
            VMEM((2, m, m), f32),
            VMEM((2, m, m), f32),
            VMEM((2, 2, 1, h, wide // 2), f32),
            VMEM((4, 2, h, wide), f32),
            VMEM((4, 2, h, wide), f32),
            VMEM((2, 2, 2, h, wide // 4), f32),
            VMEM((2, 2, h, wide), f32),
            VMEM((4, 1, h, wide), f32),
            VMEM((4, 1, h, wide), f32),
            VMEM((2, 2, 1, h, wide // 4), f32),
            VMEM((2, 1, h, wide), f32),
            VMEM((m, m), f32),
            VMEM((ny, m // ny, m), f32),
            VMEM((m // ny, m), f32),
            VMEM((m // ny, m), f32),
            VMEM((m // ny, m), f32),
            dma((20,)),
            dma((20,)),
            dma((5,)),
            dma((8,)),
            dma((8,)),
            dma((8,)),
            dma((8,)),
            dma((1 + 2 * ny,)),
            dma((1 + 2 * ny, chunks)),
            dma((1 + ny,)),
            pltpu.SemaphoreType.REGULAR((2,)),
        ],
        compiler_params=pltpu.CompilerParams(vmem_limit_bytes=56 * 2**20, collective_id=0, has_side_effects=True),
        name="whole",
    )(offsets, *[pltpu.with_memory_space_constraint(x, pltpu.HBM) for x in (specimen.reshape(2, tile // 8, 8, tile), *held)])
    return pl.pallas_call(
        emit_kernel,
        out_shape=[jax.ShapeDtypeStruct(specimen.shape, f32), jax.ShapeDtypeStruct(probe_wave.shape, f32)],
        in_specs=[vm] * 2,
        out_specs=[pl.BlockSpec(memory_space=pl.ANY)] * 2,
        scratch_shapes=[dma((2, 2, 2))],
        compiler_params=pltpu.CompilerParams(vmem_limit_bytes=2 * 2**20),
        name="emit",
    )(*results)


def solution(mesh):
    nx, ny = mesh.shape["scanx"], mesh.shape["scany"]

    def run(specimen, probe_wave, amplitudes, offsets):
        consts = tables(probe_wave.shape[2])
        return jax.shard_map(
            lambda *args: shards(nx, ny, [jnp.asarray(t) for t in consts], *args),
            mesh=mesh,
            in_specs=(
                P(None, ("groups", "scanx"), "scany"),
                P(None, "groups", None),
                P(("groups", "scanx", "scany", "pos"), None, None),
                P(("groups", "scanx", "scany", "pos"), None),
            ),
            out_specs=(P(None, ("groups", "scanx"), "scany"), P(None, "groups", None)),
            check_vma=False,
        )(specimen, probe_wave, amplitudes, offsets)

    return run
```

```python
import functools
import math

import jax
import jax.numpy as jnp
import numpy as np
from jax import lax
from jax.experimental import pallas as pl
from jax.experimental.pallas import tpu as pltpu
from jax.sharding import PartitionSpec as P

MESH = pl.DeviceIdType.MESH
VMEM = pltpu.VMEM


def remote(src, dst, send, recv, where):
    return pltpu.make_async_remote_copy(
        src_ref=src, dst_ref=dst, send_sem=send, recv_sem=recv, device_id=where, device_id_type=MESH
    )


def greet(conditions_devices):
    barrier = pltpu.get_barrier_semaphore()
    for present, where in conditions_devices:
        if present is True:
            pl.semaphore_signal(barrier, inc=1, device_id=where, device_id_type=MESH)
        else:

            @pl.when(present)
            def _(where=where):
                pl.semaphore_signal(barrier, inc=1, device_id=where, device_id_type=MESH)

    fixed = sum(1 for present, _ in conditions_devices if present is True)
    peers = [present.astype(jnp.int32) for present, _ in conditions_devices if present is not True]
    pl.semaphore_wait(barrier, sum(peers, fixed))


class Side:
    def __init__(self, axis, count, step):
        me = lax.axis_index(axis)
        self.has = me > 0 if step < 0 else me < count - 1
        self.where = {axis: me + step}


class Role:
    def __init__(self, q, nx, ny, order=None):
        order = q if order is None else order
        along_x = ("scanx", nx, Side("scanx", nx, -1), Side("scanx", nx, 1))
        along_y = ("scany", ny, Side("scany", ny, -1), Side("scany", ny, 1))
        one, two = (along_y, along_x) if order == 0 else (along_x, along_y)
        self.q, self.o, self.rows_first = q, 1 - q, order == 1
        self.axis1, self.n1, self.sides1 = one[0], one[1], one[2:]
        self.axis2, self.n2, self.sides2 = two[0], two[1], two[2:]
        self.me1, self.me2 = lax.axis_index(self.axis1), lax.axis_index(self.axis2)


def when(*conditions):
    return pl.when(functools.reduce(jnp.logical_and, [c for c in conditions if c is not True]))


def dot(a, b):
    return jnp.dot(a, b, preferred_element_type=jnp.float32)


class Halo:
    def __init__(self, role, spec, pad, send, recv, partner):
        self.r, self.spec, self.pad, self.partner = role, spec, pad, partner
        self.send, self.recv = send, recv
        self.direct = not role.rows_first
        tile = spec.shape[3]
        half = (pad.shape[3] - tile) // 2
        self.own = (half, tile)
        self.margins = ((0, half), (half + tile, half))
        self.edges = ((0, half), (tile - half, half))
        self.pad_edges = ((half, half), (tile, half))
        self.whole = (0, tile)

    def at(self, one, two):
        rows, cols = (one, two) if self.r.rows_first else (two, one)
        return (self.r.q, pl.ds(rows[0] // 8, rows[1] // 8), slice(None), pl.ds(*cols))

    def copy(self, src, dst, i, where):
        return remote(src, dst, self.send.at[i], self.recv.at[i], where)

    def strip1(self, m, e):
        return self.copy(
            self.spec.at[self.at(self.edges[1 - m], self.edges[e])],
            self.pad.at[self.at(self.margins[m], self.pad_edges[e])],
            2 * m + e,
            self.r.sides1[1 - m].where,
        )

    def strip2(self, m):
        return self.copy(
            self.spec.at[self.at(self.whole, self.edges[1 - m])],
            self.pad.at[self.at(self.own, self.margins[m])],
            4 + m,
            self.r.sides2[1 - m].where,
        )

    def corner(self, m1, m2):
        if self.direct:
            return self.copy(
                self.spec.at[self.at(self.edges[1 - m1], self.edges[1 - m2])],
                self.pad.at[self.at(self.margins[m1], self.margins[m2])],
                6 + 2 * m1 + m2,
                {**self.r.sides1[1 - m1].where, **self.r.sides2[1 - m2].where},
            )
        return self.copy(
            self.pad.at[self.at(self.margins[m1], self.pad_edges[1 - m2])],
            self.pad.at[self.at(self.margins[m1], self.margins[m2])],
            6 + 2 * m1 + m2,
            self.r.sides2[1 - m2].where,
        )

    def share(self, i, one, two):
        ref = self.pad.at[self.at(one, two)]
        return self.copy(ref, ref, 10 + i, self.partner)

    def share1(self, m, e):
        return self.share(2 * m + e, self.margins[m], self.pad_edges[e])

    def share2(self, m):
        return self.share(4 + m, self.own, self.margins[m])

    def share_corner(self, m1, m2):
        return self.share(6 + 2 * m1 + m2, self.margins[m1], self.margins[m2])

    def begin(self):
        r = self.r
        for m in range(2):
            for e in range(2):
                when(r.sides1[1 - m].has, r.sides2[e].has)(self.strip1(m, e).start)
        for m in range(2):
            when(r.sides2[1 - m].has)(self.strip2(m).start)
        for m in range(2):
            for e in range(2):
                when(r.sides1[1 - m].has, jnp.logical_not(r.sides2[e].has))(self.strip1(m, e).start)

    def begin_corners(self):
        r = self.r
        for m1 in range(2):
            for m2 in range(2):
                when(r.sides1[1 - m1].has, r.sides2[1 - m2].has)(self.corner(m1, m2).start)

    def relay(self):
        r = self.r
        for m1 in range(2):
            for e in range(2):

                @when(r.sides1[m1].has, r.sides2[e].has)
                def _():
                    self.strip1(m1, e).wait_recv()
                    if not self.direct:
                        self.corner(m1, 1 - e).start()
                    self.share1(m1, e).start()

        for m1 in range(2):
            for e in range(2):

                @when(r.sides1[m1].has, jnp.logical_not(r.sides2[e].has))
                def _():
                    self.strip1(m1, e).wait_recv()
                    self.share1(m1, e).start()

    def relay_second(self):
        r = self.r
        for m in range(2):

            @when(r.sides2[m].has)
            def _():
                self.strip2(m).wait_recv()
                self.share2(m).start()

    def relay_corners(self):
        r = self.r
        for m1 in range(2):
            for m2 in range(2):

                @when(r.sides1[m1].has, r.sides2[m2].has)
                def _():
                    self.corner(m1, m2).wait_recv()
                    self.share_corner(m1, m2).start()

    def arrive(self):
        r = self.r
        for m in range(2):
            for e in range(2):
                when(r.sides1[m].has)(self.share1(m, e).wait_recv)
            when(r.sides2[m].has)(self.share2(m).wait_recv)
        for m1 in range(2):
            for m2 in range(2):
                when(r.sides1[m1].has, r.sides2[m2].has)(self.share_corner(m1, m2).wait_recv)

    def finish(self):
        r = self.r
        for m in range(2):
            for e in range(2):
                when(r.sides1[1 - m].has)(self.strip1(m, e).wait_send)
                when(r.sides1[m].has)(self.share1(m, e).wait_send)
            when(r.sides2[1 - m].has)(self.strip2(m).wait_send)
            when(r.sides2[m].has)(self.share2(m).wait_send)
        for m1 in range(2):
            for m2 in range(2):
                sent = r.sides1[1 - m1].has if self.direct else r.sides1[m1].has
                when(sent, r.sides2[1 - m2].has)(self.corner(m1, m2).wait_send)
                when(r.sides1[m1].has, r.sides2[m2].has)(self.share_corner(m1, m2).wait_send)


class Fold:
    def __init__(self, role, other, mine, theirs, pair, acc, rims, core, send, recv, partner):
        self.r, self.other, self.mine, self.theirs, self.pair, self.acc = role, other, mine, theirs, pair, acc
        self.rows1, self.cols1, self.rows2, self.cols2 = rims
        self.core, self.send, self.recv, self.partner = core, send, recv, partner
        w = acc.shape[-1]
        self.w, self.q4 = w, w // 4

    def piece(self, i, r):
        q4, cols = self.q4, (slice(None),) * 3
        if r.rows_first:
            return ((pl.ds(0, 1), pl.ds(3, 1), pl.ds(1, 2))[i], slice(None), slice(None), self.columns())
        return cols + ((pl.ds(0, q4),), (pl.ds(3 * q4, q4),), (pl.ds(q4, 2 * q4),))[i]

    def columns(self):
        q4 = self.q4
        if self.r.n2 == 2 and self.r.rows_first:
            return pl.ds(pl.multiple_of((1 - self.r.me2) * q4, q4), 3 * q4)
        return pl.ds(0, self.w)

    def needed(self, i, r):
        return pl.when(r.sides1[i].has) if i < 2 else lambda f: f()

    def pair_copy(self, i, r):
        at = self.piece(i, r)
        return remote(self.theirs.at[at], self.pair.at[at], self.send.at[i], self.recv.at[i], self.partner)

    def begin(self):
        for i in range(3):
            self.needed(i, self.other)(self.pair_copy(i, self.other).start)

    def add(self, i):
        @self.needed(i, self.r)
        def _():
            self.pair_copy(i, self.r).wait_recv()
            at = self.piece(i, self.r)
            self.acc[at] = self.mine[at] + self.pair[at]

    def spot(self, stage, i, m):
        r, q4, w = self.r, self.q4, self.w
        if r.rows_first == (stage == 0):
            if stage == 1:
                return (i, slice(None), slice(None), pl.ds(q4, 2 * q4)), self.rows2.at[m]
            cols = self.columns()
            return (i, slice(None), slice(None), cols), self.rows1.at[m, :, :, cols]
        groups = pl.ds(0, 4) if stage == 0 else pl.ds(1, 2)
        return (groups, slice(None), slice(None), pl.ds(i * q4, q4)), (self.cols1 if stage == 0 else self.cols2).at[m]

    def rim_copy(self, stage, m):
        sides = self.r.sides1 if stage == 0 else self.r.sides2
        at, rim = self.spot(stage, 3 * (1 - m), m)
        i = 3 + 2 * stage + m
        return remote(self.acc.at[at], rim, self.send.at[i], self.recv.at[i], sides[1 - m].where)

    def send_rims(self, stage, only=lambda k: True):
        sides = self.r.sides1 if stage == 0 else self.r.sides2
        for m in range(2):
            when(sides[1 - m].has, only(1 - m))(self.rim_copy(stage, m).start)

    def fold(self, stage, only=lambda k: True):
        sides = self.r.sides1 if stage == 0 else self.r.sides2
        for m in range(2):

            @when(sides[m].has, only(m))
            def _():
                self.rim_copy(stage, m).wait_recv()
                at, rim = self.spot(stage, 1 + m, m)
                self.acc[at] = self.acc[at] + rim[...]

    def share_copy(self, q):
        return remote(self.core.at[q], self.core.at[q], self.send.at[7], self.recv.at[7], self.partner)

    def share(self):
        q4 = self.q4
        self.core[self.r.q] = self.acc[1:3, :, :, q4 : 3 * q4]
        self.share_copy(self.r.q).start()

    def arrive(self):
        self.share_copy(self.r.o).wait_recv()

    def finish(self):
        r = self.r
        for i in range(3):
            self.needed(i, self.other)(self.pair_copy(i, self.other).wait_send)
        for m in range(2):
            when(r.sides1[1 - m].has)(self.rim_copy(0, m).wait_send)
            when(r.sides2[1 - m].has)(self.rim_copy(1, m).wait_send)
        if self.core is not None:
            self.share_copy(r.q).wait_send()


class ProbeSum:
    PAIR, INNER, OUTER, ROW = range(4)

    def __init__(self, q, nx, ny, prob, ppair, row_in, out_in, part, hub, total, send, recv, shared, partner):
        self.q, self.ny, self.chunks = q, ny, range(recv.shape[1])
        self.shared_sems = shared
        self.prob, self.ppair, self.row_in, self.out_in = prob, ppair, row_in, out_in
        self.part, self.hub, self.total = part, hub, total
        self.send, self.recv, self.partner = send, recv, partner
        self.size = prob.shape[1] // ny
        self.rows = self.size // len(self.chunks)
        me, mid = lax.axis_index("scanx"), nx // 2
        self.lower, self.upper = me < mid, me >= mid
        step = 2 * self.lower.astype(jnp.int32) - 1
        self.inner, self.outer = {"scanx": me + step}, {"scanx": me - step}
        self.has_outer = jnp.logical_and(me > 0, me < nx - 1)
        self.is_hub = jnp.logical_or(me == mid - 1, me == mid)
        self.not_hub = jnp.logical_not(self.is_hub)
        self.is_last = jnp.logical_and(self.not_hub, jnp.logical_not(self.has_outer))
        self.not_last = jnp.logical_not(self.is_last)
        near_end = jnp.logical_or(me == 1, me == nx - 2)
        self.outer_last = jnp.logical_and(self.has_outer, near_end)
        self.first_direct = len(self.chunks) - len(self.chunks) * 4 // 8
        self.mine = lax.axis_index("scany")

    def column(self, d):
        return lax.rem(self.mine + d, self.ny)

    def origin(self, d):
        return lax.rem(self.mine - d + self.ny, self.ny)

    def at(self, h, c):
        if isinstance(h, int):
            return pl.ds(h * self.size + c * self.rows, self.rows)
        return pl.ds(pl.multiple_of(h * self.size + c * self.rows, 8), self.rows)

    def copy(self, src, dst, s, r, c, where):
        return remote(src, dst, self.send.at[s], self.recv.at[r, c], where)

    def pair(self, h, c):
        at = self.at(h, c)
        return self.copy(self.prob.at[1 - self.q, at], self.ppair.at[at], self.PAIR, self.PAIR, c, self.partner)

    def to_owner(self, d, c):
        to = self.column(d)
        src, dst = self.ppair.at[self.at(to, c)], self.row_in.at[self.mine, self.at(0, c)]
        return self.copy(src, dst, self.ROW + d - 1, self.ROW + d - 1, c, {"scany": to})

    def pass_in(self, c):
        at = self.at(0, c)
        return self.copy(self.part.at[at], self.out_in.at[at], self.INNER, self.INNER, c, self.inner)

    def between_hubs(self, c):
        at = self.at(0, c)
        return self.copy(self.part.at[at], self.hub.at[at], self.INNER, self.OUTER, c, self.inner)

    def pass_out(self, c):
        src, dst = self.total.at[self.q, self.at(self.mine, c)], self.hub.at[self.at(0, c)]
        return self.copy(src, dst, self.OUTER, self.OUTER, c, self.outer)

    def to_row(self, d, c):
        ref = self.total.at[self.q, self.at(self.mine, c)]
        return self.copy(ref, ref, self.ROW + self.ny + d - 2, self.ROW + self.ny + d - 2, c, {"scany": self.column(d)})

    def to_end(self, d, c):
        ref = self.total.at[self.q, self.at(self.mine, c)]
        where = {"scanx": self.outer["scanx"], "scany": self.column(d)}
        return remote(ref, ref, self.shared_sems.at[1 + d], self.recv.at[self.ROW + self.ny + d - 2, c], where)

    def share(self, d, c, q):
        ref = self.total.at[q, self.at(self.origin(d), c)]
        return remote(ref, ref, self.shared_sems.at[0], self.shared_sems.at[1], self.partner)

    def wait(self, ref, r, c):
        self.copy(ref, ref, self.PAIR, r, c, self.partner).wait_recv()

    def one(self):
        for c in self.chunks:
            self.wait(self.ppair.at[pl.ds(0, self.ny * self.rows)], self.PAIR, c)
            for h in range(self.ny):
                at = self.at(h, c)
                self.ppair[at] = self.prob[self.q, at] + self.ppair[at]
            for d in range(1, self.ny):
                self.to_owner(d, c).start()

    def two(self):
        for c in self.chunks:
            at = self.at(0, c)
            value = self.ppair[self.at(self.mine, c)]
            for d in range(1, self.ny):
                slot = self.row_in.at[self.origin(d), at]
                self.wait(slot, self.ROW + d - 1, c)
                value = value + slot[...]
            self.part[at] = value

            @pl.when(self.has_outer)
            def _():
                slot = self.out_in.at[at]
                self.wait(slot, self.INNER, c)
                self.part[at] = self.part[at] + slot[...]

            pl.when(self.is_hub)(self.between_hubs(c).start)
            pl.when(self.not_hub)(self.pass_in(c).start)

    def inward(self, k):
        return self.upper if k == 0 else self.lower

    def late(self, k):
        return jnp.logical_and(self.inward(k), self.not_hub)

    def early(self, k):
        return jnp.logical_not(self.late(k))

    def three(self, chunks):
        for c in chunks:
            at, mine = self.at(0, c), self.at(self.mine, c)
            self.wait(self.hub.at[at], self.OUTER, c)

            @pl.when(self.is_hub)
            def _():
                self.total[self.q, mine] = self.part[at] + self.hub[at]

            @pl.when(self.not_hub)
            def _():
                self.total[self.q, mine] = self.hub[at]

            pl.when(self.has_outer)(self.pass_out(c).start)
            for d in range(1, self.ny):
                if c < self.first_direct:
                    self.to_row(d, c).start()
                else:
                    pl.when(self.outer_last)(self.to_end(d, c).start)
                    pl.when(self.not_last)(self.to_row(d, c).start)
            self.share(0, c, self.q).start()

    def four(self):
        for c in self.chunks:
            for d in range(1, self.ny):
                self.wait(self.total.at[self.q, self.at(self.origin(d), c)], self.ROW + self.ny + d - 2, c)
                self.share(d, c, self.q).start()

    def shared(self):
        ref = self.total.at[1 - self.q]
        remote(ref, ref, self.shared_sems.at[0], self.shared_sems.at[1], self.partner).wait_recv()

    def end(self):
        def sent(ref, stage):
            remote(ref, ref, self.send.at[stage], self.recv.at[0, 0], self.partner).wait_send()

        sent(self.ppair, self.PAIR)
        ref = self.total.at[self.q]
        remote(ref, ref, self.shared_sems.at[0], self.shared_sems.at[1], self.partner).wait_send()
        sent(self.part, self.INNER)
        pl.when(self.has_outer)(functools.partial(sent, self.part, self.OUTER))
        for d in range(1, self.ny):
            sent(self.part, self.ROW + d - 1)
            first = self.first_direct * self.rows
            stage = self.ROW + self.ny + d - 2
            pl.when(self.not_last)(functools.partial(sent, self.part, stage))
            pl.when(self.is_last)(functools.partial(sent, self.part.at[pl.ds(0, first)], stage))

            @pl.when(self.outer_last)
            def _():
                ref = self.part.at[pl.ds(0, self.size - first)]
                remote(ref, ref, self.shared_sems.at[1 + d], self.recv.at[0, 0], self.partner).wait_send()


def near_greet(ny, partner, rows):
    my = lax.axis_index("scany")
    greet(
        [(True, partner)]
        + [(True, {"scany": lax.rem(my + d, ny)}) for d in range(1, ny)]
        + [(side.has, side.where) for side in rows]
    )


def row_ready(sem, rows):
    for i, side in enumerate(rows):

        @pl.when(side.has)
        def _(i=i, side=side):
            pl.semaphore_signal(sem.at[1 - i], inc=1, device_id=side.where, device_id_type=MESH)


def row_wait(sem, rows):
    for i, side in enumerate(rows):
        pl.when(side.has)(functools.partial(pl.semaphore_wait, sem.at[i], 1))


def each(step):
    p = lax.axis_index("pos")
    for q in range(2):
        pl.when(p == q)(functools.partial(step, q))


class Placer:
    def __init__(self, offsets, bufs, m, positions):
        self.bufs, self.m = bufs, m
        self.tall, self.span = m + 8, m + 128
        self.top = (bufs.shape[2] - self.tall // 8) // 2
        self.spots = []
        for j in range(positions):
            row, col = offsets[j, 0], offsets[j, 1]
            self.spots.append((lax.rem(row, 8), lax.rem(col, 128), lax.div(row, 8), lax.div(col, 128)))

    def clear(self):
        n, k, rows = self.bufs.shape[:3]
        bottom = self.top + self.tall // 8
        for j in range(n):
            for c in range(k):
                self.bufs[j, c, 0 : self.top] = jnp.zeros((self.top, *self.bufs.shape[3:]), jnp.float32)
                self.bufs[j, c, bottom:rows] = jnp.zeros((rows - bottom, *self.bufs.shape[3:]), jnp.float32)

    def put(self, j, k, term):
        row_in, col_in, _, step = self.spots[j]
        m, wide = self.m, self.bufs.shape[4]
        blank_rows = jnp.zeros((self.tall - m, m), jnp.float32)
        blank_cols = jnp.zeros((self.tall, self.span - m), jnp.float32)
        moved = pltpu.roll(jnp.concatenate([term, blank_rows], 0), row_in, 0)
        moved = pltpu.roll(jnp.concatenate([moved, blank_cols], 1), col_in, 1)
        out = None
        for d in range((wide - self.span) // 128 + 1):
            parts = [jnp.zeros((self.tall, w), jnp.float32) for w in (128 * d, wide - self.span - 128 * d)]
            here = jnp.concatenate([x for x in (parts[0], moved, parts[1]) if x.shape[1]], 1)
            out = here if out is None else jnp.where(step == d, here, out)
        self.bufs[j, k, self.top : self.top + self.tall // 8] = out.reshape(self.tall // 8, 8, wide)

    def rows(self, k, r0, count):
        out = None
        for j, (_, _, row, _) in enumerate(self.spots):
            part = self.bufs[j, k, pl.ds(self.top - row + r0 // 8, count // 8)]
            out = part if out is None else out + part
        return out.reshape(count, self.bufs.shape[4])

    def window(self, j, pad, k):
        row_in, col_in, row, step = self.spots[j]
        wide = pad.shape[3]
        block = pad[k, pl.ds(row, self.tall // 8)].reshape(self.tall, wide)
        out = block[:, : self.span]
        for d in range(1, (wide - self.span) // 128 + 1):
            out = jnp.where(step == d, block[:, 128 * d : 128 * d + self.span], out)
        out = pltpu.roll(out, lax.rem(self.span - col_in, self.span), 1)[:, : self.m]
        return pltpu.roll(out, lax.rem(self.tall - row_in, self.tall), 0)[: self.m]


def forward(window, pr, pi, table_a, table_b):
    m = pr.shape[0]
    bf = jnp.bfloat16
    ar, ai = window
    er = pr * ar - pi * ai
    ei = pr * ai + pi * ar
    left = dot(table_a[...], jnp.concatenate([er.astype(bf), ei.astype(bf)], 0)).astype(bf)
    return er, ei, dot(jnp.concatenate([left[:m], left[m:]], 1), table_b[...])


def backward(er, ei, far, amplitude, table_a, table_b):
    m = er.shape[0]
    bf = jnp.bfloat16
    fr, fi = far[:, :m], far[:, m:]
    ratio = amplitude.astype(jnp.float32) / jnp.maximum(jnp.sqrt(fr * fr + fi * fi), 0.2)
    projected = jnp.concatenate([(fr * ratio).astype(bf), (fi * ratio).astype(bf)], 0)
    back_half = dot(table_b[...], projected).astype(bf)
    back = dot(jnp.concatenate([back_half[:m], back_half[m:]], 1), table_a[...])
    return back[:, :m] - er, back[:, m:] - ei


def whole_kernel(nx, ny, step_size, *refs):
    offsets, spec, *given = refs[:6]
    new_spec, new_probe = refs[6:8]
    pad, probe, amplitudes, table_a, table_b, bufs, grad, prob, total, light_all = refs[8:18]
    pair, acc, xr2, zr1, ipair, iacc, ixr, izr, ppair, row_in, out_in, part, hub = refs[18:31]
    hsend, hrecv, local, gsend, grecv, isend, irecv, psend, precv, ssems, ready = refs[31:]
    tile, m = spec.shape[3], probe.shape[1]
    wide = pad.shape[3]
    half = (wide - tile) // 2
    h = grad.shape[3]
    positions, chunks = amplitudes.shape[0], precv.shape[1]
    p = lax.axis_index("pos")
    partner = {"pos": 1 - p}
    loads = [pltpu.make_async_copy(spec, pad.at[:, pl.ds(half // 8, tile // 8), :, pl.ds(half, tile)], local.at[0])]
    for i, (src, dst) in enumerate(zip(given, (probe, amplitudes, table_a, table_b)), 1):
        loads.append(pltpu.make_async_copy(src, dst, local.at[i]))
    for c in loads:
        c.start()
    roles = [Role(q, nx, ny) for q in range(2)]
    sides = roles[1].sides1 + roles[0].sides1
    near_greet(ny, partner, roles[1].sides1)
    halos = [Halo(r, spec, pad, hsend, hrecv, partner) for r in roles]
    role = Role(p, nx, ny, 1)
    fold = Fold(role, role, grad.at[p], grad.at[1 - p], pair, acc, (zr1, None, None, xr2), None, gsend, grecv, partner)
    light = Fold(
        role,
        role,
        grad.at[2, :, pl.ds(p, 1)],
        grad.at[2, :, pl.ds(1 - p, 1)],
        ipair,
        iacc,
        (izr, None, None, ixr),
        light_all,
        isend,
        irecv,
        partner,
    )
    probe_sum = ProbeSum(p, nx, ny, prob, ppair, row_in, out_in, part, hub, total, psend, precv, ssems, partner)
    placer = Placer(offsets, bufs, m, positions)

    def gather(k):
        for g in range(4):
            for b in range(2):
                grad[k, g, b] = placer.rows(k, (2 * g + b) * h, h)

    rows = roles[1].sides1
    pl.when(p == 0)(functools.partial(row_ready, ready, rows))
    each(lambda q: halos[q].begin())
    for i, at in enumerate(
        (
            (slice(None), pl.ds(0, half // 8)),
            (slice(None), pl.ds((half + tile) // 8, half // 8)),
            (slice(None), slice(None), slice(None), pl.ds(0, half)),
            (slice(None), slice(None), slice(None), pl.ds(half + tile, half)),
        )
    ):

        @pl.when(jnp.logical_not(sides[i].has))
        def _(at=at):
            pad[at] = jnp.zeros(pad.at[at].shape, pad.dtype)

    placer.clear()

    @pl.when(p == 0)
    def _():
        row_wait(ready, rows)
        halos[0].begin_corners()

    loads[1].wait()
    power = probe[0] * probe[0] + probe[1] * probe[1]
    for j in range(positions):
        placer.put(j, 2, power)
    gather(2)
    light.begin()

    def strips(q):
        halos[q].relay()

    def corners(q):
        halos[q].relay_second()
        halos[q].relay_corners()
        halos[1 - q].arrive()

    for i in range(3):
        light.add(i)
    light.send_rims(0)
    each(strips)
    each(corners)
    for c in loads[:1] + loads[2:]:
        c.wait()
    pr, pi = probe[0], probe[1]
    windows = [[placer.window(j, pad, k) for k in range(2)] for j in range(positions)]
    fields = [forward(windows[j], pr, pi, table_a, table_b) for j in range(positions)]
    light.fold(0)
    light.send_rims(1)
    diffs = [backward(*fields[j], amplitudes[j], table_a, table_b) for j in range(positions)]
    sums = [None, None]
    for (ar, ai), (dr, di) in zip(windows, diffs):
        for k, t in enumerate((ar * dr + ai * di, ar * di - ai * dr)):
            sums[k] = t if sums[k] is None else sums[k] + t
    for c in range(chunks):
        for part_of in range(ny):
            at = probe_sum.at(part_of, c)
            for k in range(2):
                prob[k, at] = sums[k][at.start : at.start + at.size]
            probe_sum.pair(part_of, c).start()
    for j, (dr, di) in enumerate(diffs):
        placer.put(j, 0, pr * dr + pi * di)
        placer.put(j, 1, pr * di - pi * dr)
    gather(1 - p)
    fold.begin()
    gather(p)

    def share_copy(q):
        return remote(new_spec.at[q], new_spec.at[q], gsend.at[7], grecv.at[7], partner)

    probe_sum.one()
    fold.add(0)
    fold.add(1)
    fold.send_rims(0, probe_sum.early)
    fold.add(2)
    light.fold(1)
    light.share()
    probe_sum.two()
    fold.send_rims(0, probe_sum.late)

    def strips_in():
        fold.fold(0)
        fold.send_rims(1)

    pl.when(jnp.logical_not(probe_sum.has_outer))(strips_in)
    probe_sum.three(range(chunks - chunks // 4))
    pl.when(probe_sum.has_outer)(strips_in)
    probe_sum.three(range(chunks - chunks // 4, chunks))
    light.arrive()
    fold.fold(1)
    q4 = fold.q4
    for g in range(2):
        for b in range(2):
            r0 = (2 * g + b) * h
            old = pad[p, (half + r0) // 8 : (half + r0 + h) // 8, :, half : half + tile].reshape(h, tile)
            new_spec[p, r0 : r0 + h] = old + acc[1 + g, b, :, q4 : 3 * q4] / (light_all[b, g, 0] + 1.0)
    share_copy(p).start()
    probe_sum.four()
    probe_sum.shared()
    share_copy(1 - p).wait_recv()
    share_copy(p).wait_send()
    light.finish()
    fold.finish()
    probe_sum.end()
    each(lambda q: halos[q].finish())
    for k in range(2):
        new_probe[k] = probe[k] + total[k] * step_size


def emit_kernel(spec, probe, new_spec, new_probe, sem):
    copies = [
        pltpu.make_async_copy(src.at[k, at], dst.at[k, at], sem.at[i, k, j])
        for i, (src, dst) in enumerate(((spec, new_spec), (probe, new_probe)))
        for k in range(2)
        for j, at in enumerate((pl.ds(0, src.shape[1] // 2), pl.ds(src.shape[1] // 2, src.shape[1] // 2)))
    ]
    for c in copies:
        c.start()
    for c in copies:
        c.wait()


def tables(length):
    index = np.arange(length)
    angle = ((index[:, None] * index[None, :]) % length).astype(np.float32) * np.float32(2.0 * math.pi / length)
    scale = np.float32(1.0 / math.sqrt(length))
    c = np.cos(angle) * scale
    s = np.sin(angle) * scale
    a = np.block([[c, s], [-s, c]]).astype(jnp.bfloat16)
    b = np.block([[c, -s], [s, c]]).astype(jnp.bfloat16)
    return a, b


def shards(nx, ny, consts, specimen, probe_wave, amplitudes, offsets):
    m = probe_wave.shape[1]
    tile = specimen.shape[1]
    wide = tile + m
    f32 = jnp.float32
    vm = pl.BlockSpec(memory_space=VMEM)
    sm = pl.BlockSpec(memory_space=pltpu.SMEM)
    hbm = pl.BlockSpec(memory_space=pltpu.HBM)
    dma = pltpu.SemaphoreType.DMA
    n = nx * ny
    h = wide // 8
    chunks = 8
    positions = offsets.shape[0]
    held = (probe_wave, amplitudes, consts[0], consts[1])

    step_size = 1.0 / math.sqrt(positions * n * 2)
    results = pl.pallas_call(
        functools.partial(whole_kernel, nx, ny, step_size),
        out_shape=[VMEM(specimen.shape, f32), VMEM(probe_wave.shape, f32)],
        in_specs=[sm] + [hbm] * 5,
        out_specs=[vm, vm],
        scratch_shapes=[
            VMEM((2, wide // 8, 8, wide), f32),
            *[VMEM(x.shape, x.dtype) for x in held],
            VMEM((positions, 3, (2 * (tile - 8) + m + 8) // 8, 8, wide), f32),
            VMEM((3, 4, 2, h, wide), f32),
            VMEM((2, m, m), f32),
            VMEM((2, m, m), f32),
            VMEM((2, 2, 1, h, wide // 2), f32),
            VMEM((4, 2, h, wide), f32),
            VMEM((4, 2, h, wide), f32),
            VMEM((2, 2, 2, h, wide // 4), f32),
            VMEM((2, 2, h, wide), f32),
            VMEM((4, 1, h, wide), f32),
            VMEM((4, 1, h, wide), f32),
            VMEM((2, 2, 1, h, wide // 4), f32),
            VMEM((2, 1, h, wide), f32),
            VMEM((m, m), f32),
            VMEM((ny, m // ny, m), f32),
            VMEM((m // ny, m), f32),
            VMEM((m // ny, m), f32),
            VMEM((m // ny, m), f32),
            dma((20,)),
            dma((20,)),
            dma((5,)),
            dma((8,)),
            dma((8,)),
            dma((8,)),
            dma((8,)),
            dma((1 + 2 * ny,)),
            dma((1 + 2 * ny, chunks)),
            dma((1 + ny,)),
            pltpu.SemaphoreType.REGULAR((2,)),
        ],
        compiler_params=pltpu.CompilerParams(vmem_limit_bytes=56 * 2**20, collective_id=0, has_side_effects=True),
        name="whole",
    )(offsets, *[pltpu.with_memory_space_constraint(x, pltpu.HBM) for x in (specimen.reshape(2, tile // 8, 8, tile), *held)])
    return pl.pallas_call(
        emit_kernel,
        out_shape=[jax.ShapeDtypeStruct(specimen.shape, f32), jax.ShapeDtypeStruct(probe_wave.shape, f32)],
        in_specs=[vm] * 2,
        out_specs=[pl.BlockSpec(memory_space=pl.ANY)] * 2,
        scratch_shapes=[dma((2, 2, 2))],
        compiler_params=pltpu.CompilerParams(vmem_limit_bytes=2 * 2**20),
        name="emit",
    )(*results)


def solution(mesh):
    nx, ny = mesh.shape["scanx"], mesh.shape["scany"]

    def run(specimen, probe_wave, amplitudes, offsets):
        consts = tables(probe_wave.shape[2])
        return jax.shard_map(
            lambda *args: shards(nx, ny, [jnp.asarray(t) for t in consts], *args),
            mesh=mesh,
            in_specs=(
                P(None, ("groups", "scanx"), "scany"),
                P(None, "groups", None),
                P(("groups", "scanx", "scany", "pos"), None, None),
                P(("groups", "scanx", "scany", "pos"), None),
            ),
            out_specs=(P(None, ("groups", "scanx"), "scany"), P(None, "groups", None)),
            check_vma=False,
        )(specimen, probe_wave, amplitudes, offsets)

    return run
```

```python
import functools
import math

import jax
import jax.numpy as jnp
import numpy as np
from jax import lax
from jax.experimental import pallas as pl
from jax.experimental.pallas import tpu as pltpu
from jax.sharding import PartitionSpec as P

MESH = pl.DeviceIdType.MESH
VMEM = pltpu.VMEM


def remote(src, dst, send, recv, where):
    return pltpu.make_async_remote_copy(
        src_ref=src, dst_ref=dst, send_sem=send, recv_sem=recv, device_id=where, device_id_type=MESH
    )


def greet(conditions_devices):
    barrier = pltpu.get_barrier_semaphore()
    for present, where in conditions_devices:
        if present is True:
            pl.semaphore_signal(barrier, inc=1, device_id=where, device_id_type=MESH)
        else:

            @pl.when(present)
            def _(where=where):
                pl.semaphore_signal(barrier, inc=1, device_id=where, device_id_type=MESH)

    fixed = sum(1 for present, _ in conditions_devices if present is True)
    peers = [present.astype(jnp.int32) for present, _ in conditions_devices if present is not True]
    pl.semaphore_wait(barrier, sum(peers, fixed))


class Side:
    def __init__(self, axis, count, step):
        me = lax.axis_index(axis)
        self.has = me > 0 if step < 0 else me < count - 1
        self.where = {axis: me + step}


class Role:
    def __init__(self, q, nx, ny, order=None):
        order = q if order is None else order
        along_x = ("scanx", nx, Side("scanx", nx, -1), Side("scanx", nx, 1))
        along_y = ("scany", ny, Side("scany", ny, -1), Side("scany", ny, 1))
        one, two = (along_y, along_x) if order == 0 else (along_x, along_y)
        self.q, self.o, self.rows_first = q, 1 - q, order == 1
        self.axis1, self.n1, self.sides1 = one[0], one[1], one[2:]
        self.axis2, self.n2, self.sides2 = two[0], two[1], two[2:]
        self.me1, self.me2 = lax.axis_index(self.axis1), lax.axis_index(self.axis2)


def when(*conditions):
    return pl.when(functools.reduce(jnp.logical_and, [c for c in conditions if c is not True]))


def dot(a, b):
    return jnp.dot(a, b, preferred_element_type=jnp.float32)


class Halo:
    def __init__(self, role, spec, pad, send, recv, partner):
        self.r, self.spec, self.pad, self.partner = role, spec, pad, partner
        self.send, self.recv = send, recv
        self.direct = not role.rows_first
        tile = spec.shape[3]
        half = (pad.shape[3] - tile) // 2
        self.own = (half, tile)
        self.margins = ((0, half), (half + tile, half))
        self.edges = ((0, half), (tile - half, half))
        self.pad_edges = ((half, half), (tile, half))
        self.whole = (0, tile)

    def at(self, one, two):
        rows, cols = (one, two) if self.r.rows_first else (two, one)
        return (self.r.q, pl.ds(rows[0] // 8, rows[1] // 8), slice(None), pl.ds(*cols))

    def copy(self, src, dst, i, where):
        return remote(src, dst, self.send.at[i], self.recv.at[i], where)

    def strip1(self, m, e):
        return self.copy(
            self.spec.at[self.at(self.edges[1 - m], self.edges[e])],
            self.pad.at[self.at(self.margins[m], self.pad_edges[e])],
            2 * m + e,
            self.r.sides1[1 - m].where,
        )

    def strip2(self, m):
        return self.copy(
            self.spec.at[self.at(self.whole, self.edges[1 - m])],
            self.pad.at[self.at(self.own, self.margins[m])],
            4 + m,
            self.r.sides2[1 - m].where,
        )

    def corner(self, m1, m2):
        if self.direct:
            return self.copy(
                self.spec.at[self.at(self.edges[1 - m1], self.edges[1 - m2])],
                self.pad.at[self.at(self.margins[m1], self.margins[m2])],
                6 + 2 * m1 + m2,
                {**self.r.sides1[1 - m1].where, **self.r.sides2[1 - m2].where},
            )
        return self.copy(
            self.pad.at[self.at(self.margins[m1], self.pad_edges[1 - m2])],
            self.pad.at[self.at(self.margins[m1], self.margins[m2])],
            6 + 2 * m1 + m2,
            self.r.sides2[1 - m2].where,
        )

    def share(self, i, one, two):
        ref = self.pad.at[self.at(one, two)]
        return self.copy(ref, ref, 10 + i, self.partner)

    def share1(self, m, e):
        return self.share(2 * m + e, self.margins[m], self.pad_edges[e])

    def share2(self, m):
        return self.share(4 + m, self.own, self.margins[m])

    def share_corner(self, m1, m2):
        return self.share(6 + 2 * m1 + m2, self.margins[m1], self.margins[m2])

    def begin(self):
        r = self.r
        for m in range(2):
            for e in range(2):
                when(r.sides1[1 - m].has, r.sides2[e].has)(self.strip1(m, e).start)
        for m in range(2):
            when(r.sides2[1 - m].has)(self.strip2(m).start)
        for m in range(2):
            for e in range(2):
                when(r.sides1[1 - m].has, jnp.logical_not(r.sides2[e].has))(self.strip1(m, e).start)

    def begin_corners(self):
        r = self.r
        for m1 in range(2):
            for m2 in range(2):
                when(r.sides1[1 - m1].has, r.sides2[1 - m2].has)(self.corner(m1, m2).start)

    def relay(self):
        r = self.r
        for m1 in range(2):
            for e in range(2):

                @when(r.sides1[m1].has, r.sides2[e].has)
                def _():
                    self.strip1(m1, e).wait_recv()
                    if not self.direct:
                        self.corner(m1, 1 - e).start()
                    self.share1(m1, e).start()

        for m1 in range(2):
            for e in range(2):

                @when(r.sides1[m1].has, jnp.logical_not(r.sides2[e].has))
                def _():
                    self.strip1(m1, e).wait_recv()
                    self.share1(m1, e).start()

    def relay_second(self):
        r = self.r
        for m in range(2):

            @when(r.sides2[m].has)
            def _():
                self.strip2(m).wait_recv()
                self.share2(m).start()

    def relay_corners(self):
        r = self.r
        for m1 in range(2):
            for m2 in range(2):

                @when(r.sides1[m1].has, r.sides2[m2].has)
                def _():
                    self.corner(m1, m2).wait_recv()
                    self.share_corner(m1, m2).start()

    def arrive(self):
        r = self.r
        for m in range(2):
            for e in range(2):
                when(r.sides1[m].has)(self.share1(m, e).wait_recv)
            when(r.sides2[m].has)(self.share2(m).wait_recv)
        for m1 in range(2):
            for m2 in range(2):
                when(r.sides1[m1].has, r.sides2[m2].has)(self.share_corner(m1, m2).wait_recv)

    def finish(self):
        r = self.r
        for m in range(2):
            for e in range(2):
                when(r.sides1[1 - m].has)(self.strip1(m, e).wait_send)
                when(r.sides1[m].has)(self.share1(m, e).wait_send)
            when(r.sides2[1 - m].has)(self.strip2(m).wait_send)
            when(r.sides2[m].has)(self.share2(m).wait_send)
        for m1 in range(2):
            for m2 in range(2):
                sent = r.sides1[1 - m1].has if self.direct else r.sides1[m1].has
                when(sent, r.sides2[1 - m2].has)(self.corner(m1, m2).wait_send)
                when(r.sides1[m1].has, r.sides2[m2].has)(self.share_corner(m1, m2).wait_send)


class Fold:
    def __init__(self, role, other, mine, theirs, pair, acc, rims, core, send, recv, partner):
        self.r, self.other, self.mine, self.theirs, self.pair, self.acc = role, other, mine, theirs, pair, acc
        self.rows1, self.cols1, self.rows2, self.cols2 = rims
        self.core, self.send, self.recv, self.partner = core, send, recv, partner
        w = acc.shape[-1]
        self.w, self.q4 = w, w // 4

    def piece(self, i, r):
        q4, cols = self.q4, (slice(None),) * 3
        if r.rows_first:
            return ((pl.ds(0, 1), pl.ds(3, 1), pl.ds(1, 2))[i], slice(None), slice(None), self.columns())
        return cols + ((pl.ds(0, q4),), (pl.ds(3 * q4, q4),), (pl.ds(q4, 2 * q4),))[i]

    def columns(self):
        q4 = self.q4
        if self.r.n2 == 2 and self.r.rows_first:
            return pl.ds(pl.multiple_of((1 - self.r.me2) * q4, q4), 3 * q4)
        return pl.ds(0, self.w)

    def needed(self, i, r):
        return pl.when(r.sides1[i].has) if i < 2 else lambda f: f()

    def pair_copy(self, i, r):
        at = self.piece(i, r)
        return remote(self.theirs.at[at], self.pair.at[at], self.send.at[i], self.recv.at[i], self.partner)

    def begin(self):
        for i in range(3):
            self.needed(i, self.other)(self.pair_copy(i, self.other).start)

    def add(self, i):
        @self.needed(i, self.r)
        def _():
            self.pair_copy(i, self.r).wait_recv()
            at = self.piece(i, self.r)
            self.acc[at] = self.mine[at] + self.pair[at]

    def spot(self, stage, i, m):
        r, q4, w = self.r, self.q4, self.w
        if r.rows_first == (stage == 0):
            if stage == 1:
                return (i, slice(None), slice(None), pl.ds(q4, 2 * q4)), self.rows2.at[m]
            cols = self.columns()
            return (i, slice(None), slice(None), cols), self.rows1.at[m, :, :, cols]
        groups = pl.ds(0, 4) if stage == 0 else pl.ds(1, 2)
        return (groups, slice(None), slice(None), pl.ds(i * q4, q4)), (self.cols1 if stage == 0 else self.cols2).at[m]

    def rim_copy(self, stage, m):
        sides = self.r.sides1 if stage == 0 else self.r.sides2
        at, rim = self.spot(stage, 3 * (1 - m), m)
        i = 3 + 2 * stage + m
        return remote(self.acc.at[at], rim, self.send.at[i], self.recv.at[i], sides[1 - m].where)

    def send_rims(self, stage, only=lambda k: True):
        sides = self.r.sides1 if stage == 0 else self.r.sides2
        for m in range(2):
            when(sides[1 - m].has, only(1 - m))(self.rim_copy(stage, m).start)

    def fold(self, stage, only=lambda k: True):
        sides = self.r.sides1 if stage == 0 else self.r.sides2
        for m in range(2):

            @when(sides[m].has, only(m))
            def _():
                self.rim_copy(stage, m).wait_recv()
                at, rim = self.spot(stage, 1 + m, m)
                self.acc[at] = self.acc[at] + rim[...]

    def share_copy(self, q):
        return remote(self.core.at[q], self.core.at[q], self.send.at[7], self.recv.at[7], self.partner)

    def share(self):
        q4 = self.q4
        self.core[self.r.q] = self.acc[1:3, :, :, q4 : 3 * q4]
        self.share_copy(self.r.q).start()

    def arrive(self):
        self.share_copy(self.r.o).wait_recv()

    def finish(self):
        r = self.r
        for i in range(3):
            self.needed(i, self.other)(self.pair_copy(i, self.other).wait_send)
        for m in range(2):
            when(r.sides1[1 - m].has)(self.rim_copy(0, m).wait_send)
            when(r.sides2[1 - m].has)(self.rim_copy(1, m).wait_send)
        if self.core is not None:
            self.share_copy(r.q).wait_send()


class ProbeSum:
    PAIR, INNER, OUTER, ROW = range(4)

    def __init__(self, q, nx, ny, prob, ppair, row_in, out_in, part, hub, total, send, recv, shared, partner):
        self.q, self.ny, self.chunks = q, ny, range(recv.shape[1])
        self.shared_sems = shared
        self.prob, self.ppair, self.row_in, self.out_in = prob, ppair, row_in, out_in
        self.part, self.hub, self.total = part, hub, total
        self.send, self.recv, self.partner = send, recv, partner
        self.size = prob.shape[1] // ny
        self.rows = self.size // len(self.chunks)
        me, mid = lax.axis_index("scanx"), nx // 2
        self.lower, self.upper = me < mid, me >= mid
        step = 2 * self.lower.astype(jnp.int32) - 1
        self.inner, self.outer = {"scanx": me + step}, {"scanx": me - step}
        self.has_outer = jnp.logical_and(me > 0, me < nx - 1)
        self.is_hub = jnp.logical_or(me == mid - 1, me == mid)
        self.not_hub = jnp.logical_not(self.is_hub)
        self.is_last = jnp.logical_and(self.not_hub, jnp.logical_not(self.has_outer))
        self.not_last = jnp.logical_not(self.is_last)
        near_end = jnp.logical_or(me == 1, me == nx - 2)
        self.outer_last = jnp.logical_and(self.has_outer, near_end)
        self.first_direct = len(self.chunks) - len(self.chunks) * 4 // 8
        self.mine = lax.axis_index("scany")

    def column(self, d):
        return lax.rem(self.mine + d, self.ny)

    def origin(self, d):
        return lax.rem(self.mine - d + self.ny, self.ny)

    def at(self, h, c):
        if isinstance(h, int):
            return pl.ds(h * self.size + c * self.rows, self.rows)
        return pl.ds(pl.multiple_of(h * self.size + c * self.rows, 8), self.rows)

    def copy(self, src, dst, s, r, c, where):
        return remote(src, dst, self.send.at[s], self.recv.at[r, c], where)

    def pair(self, h, c):
        at = self.at(h, c)
        return self.copy(self.prob.at[1 - self.q, at], self.ppair.at[at], self.PAIR, self.PAIR, c, self.partner)

    def to_owner(self, d, c):
        to = self.column(d)
        src, dst = self.ppair.at[self.at(to, c)], self.row_in.at[self.mine, self.at(0, c)]
        return self.copy(src, dst, self.ROW + d - 1, self.ROW + d - 1, c, {"scany": to})

    def pass_in(self, c):
        at = self.at(0, c)
        return self.copy(self.part.at[at], self.out_in.at[at], self.INNER, self.INNER, c, self.inner)

    def between_hubs(self, c):
        at = self.at(0, c)
        return self.copy(self.part.at[at], self.hub.at[at], self.INNER, self.OUTER, c, self.inner)

    def pass_out(self, c):
        src, dst = self.total.at[self.q, self.at(self.mine, c)], self.hub.at[self.at(0, c)]
        return self.copy(src, dst, self.OUTER, self.OUTER, c, self.outer)

    def to_row(self, d, c):
        ref = self.total.at[self.q, self.at(self.mine, c)]
        return self.copy(ref, ref, self.ROW + self.ny + d - 2, self.ROW + self.ny + d - 2, c, {"scany": self.column(d)})

    def to_end(self, d, c):
        ref = self.total.at[self.q, self.at(self.mine, c)]
        where = {"scanx": self.outer["scanx"], "scany": self.column(d)}
        return remote(ref, ref, self.shared_sems.at[1 + d], self.recv.at[self.ROW + self.ny + d - 2, c], where)

    def share(self, d, c, q):
        ref = self.total.at[q, self.at(self.origin(d), c)]
        return remote(ref, ref, self.shared_sems.at[0], self.shared_sems.at[1], self.partner)

    def wait(self, ref, r, c):
        self.copy(ref, ref, self.PAIR, r, c, self.partner).wait_recv()

    def one(self):
        for c in self.chunks:
            self.wait(self.ppair.at[pl.ds(0, self.ny * self.rows)], self.PAIR, c)
            for h in range(self.ny):
                at = self.at(h, c)
                self.ppair[at] = self.prob[self.q, at] + self.ppair[at]
            for d in range(1, self.ny):
                self.to_owner(d, c).start()

    def two(self):
        for c in self.chunks:
            at = self.at(0, c)
            value = self.ppair[self.at(self.mine, c)]
            for d in range(1, self.ny):
                slot = self.row_in.at[self.origin(d), at]
                self.wait(slot, self.ROW + d - 1, c)
                value = value + slot[...]
            self.part[at] = value

            @pl.when(self.has_outer)
            def _():
                slot = self.out_in.at[at]
                self.wait(slot, self.INNER, c)
                self.part[at] = self.part[at] + slot[...]

            pl.when(self.is_hub)(self.between_hubs(c).start)
            pl.when(self.not_hub)(self.pass_in(c).start)

    def inward(self, k):
        return self.upper if k == 0 else self.lower

    def late(self, k):
        return jnp.logical_and(self.inward(k), self.not_hub)

    def early(self, k):
        return jnp.logical_not(self.late(k))

    def three(self, chunks):
        for c in chunks:
            at, mine = self.at(0, c), self.at(self.mine, c)
            self.wait(self.hub.at[at], self.OUTER, c)

            @pl.when(self.is_hub)
            def _():
                self.total[self.q, mine] = self.part[at] + self.hub[at]

            @pl.when(self.not_hub)
            def _():
                self.total[self.q, mine] = self.hub[at]

            pl.when(self.has_outer)(self.pass_out(c).start)
            for d in range(1, self.ny):
                if c < self.first_direct:
                    self.to_row(d, c).start()
                else:
                    pl.when(self.outer_last)(self.to_end(d, c).start)
                    pl.when(self.not_last)(self.to_row(d, c).start)
            self.share(0, c, self.q).start()

    def four(self):
        for c in self.chunks:
            for d in range(1, self.ny):
                self.wait(self.total.at[self.q, self.at(self.origin(d), c)], self.ROW + self.ny + d - 2, c)
                self.share(d, c, self.q).start()

    def shared(self):
        ref = self.total.at[1 - self.q]
        remote(ref, ref, self.shared_sems.at[0], self.shared_sems.at[1], self.partner).wait_recv()

    def end(self):
        def sent(ref, stage):
            remote(ref, ref, self.send.at[stage], self.recv.at[0, 0], self.partner).wait_send()

        sent(self.ppair, self.PAIR)
        ref = self.total.at[self.q]
        remote(ref, ref, self.shared_sems.at[0], self.shared_sems.at[1], self.partner).wait_send()
        sent(self.part, self.INNER)
        pl.when(self.has_outer)(functools.partial(sent, self.part, self.OUTER))
        for d in range(1, self.ny):
            sent(self.part, self.ROW + d - 1)
            first = self.first_direct * self.rows
            stage = self.ROW + self.ny + d - 2
            pl.when(self.not_last)(functools.partial(sent, self.part, stage))
            pl.when(self.is_last)(functools.partial(sent, self.part.at[pl.ds(0, first)], stage))

            @pl.when(self.outer_last)
            def _():
                ref = self.part.at[pl.ds(0, self.size - first)]
                remote(ref, ref, self.shared_sems.at[1 + d], self.recv.at[0, 0], self.partner).wait_send()


def near_greet(ny, partner, rows):
    my = lax.axis_index("scany")
    greet(
        [(True, partner)]
        + [(True, {"scany": lax.rem(my + d, ny)}) for d in range(1, ny)]
        + [(side.has, side.where) for side in rows]
    )


def row_ready(sem, rows):
    for i, side in enumerate(rows):

        @pl.when(side.has)
        def _(i=i, side=side):
            pl.semaphore_signal(sem.at[1 - i], inc=1, device_id=side.where, device_id_type=MESH)


def row_wait(sem, rows):
    for i, side in enumerate(rows):
        pl.when(side.has)(functools.partial(pl.semaphore_wait, sem.at[i], 1))


def each(step):
    p = lax.axis_index("pos")
    for q in range(2):
        pl.when(p == q)(functools.partial(step, q))


class Placer:
    def __init__(self, offsets, bufs, m, positions):
        self.bufs, self.m = bufs, m
        self.tall, self.span = m + 8, m + 128
        self.top = (bufs.shape[2] - self.tall // 8) // 2
        self.spots = []
        for j in range(positions):
            row, col = offsets[j, 0], offsets[j, 1]
            self.spots.append((lax.rem(row, 8), lax.rem(col, 128), lax.div(row, 8), lax.div(col, 128)))

    def clear(self):
        n, k, rows = self.bufs.shape[:3]
        bottom = self.top + self.tall // 8
        for j in range(n):
            for c in range(k):
                self.bufs[j, c, 0 : self.top] = jnp.zeros((self.top, *self.bufs.shape[3:]), jnp.float32)
                self.bufs[j, c, bottom:rows] = jnp.zeros((rows - bottom, *self.bufs.shape[3:]), jnp.float32)

    def put(self, j, k, term):
        row_in, col_in, _, step = self.spots[j]
        m, wide = self.m, self.bufs.shape[4]
        blank_rows = jnp.zeros((self.tall - m, m), jnp.float32)
        blank_cols = jnp.zeros((self.tall, self.span - m), jnp.float32)
        moved = pltpu.roll(jnp.concatenate([term, blank_rows], 0), row_in, 0)
        moved = pltpu.roll(jnp.concatenate([moved, blank_cols], 1), col_in, 1)
        out = None
        for d in range((wide - self.span) // 128 + 1):
            parts = [jnp.zeros((self.tall, w), jnp.float32) for w in (128 * d, wide - self.span - 128 * d)]
            here = jnp.concatenate([x for x in (parts[0], moved, parts[1]) if x.shape[1]], 1)
            out = here if out is None else jnp.where(step == d, here, out)
        self.bufs[j, k, self.top : self.top + self.tall // 8] = out.reshape(self.tall // 8, 8, wide)

    def rows(self, k, r0, count):
        out = None
        for j, (_, _, row, _) in enumerate(self.spots):
            part = self.bufs[j, k, pl.ds(self.top - row + r0 // 8, count // 8)]
            out = part if out is None else out + part
        return out.reshape(count, self.bufs.shape[4])

    def window(self, j, pad, k):
        row_in, col_in, row, step = self.spots[j]
        wide = pad.shape[3]
        block = pad[k, pl.ds(row, self.tall // 8)].reshape(self.tall, wide)
        out = block[:, : self.span]
        for d in range(1, (wide - self.span) // 128 + 1):
            out = jnp.where(step == d, block[:, 128 * d : 128 * d + self.span], out)
        out = pltpu.roll(out, lax.rem(self.span - col_in, self.span), 1)[:, : self.m]
        return pltpu.roll(out, lax.rem(self.tall - row_in, self.tall), 0)[: self.m]


def forward(window, pr, pi, table_a, table_b):
    m = pr.shape[0]
    bf = jnp.bfloat16
    ar, ai = window
    er = pr * ar - pi * ai
    ei = pr * ai + pi * ar
    left = dot(table_a[...], jnp.concatenate([er.astype(bf), ei.astype(bf)], 0)).astype(bf)
    return er, ei, dot(jnp.concatenate([left[:m], left[m:]], 1), table_b[...])


def backward(er, ei, far, amplitude, table_a, table_b):
    m = er.shape[0]
    bf = jnp.bfloat16
    fr, fi = far[:, :m], far[:, m:]
    ratio = amplitude.astype(jnp.float32) / jnp.maximum(jnp.sqrt(fr * fr + fi * fi), 0.2)
    projected = jnp.concatenate([(fr * ratio).astype(bf), (fi * ratio).astype(bf)], 0)
    back_half = dot(table_b[...], projected).astype(bf)
    back = dot(jnp.concatenate([back_half[:m], back_half[m:]], 1), table_a[...])
    return back[:, :m] - er, back[:, m:] - ei


def whole_kernel(nx, ny, step_size, *refs):
    offsets, spec, *given = refs[:6]
    new_spec, new_probe = refs[6:8]
    pad, probe, amplitudes, table_a, table_b, bufs, grad, prob, total, light_all = refs[8:18]
    pair, acc, xr2, zr1, ipair, iacc, ixr, izr, ppair, row_in, out_in, part, hub = refs[18:31]
    hsend, hrecv, local, gsend, grecv, isend, irecv, psend, precv, ssems, ready = refs[31:]
    tile, m = spec.shape[3], probe.shape[1]
    wide = pad.shape[3]
    half = (wide - tile) // 2
    h = grad.shape[3]
    positions, chunks = amplitudes.shape[0], precv.shape[1]
    p = lax.axis_index("pos")
    partner = {"pos": 1 - p}
    loads = [pltpu.make_async_copy(spec, pad.at[:, pl.ds(half // 8, tile // 8), :, pl.ds(half, tile)], local.at[0])]
    for i, (src, dst) in enumerate(zip(given, (probe, amplitudes, table_a, table_b)), 1):
        loads.append(pltpu.make_async_copy(src, dst, local.at[i]))
    for c in loads:
        c.start()
    roles = [Role(q, nx, ny) for q in range(2)]
    sides = roles[1].sides1 + roles[0].sides1
    near_greet(ny, partner, roles[1].sides1)
    halos = [Halo(r, spec, pad, hsend, hrecv, partner) for r in roles]
    role = Role(p, nx, ny, 1)
    fold = Fold(role, role, grad.at[p], grad.at[1 - p], pair, acc, (zr1, None, None, xr2), None, gsend, grecv, partner)
    light = Fold(
        role,
        role,
        grad.at[2, :, pl.ds(p, 1)],
        grad.at[2, :, pl.ds(1 - p, 1)],
        ipair,
        iacc,
        (izr, None, None, ixr),
        light_all,
        isend,
        irecv,
        partner,
    )
    probe_sum = ProbeSum(p, nx, ny, prob, ppair, row_in, out_in, part, hub, total, psend, precv, ssems, partner)
    placer = Placer(offsets, bufs, m, positions)

    def gather(k):
        for g in range(4):
            for b in range(2):
                grad[k, g, b] = placer.rows(k, (2 * g + b) * h, h)

    rows = roles[1].sides1
    pl.when(p == 0)(functools.partial(row_ready, ready, rows))
    each(lambda q: halos[q].begin())
    for i, at in enumerate(
        (
            (slice(None), pl.ds(0, half // 8)),
            (slice(None), pl.ds((half + tile) // 8, half // 8)),
            (slice(None), slice(None), slice(None), pl.ds(0, half)),
            (slice(None), slice(None), slice(None), pl.ds(half + tile, half)),
        )
    ):

        @pl.when(jnp.logical_not(sides[i].has))
        def _(at=at):
            pad[at] = jnp.zeros(pad.at[at].shape, pad.dtype)

    placer.clear()

    @pl.when(p == 0)
    def _():
        row_wait(ready, rows)
        halos[0].begin_corners()

    loads[1].wait()
    power = probe[0] * probe[0] + probe[1] * probe[1]
    for j in range(positions):
        placer.put(j, 2, power)
    gather(2)
    light.begin()

    def strips(q):
        halos[q].relay()

    def corners(q):
        halos[q].relay_second()
        halos[q].relay_corners()
        halos[1 - q].arrive()

    for i in range(3):
        light.add(i)
    light.send_rims(0)
    each(strips)
    each(corners)
    for c in loads[:1] + loads[2:]:
        c.wait()
    pr, pi = probe[0], probe[1]
    windows = [[placer.window(j, pad, k) for k in range(2)] for j in range(positions)]
    fields = [forward(windows[j], pr, pi, table_a, table_b) for j in range(positions)]
    light.fold(0)
    light.send_rims(1)
    diffs = [backward(*fields[j], amplitudes[j], table_a, table_b) for j in range(positions)]
    sums = [None, None]
    for (ar, ai), (dr, di) in zip(windows, diffs):
        for k, t in enumerate((ar * dr + ai * di, ar * di - ai * dr)):
            sums[k] = t if sums[k] is None else sums[k] + t
    for c in range(chunks):
        for part_of in range(ny):
            at = probe_sum.at(part_of, c)
            for k in range(2):
                prob[k, at] = sums[k][at.start : at.start + at.size]
            probe_sum.pair(part_of, c).start()
    for j, (dr, di) in enumerate(diffs):
        placer.put(j, 0, pr * dr + pi * di)
        placer.put(j, 1, pr * di - pi * dr)
    gather(1 - p)
    fold.begin()
    gather(p)

    def share_copy(q):
        return remote(new_spec.at[q], new_spec.at[q], gsend.at[7], grecv.at[7], partner)

    probe_sum.one()
    fold.add(0)
    fold.add(1)
    fold.send_rims(0, probe_sum.early)
    fold.add(2)
    light.fold(1)
    light.share()
    probe_sum.two()
    fold.send_rims(0, probe_sum.late)

    def strips_in():
        fold.fold(0)
        fold.send_rims(1)

    pl.when(jnp.logical_not(probe_sum.has_outer))(strips_in)
    probe_sum.three(range(chunks - chunks // 4))
    pl.when(probe_sum.has_outer)(strips_in)
    probe_sum.three(range(chunks - chunks // 4, chunks))
    pl.when(probe_sum.has_outer)(probe_sum.four)
    light.arrive()
    fold.fold(1)
    q4 = fold.q4
    for g in range(2):
        for b in range(2):
            r0 = (2 * g + b) * h
            old = pad[p, (half + r0) // 8 : (half + r0 + h) // 8, :, half : half + tile].reshape(h, tile)
            new_spec[p, r0 : r0 + h] = old + acc[1 + g, b, :, q4 : 3 * q4] / (light_all[b, g, 0] + 1.0)
    share_copy(p).start()
    pl.when(jnp.logical_not(probe_sum.has_outer))(probe_sum.four)
    probe_sum.shared()
    share_copy(1 - p).wait_recv()
    share_copy(p).wait_send()
    light.finish()
    fold.finish()
    probe_sum.end()
    each(lambda q: halos[q].finish())
    for k in range(2):
        new_probe[k] = probe[k] + total[k] * step_size


def emit_kernel(spec, probe, new_spec, new_probe, sem):
    copies = [
        pltpu.make_async_copy(src.at[k, at], dst.at[k, at], sem.at[i, k, j])
        for i, (src, dst) in enumerate(((spec, new_spec), (probe, new_probe)))
        for k in range(2)
        for j, at in enumerate((pl.ds(0, src.shape[1] // 2), pl.ds(src.shape[1] // 2, src.shape[1] // 2)))
    ]
    for c in copies:
        c.start()
    for c in copies:
        c.wait()


def tables(length):
    index = np.arange(length)
    angle = ((index[:, None] * index[None, :]) % length).astype(np.float32) * np.float32(2.0 * math.pi / length)
    scale = np.float32(1.0 / math.sqrt(length))
    c = np.cos(angle) * scale
    s = np.sin(angle) * scale
    a = np.block([[c, s], [-s, c]]).astype(jnp.bfloat16)
    b = np.block([[c, -s], [s, c]]).astype(jnp.bfloat16)
    return a, b


def shards(nx, ny, consts, specimen, probe_wave, amplitudes, offsets):
    m = probe_wave.shape[1]
    tile = specimen.shape[1]
    wide = tile + m
    f32 = jnp.float32
    vm = pl.BlockSpec(memory_space=VMEM)
    sm = pl.BlockSpec(memory_space=pltpu.SMEM)
    hbm = pl.BlockSpec(memory_space=pltpu.HBM)
    dma = pltpu.SemaphoreType.DMA
    n = nx * ny
    h = wide // 8
    chunks = 8
    positions = offsets.shape[0]
    held = (probe_wave, amplitudes, consts[0], consts[1])

    step_size = 1.0 / math.sqrt(positions * n * 2)
    results = pl.pallas_call(
        functools.partial(whole_kernel, nx, ny, step_size),
        out_shape=[VMEM(specimen.shape, f32), VMEM(probe_wave.shape, f32)],
        in_specs=[sm] + [hbm] * 5,
        out_specs=[vm, vm],
        scratch_shapes=[
            VMEM((2, wide // 8, 8, wide), f32),
            *[VMEM(x.shape, x.dtype) for x in held],
            VMEM((positions, 3, (2 * (tile - 8) + m + 8) // 8, 8, wide), f32),
            VMEM((3, 4, 2, h, wide), f32),
            VMEM((2, m, m), f32),
            VMEM((2, m, m), f32),
            VMEM((2, 2, 1, h, wide // 2), f32),
            VMEM((4, 2, h, wide), f32),
            VMEM((4, 2, h, wide), f32),
            VMEM((2, 2, 2, h, wide // 4), f32),
            VMEM((2, 2, h, wide), f32),
            VMEM((4, 1, h, wide), f32),
            VMEM((4, 1, h, wide), f32),
            VMEM((2, 2, 1, h, wide // 4), f32),
            VMEM((2, 1, h, wide), f32),
            VMEM((m, m), f32),
            VMEM((ny, m // ny, m), f32),
            VMEM((m // ny, m), f32),
            VMEM((m // ny, m), f32),
            VMEM((m // ny, m), f32),
            dma((20,)),
            dma((20,)),
            dma((5,)),
            dma((8,)),
            dma((8,)),
            dma((8,)),
            dma((8,)),
            dma((1 + 2 * ny,)),
            dma((1 + 2 * ny, chunks)),
            dma((1 + ny,)),
            pltpu.SemaphoreType.REGULAR((2,)),
        ],
        compiler_params=pltpu.CompilerParams(vmem_limit_bytes=56 * 2**20, collective_id=0, has_side_effects=True),
        name="whole",
    )(offsets, *[pltpu.with_memory_space_constraint(x, pltpu.HBM) for x in (specimen.reshape(2, tile // 8, 8, tile), *held)])
    return pl.pallas_call(
        emit_kernel,
        out_shape=[jax.ShapeDtypeStruct(specimen.shape, f32), jax.ShapeDtypeStruct(probe_wave.shape, f32)],
        in_specs=[vm] * 2,
        out_specs=[pl.BlockSpec(memory_space=pl.ANY)] * 2,
        scratch_shapes=[dma((2, 2, 2))],
        compiler_params=pltpu.CompilerParams(vmem_limit_bytes=2 * 2**20),
        name="emit",
    )(*results)


def solution(mesh):
    nx, ny = mesh.shape["scanx"], mesh.shape["scany"]

    def run(specimen, probe_wave, amplitudes, offsets):
        consts = tables(probe_wave.shape[2])
        return jax.shard_map(
            lambda *args: shards(nx, ny, [jnp.asarray(t) for t in consts], *args),
            mesh=mesh,
            in_specs=(
                P(None, ("groups", "scanx"), "scany"),
                P(None, "groups", None),
                P(("groups", "scanx", "scany", "pos"), None, None),
                P(("groups", "scanx", "scany", "pos"), None),
            ),
            out_specs=(P(None, ("groups", "scanx"), "scany"), P(None, "groups", None)),
            check_vma=False,
        )(specimen, probe_wave, amplitudes, offsets)

    return run
```
